32 devices in a mesh: ctx: 8 (over z, x), tp: 4 (over y, core).
Axes of the slice: x: 2, y: 2, z: 4, core: 2. Of those that a mesh axis runs over, the one named last changes fastest.
Arguments:
- inputs: bfloat16 [2048, 3, 4096], P('ctx', None, 'tp'), may hold values from -6 to 6
- short_filter: float32 [3, 3, 4096], P(None, None, 'tp'), may hold values from -2.5 to 2.5
- long_filter: bfloat16 [256, 128], P('tp'), may hold values from -0.5 to 0.5
- out_weight: bfloat16 [4096, 4096], P('tp'), may hold values from -0.09375 to 0.09375
- out_cotangent: bfloat16 [2048, 4096], P('ctx'), may hold values from -6 to 6
Outputs:
- result: bfloat16 [2048, 4096], P('ctx')
- grad_inputs: bfloat16 [2048, 3, 4096], P('ctx', None, 'tp')
- grad_short: float32 [3, 3, 4096], P(None, None, 'tp')
- grad_long: float32 [256, 128], P('tp')
The draws below stay inside these ranges and needn't reach their ends.
All inputs are finite; a program needn't handle non-finite values.
Results may differ from the reference program's by a relative error of at most 0.009.
Values may be sent and summed in bfloat16 or wider, within the bound.
No kernel may reach another device: no remote copies, remote signals or barrier semaphores. Data moves between devices by JAX's collectives and lax.ppermute only.
A program may use at most 128 MiB of HBM per device.

```python
import jax
import jax.numpy as jnp
from jax import lax

D = 4096
GS = 16
L = 128
S = 3
FILTERS = 256
TOKENS = 2048
N_TP = 4


def level_of(own_key, dims, split, smallest, high):
    loudness = 1.0
    for dim, parts in split:
        draws = jax.random.uniform(jax.random.fold_in(jax.random.fold_in(own_key, 6), dim), (parts,), jnp.float32, smallest / len(split), high / len(split))
        loudness = loudness * jnp.repeat(jnp.exp(draws), dims[dim] // parts).reshape((-1,) + (1,) * (len(dims) - 1 - dim))
    return loudness


def scatter_about(own_key, extent, scale, most, cuts=(), held_as=jnp.bfloat16):
    array = jax.random.normal(own_key, extent, jnp.float32) * scale
    if len(cuts) > 0:
        array = level_of(own_key, extent, cuts, -0.22, 0.18) * array
    return jnp.clip(array, min=-most, max=most).astype(held_as)


def setup_inputs(seed: int = 0) -> dict:
    key_list = jax.random.split(jax.random.key(seed), 6)
    inputs = scatter_about(key_list[0], (TOKENS, 3, D), 1.0, 6.0, ((0, 8), (2, 4)))
    short_filter = scatter_about(key_list[1], (S, 3, D), 0.4, 2.5, ((2, 4),), jnp.float32)
    long_filter = scatter_about(key_list[2], (FILTERS, L), L ** -0.5, 0.5, ((0, 4),))
    out_weight = scatter_about(key_list[3], (D, D), D ** -0.5, 0.09375, ((0, 4),))
    out_cotangent = scatter_about(key_list[4], (TOKENS, D), 1.0, 6.0, ((0, 8),))
    return {"inputs": inputs, "short_filter": short_filter, "long_filter": long_filter, "out_weight": out_weight, "out_cotangent": out_cotangent}


def delay(values, lag):
    if lag == 0:
        return values
    filler = jnp.zeros((lag,) + values.shape[1:], values.dtype)
    return jnp.concatenate([filler, values[:-lag]], axis=0)

def advance(values, lag):
    if lag == 0:
        return values
    filler = jnp.zeros((lag,) + values.shape[1:], values.dtype)
    return jnp.concatenate([values[lag:], filler], axis=0)

def causal_long(signal, chan_taps):
    count = signal.shape[0]
    span = chan_taps.shape[0]
    padded = jnp.concatenate([jnp.zeros((span, signal.shape[1]), jnp.float32), signal], axis=0)

    def step(lag, total):
        window = lax.dynamic_slice_in_dim(padded, (span - lag).astype(jnp.int32), count, 0)
        return total + chan_taps[lag] * window
    return lax.fori_loop(jnp.int32(0), jnp.int32(span), step, jnp.zeros(signal.shape, jnp.float32))

def anticausal_long(signal, chan_taps):
    count = signal.shape[0]
    span = chan_taps.shape[0]
    padded = jnp.concatenate([signal, jnp.zeros((span, signal.shape[1]), jnp.float32)], axis=0)

    def step(lag, total):
        window = lax.dynamic_slice_in_dim(padded, lag.astype(jnp.int32), count, 0)
        return total + chan_taps[lag] * window
    return lax.fori_loop(jnp.int32(0), jnp.int32(span), step, jnp.zeros(signal.shape, jnp.float32))

def long_tap_grad(cotangent, signal, span):
    count = signal.shape[0]
    padded = jnp.concatenate([jnp.zeros((span, signal.shape[1]), jnp.float32), signal], axis=0)

    def step(lag, table):
        window = lax.dynamic_slice_in_dim(padded, (span - lag).astype(jnp.int32), count, 0)
        return table.at[lag].set(lax.optimization_barrier(jnp.sum(cotangent * window, axis=0)))
    return lax.fori_loop(jnp.int32(0), jnp.int32(span), step, jnp.zeros((span, signal.shape[1]), jnp.float32))

def reference(inputs, short_filter, long_filter, out_weight, out_cotangent):
    tokens = inputs.shape[0]
    width = D // N_TP
    groups = width // GS
    short_scale = float(tokens) ** (-0.5)
    long_scale = float(tokens * GS) ** (-0.5)

    def one_block(carry, index):
        start = (index * width).astype(jnp.int32)
        signal = lax.dynamic_slice_in_dim(inputs, start, width, 2).astype(jnp.float32)
        taps = lax.dynamic_slice_in_dim(short_filter, start, width, 2)
        filt = lax.dynamic_slice_in_dim(long_filter, (index * groups).astype(jnp.int32), groups, 0).astype(jnp.float32)
        chan_taps = jnp.repeat(filt, GS, axis=0).T
        weight = lax.dynamic_slice_in_dim(out_weight, start, width, 0)
        feat = taps[0] * signal
        for lag in range(1, S):
            feat = feat + taps[lag] * delay(signal, lag)
        query, keyed, valued = (feat[:, 0], feat[:, 1], feat[:, 2])
        gated = (keyed * valued).astype(jnp.bfloat16)
        gated32 = lax.optimization_barrier(gated).astype(jnp.float32)
        mixed = causal_long(gated32, chan_taps)
        gate_out = (query * mixed).astype(jnp.bfloat16)
        partial_value = jnp.dot(gate_out, weight, preferred_element_type=jnp.float32).astype(jnp.bfloat16)
        partial_value = lax.optimization_barrier(partial_value).astype(jnp.float32)
        grad_gate = lax.dot_general(out_cotangent, weight, (((1,), (1,)), ((), ())), preferred_element_type=jnp.float32)
        grad_mixed = (grad_gate * query).astype(jnp.bfloat16)
        grad_mixed32 = lax.optimization_barrier(grad_mixed).astype(jnp.float32)
        grad_query = grad_gate * mixed
        grad_gated = anticausal_long(grad_mixed32, chan_taps)
        grad_feat = jnp.stack([grad_query, grad_gated * valued, grad_gated * keyed], axis=1).astype(jnp.bfloat16)
        grad_feat32 = lax.optimization_barrier(grad_feat).astype(jnp.float32)
        grad_in = taps[0] * grad_feat32
        for lag in range(1, S):
            grad_in = grad_in + taps[lag] * advance(grad_feat32, lag)
        short_rows = [lax.optimization_barrier(jnp.sum(grad_feat32 * delay(signal, lag), axis=0)) for lag in range(S)]
        grad_short_block = jnp.stack(short_rows, axis=0) * short_scale
        chan_grad = long_tap_grad(grad_mixed32, gated32, L)
        grad_long_block = chan_grad.reshape(L, groups, GS).sum(axis=2).T * long_scale
        return (carry + partial_value, (grad_in.astype(jnp.bfloat16), grad_short_block, grad_long_block))
    total, (grad_in_all, grad_short_all, grad_long_all) = lax.scan(one_block, jnp.zeros((tokens, D), jnp.float32), jnp.arange(N_TP, dtype=jnp.int32))
    result = total.astype(jnp.bfloat16)
    grad_inputs = grad_in_all.transpose(1, 2, 0, 3).reshape(tokens, 3, D)
    grad_short = grad_short_all.transpose(1, 2, 0, 3).reshape(S, 3, D)
    grad_long = grad_long_all.reshape(FILTERS, L)
    return (result, grad_inputs, grad_short, grad_long)
```

```python
import functools

import jax
import jax.numpy as jnp
from jax import lax
from jax.experimental import pallas as pl
from jax.experimental.pallas import tpu as pltpu
from jax.sharding import PartitionSpec as P

LANES = 128
F32 = jnp.float32
BF16 = jnp.bfloat16
VMEM_LIMIT = 56 * 1024 * 1024


def pairwise(axis, step):
    return [(source, source ^ step) for source in range(lax.axis_size(axis))]


def shifted(value, axis, steps):
    count = lax.axis_size(axis)
    initial, last = (max(0, -steps), min(count, count - steps))
    return lax.ppermute(value, axis, [(source, source + steps) for source in range(initial, last)])


def params():
    return pltpu.CompilerParams(vmem_limit_bytes=VMEM_LIMIT)


def fill_signal(x_ref, ext_ref, rim_ref, row):
    rows = x_ref.shape[1]
    for part in range(3):
        if rim_ref is None:
            ext_ref[part, 0:8, :] = jnp.zeros((8, LANES), F32)
        else:
            ext_ref[part, 6:8, :] = rim_ref[row + 2 * part : row + 2 * part + 2, :].astype(F32)
        ext_ref[part, 8 : 8 + rows, :] = x_ref[part].astype(F32)


def features(ext_ref, taps_ref, part, start, rows):
    total = taps_ref[0, part : part + 1, :] * ext_ref[part, 8 + start : 8 + start + rows, :]
    for lag in range(1, 3):
        first = 8 + start - lag
        total = total + taps_ref[lag, part : part + 1, :] * ext_ref[part, first : first + rows, :]
    return total


def group_of_lane(rows, group):
    return lax.broadcasted_iota(jnp.int32, (rows, LANES), 1) // group


def reversal():
    source = lax.broadcasted_iota(jnp.int32, (LANES, LANES), 0)
    target = lax.broadcasted_iota(jnp.int32, (LANES, LANES), 1)
    return ((source + target) % LANES == 0)


def fill_table(table_ref, taps, forward):
    row = lax.broadcasted_iota(jnp.int32, (LANES, LANES), 0)
    col = lax.broadcasted_iota(jnp.int32, (LANES, LANES), 1)
    early = (col > row) if forward else (col >= row)
    for g in range(taps.shape[0]):
        wide = jnp.broadcast_to(taps[g : g + 1, :], (LANES, LANES))
        ring = pltpu.roll(wide, 0, 1, stride=1, stride_axis=0)
        table_ref[g * LANES : (g + 1) * LANES, 0:LANES] = jnp.where(early, ring, 0.0).astype(BF16)
        table_ref[g * LANES : (g + 1) * LANES, LANES:] = jnp.where(early, 0.0, ring).astype(BF16)


def pick_groups(wide, group, blocks):
    count = LANES // group
    lane = group_of_lane(LANES, group)
    outs = []
    for b in range(blocks):
        total = wide[0:LANES, b * LANES : (b + 1) * LANES]
        for g in range(1, count):
            total = jnp.where(
                lane == g, wide[g * LANES : (g + 1) * LANES, b * LANES : (b + 1) * LANES], total
            )
        outs.append(total)
    return jnp.concatenate(outs, axis=0)


def tail_kernel(x_ref, taps_ref, sent_ref, ext):
    rows = x_ref.shape[1]
    fill_signal(x_ref, ext, None, 0)
    start = rows - LANES
    keyed = features(ext, taps_ref, 1, start, LANES)
    valued = features(ext, taps_ref, 2, start, LANES)
    sent_ref[0:LANES, :] = (keyed * valued).astype(BF16)
    rim = [ext[part, 8 + rows - 2 : 8 + rows, :] for part in range(3)]
    rim.append(jnp.zeros((10, LANES), F32))
    sent_ref[LANES:, :] = jnp.concatenate(rim, axis=0).astype(BF16)


def forward_kernel(
    group, x_ref, taps_ref, filt_ref, halo_ref, gg_ref, gate_ref, gm_ref, gq_ref, back_ref, ext, gext, table
):
    rows = x_ref.shape[1]
    blocks = rows // LANES
    fill_signal(x_ref, ext, halo_ref, LANES)
    query = features(ext, taps_ref, 0, 0, rows)
    keyed = features(ext, taps_ref, 1, 0, rows)
    valued = features(ext, taps_ref, 2, 0, rows)
    gext[0:LANES, :] = halo_ref[0:LANES, :]
    gext[LANES:, :] = (keyed * valued).astype(BF16)
    filt = filt_ref[...]
    backward = jnp.dot(filt, reversal().astype(BF16), preferred_element_type=F32)
    fill_table(table, backward, True)
    stacked = jnp.concatenate(
        [gext[b * LANES : (b + 2) * LANES, :] for b in range(blocks)], axis=1
    )
    wide = jnp.dot(table[...], stacked, preferred_element_type=F32)
    mixed = pick_groups(wide, group, blocks)
    gate_ref[...] = (query * mixed).astype(BF16)
    grad_gate = gg_ref[...]
    grad_mixed = (grad_gate * query).astype(BF16)
    gm_ref[...] = grad_mixed
    grad_query = (grad_gate * mixed).astype(BF16)
    gq_ref[...] = grad_query
    count = LANES // group
    owner = (
        lax.broadcasted_iota(jnp.int32, (count, LANES), 1) // group
        == lax.broadcasted_iota(jnp.int32, (count, LANES), 0)
    ).astype(BF16)
    spread = lax.dot_general(
        filt, owner, (((0,), (0,)), ((), ())), preferred_element_type=F32
    )
    gm32 = grad_mixed.astype(F32)
    heads = [
        jnp.sum(spread * gm32[t : t + LANES], axis=0, keepdims=True) for t in range(2)
    ]
    head = jnp.concatenate(heads, axis=0)
    back_ref[0:LANES, :] = grad_mixed[0:LANES]
    back_ref[LANES:, :] = jnp.concatenate(
        [
            grad_query[0:2].astype(F32),
            head * valued[0:2],
            head * keyed[0:2],
            jnp.zeros((10, LANES), F32),
        ],
        axis=0,
    ).astype(BF16)


def backward_kernel(
    group, x_ref, taps_ref, filt_ref, halo_ref, gm_ref, gq_ref, back_ref,
    gin_ref, sums_ref, ext, gext, mext, gf, table, left,
):
    rows = x_ref.shape[1]
    blocks = rows // LANES
    count = LANES // group
    fill_signal(x_ref, ext, halo_ref, LANES)
    keyed = features(ext, taps_ref, 1, 0, rows)
    valued = features(ext, taps_ref, 2, 0, rows)
    gext[0:LANES, :] = halo_ref[0:LANES, :]
    gext[LANES:, :] = (keyed * valued).astype(BF16)
    mext[0:rows, :] = gm_ref[...]
    mext[rows:, :] = back_ref[0:LANES, :]
    fill_table(table, filt_ref[...].astype(F32), False)
    stacked = jnp.concatenate(
        [mext[b * LANES : (b + 2) * LANES, :] for b in range(blocks)], axis=1
    )
    wide = jnp.dot(table[...], stacked, preferred_element_type=F32)
    grad_gated = pick_groups(wide, group, blocks)
    parts = (
        gq_ref[...].astype(F32),
        (grad_gated * valued).astype(BF16).astype(F32),
        (grad_gated * keyed).astype(BF16).astype(F32),
    )
    short_rows = [[None] * 3 for _ in range(3)]
    for part in range(3):
        gf[part, 0:rows, :] = parts[part]
        gf[part, rows : rows + 2, :] = back_ref[
            LANES + 2 * part : LANES + 2 * part + 2, :
        ].astype(F32)
        total = taps_ref[0, part : part + 1, :] * parts[part]
        for lag in range(1, 3):
            total = total + taps_ref[lag, part : part + 1, :] * gf[part, lag : lag + rows, :]
        gin_ref[part] = total.astype(BF16)
        for lag in range(3):
            short_rows[lag][part] = jnp.sum(
                parts[part] * ext[part, 8 - lag : 8 - lag + rows, :], axis=0, keepdims=True
            )
    lane = group_of_lane(LANES, group)
    for g in range(count):
        own = lane == g
        for b in range(blocks):
            left[g * LANES : (g + 1) * LANES, b * LANES : (b + 1) * LANES] = jnp.where(
                own, gm_ref[b * LANES : (b + 1) * LANES, :], jnp.zeros((), BF16)
            )
    row = lax.broadcasted_iota(jnp.int32, (LANES, LANES), 0)
    col = lax.broadcasted_iota(jnp.int32, (LANES, LANES), 1)
    upside = jnp.concatenate([gext[b * LANES : (b + 1) * LANES, :] for b in range(blocks + 1)], axis=1)
    upside = jnp.dot(
        (row + col == LANES - 1).astype(BF16), upside, preferred_element_type=F32
    ).astype(BF16)
    right = jnp.concatenate([upside[:, 0 : blocks * LANES], upside[:, LANES:]], axis=0)
    products = lax.dot_general(
        left[...], right, (((1,), (1,)), ((), ())), preferred_element_type=F32
    )
    early = row + col < LANES - 1
    lag_rows = []
    for g in range(count):
        own = products[g * LANES : (g + 1) * LANES, :]
        ring = jnp.where(early, own[:, 0:LANES], own[:, LANES:])
        ring = pltpu.roll(ring, 0, 1, stride=1, stride_axis=0)
        lag_rows.append(jnp.sum(ring, axis=0, keepdims=True))
    sums_ref[0:8, :] = pltpu.roll(jnp.concatenate(lag_rows, axis=0), 1, 1)
    flat = [short_rows[lag][part] for lag in range(3) for part in range(3)]
    flat.append(jnp.zeros((7, LANES), F32))
    sums_ref[8:24, :] = jnp.concatenate(flat, axis=0)


def unpack_kernel(short_scale, long_scale, a_ref, b_ref, short_ref, long_ref):
    total = a_ref[...] + b_ref[...]
    long_ref[...] = total[0:8] * long_scale
    for lag in range(3):
        for part in range(3):
            at = 8 + 3 * lag + part
            short_ref[lag, part : part + 1, :] = total[at : at + 1] * short_scale


def cot_kernel(c_ref, w_ref, o_ref):
    o_ref[...] = lax.dot_general(
        c_ref[...], w_ref[...], (((1,), (1,)), ((), ())), preferred_element_type=F32
    )


def half_kernel(which_ref, g_ref, w_ref, o_ref):
    o_ref[...] = jnp.dot(g_ref[...], w_ref[...], preferred_element_type=F32).astype(BF16)


def grad_gate_of(cotangent, weight):
    rows, width = cotangent.shape
    chans = weight.shape[0]
    step = min(256, chans)
    return pl.pallas_call(
        cot_kernel,
        out_shape=jax.ShapeDtypeStruct((rows, chans), F32),
        grid=(chans // step,),
        in_specs=[
            pl.BlockSpec((rows, width), lambda j: (0, 0)),
            pl.BlockSpec((step, width), lambda j: (j, 0)),
        ],
        out_specs=pl.BlockSpec((rows, step), lambda j: (0, j)),
        compiler_params=params(),
        name="grad_gate",
    )(cotangent, weight)


def half_product(which, gate, weight):
    rows, chans = gate.shape
    half = weight.shape[1] // 2
    step = 512
    tiles = half // step
    return pl.pallas_call(
        half_kernel,
        out_shape=jax.ShapeDtypeStruct((rows, half), BF16),
        grid_spec=pltpu.PrefetchScalarGridSpec(
            num_scalar_prefetch=1,
            grid=(tiles,),
            in_specs=[
                pl.BlockSpec((rows, chans), lambda j, which: (0, 0)),
                pl.BlockSpec((chans, step), lambda j, which: (0, which[0] * tiles + j)),
            ],
            out_specs=pl.BlockSpec((rows, step), lambda j, which: (0, j)),
        ),
        compiler_params=params(),
        name="half_product",
    )(which, gate, weight)


def local(inputs, short_filter, long_filter, out_weight, out_cotangent):
    rows, _, chans = inputs.shape
    groups, span = long_filter.shape
    group = chans // groups
    count = LANES // group
    tiles = chans // LANES
    tokens_all = rows * lax.axis_size("ctx")
    n_tp = lax.axis_size("tp")
    signal = inputs.transpose(1, 0, 2)
    rim_rows = LANES + 16

    x_spec = pl.BlockSpec((3, rows, LANES), lambda j: (0, 0, j))
    taps_spec = pl.BlockSpec((3, 3, LANES), lambda j: (0, 0, j))
    filt_spec = pl.BlockSpec((count, LANES), lambda j: (j, 0))
    rim_spec = pl.BlockSpec((rim_rows, LANES), lambda j: (0, j))
    full_spec = pl.BlockSpec((rows, LANES), lambda j: (0, j))
    ext_scratch = pltpu.VMEM((3, rows + 8, LANES), F32)

    sent = pl.pallas_call(
        tail_kernel,
        out_shape=jax.ShapeDtypeStruct((rim_rows, chans), BF16),
        grid=(tiles,),
        in_specs=[x_spec, taps_spec],
        out_specs=rim_spec,
        scratch_shapes=[ext_scratch],
        compiler_params=params(),
        name="tail",
    )(signal, short_filter)
    halo = shifted(sent, "ctx", 1)
    grad_gate = grad_gate_of(out_cotangent, out_weight)
    rows_bf16 = jax.ShapeDtypeStruct((rows, chans), BF16)
    gate_out, grad_mixed, grad_query, sent_back = pl.pallas_call(
        functools.partial(forward_kernel, group),
        out_shape=(rows_bf16, rows_bf16, rows_bf16, jax.ShapeDtypeStruct((rim_rows, chans), BF16)),
        grid=(tiles,),
        in_specs=[x_spec, taps_spec, filt_spec, rim_spec, full_spec],
        out_specs=(full_spec, full_spec, full_spec, rim_spec),
        scratch_shapes=[
            ext_scratch,
            pltpu.VMEM((rows + LANES, LANES), BF16),
            pltpu.VMEM((count * LANES, 2 * LANES), BF16),
        ],
        compiler_params=params(),
        name="forward",
    )(signal, short_filter, long_filter, halo, grad_gate)

    me = lax.axis_index("tp")
    core = lax.rem(me, 2)
    other = half_product(jnp.reshape(1 - core, (1,)), gate_out, out_weight)
    theirs = lax.ppermute(other, "tp", pairwise("tp", 1))
    mine = half_product(jnp.reshape(core, (1,)), gate_out, out_weight)
    mine = (mine.astype(F32) + theirs.astype(F32)).astype(BF16)
    step = 2
    while step < n_tp:
        got = lax.ppermute(mine, "tp", pairwise("tp", step))
        mine = (mine.astype(F32) + got.astype(F32)).astype(BF16)
        step *= 2
    sibling = lax.ppermute(mine, "tp", pairwise("tp", 1))
    result = jnp.where(
        core == 0,
        jnp.concatenate([mine, sibling], axis=1),
        jnp.concatenate([sibling, mine], axis=1),
    )

    back = shifted(sent_back, "ctx", -1)
    grad_in, sums = pl.pallas_call(
        functools.partial(backward_kernel, group),
        out_shape=(
            jax.ShapeDtypeStruct((3, rows, chans), BF16),
            jax.ShapeDtypeStruct((24, chans), F32),
        ),
        grid=(tiles,),
        in_specs=[x_spec, taps_spec, filt_spec, rim_spec, full_spec, full_spec, rim_spec],
        out_specs=(x_spec, pl.BlockSpec((24, LANES), lambda j: (0, j))),
        scratch_shapes=[
            ext_scratch,
            pltpu.VMEM((rows + LANES, LANES), BF16),
            pltpu.VMEM((rows + LANES, LANES), BF16),
            pltpu.VMEM((3, rows + 8, LANES), F32),
            pltpu.VMEM((count * LANES, 2 * LANES), BF16),
            pltpu.VMEM((count * LANES, (rows // LANES) * LANES), BF16),
        ],
        compiler_params=params(),
        name="backward",
    )(signal, short_filter, long_filter, halo, grad_mixed, grad_query, back)

    n_ctx = lax.axis_size("ctx")
    if n_ctx & (n_ctx - 1) == 0:
        hop = 1
        got = jnp.zeros_like(sums)
        while hop < n_ctx:
            got = lax.ppermute(sums, "ctx", pairwise("ctx", hop))
            hop *= 2
            if hop < n_ctx:
                sums = sums + got
    else:
        sums = lax.psum(sums, "ctx")
        got = jnp.zeros_like(sums)
    sums_spec = pl.BlockSpec((24, LANES), lambda j: (0, j))
    grad_short, grad_long = pl.pallas_call(
        functools.partial(
            unpack_kernel, float(tokens_all) ** (-0.5), float(tokens_all * group) ** (-0.5)
        ),
        out_shape=(
            jax.ShapeDtypeStruct((3, 3, chans), F32),
            jax.ShapeDtypeStruct((groups, span), F32),
        ),
        grid=(tiles,),
        in_specs=[sums_spec, sums_spec],
        out_specs=(taps_spec, filt_spec),
        compiler_params=params(),
        name="unpack",
    )(sums, got)
    return (result, grad_in.transpose(1, 0, 2), grad_short, grad_long)


def solution(mesh):
    in_specs = (
        P("ctx", None, "tp"),
        P(None, None, "tp"),
        P("tp", None),
        P("tp", None),
        P("ctx", None),
    )
    out_specs = (P("ctx", None), P("ctx", None, "tp"), P(None, None, "tp"), P("tp", None))
    return jax.shard_map(local, mesh=mesh, in_specs=in_specs, out_specs=out_specs, check_vma=False)
```

```python
import functools

import jax
import jax.numpy as jnp
from jax import lax
from jax.experimental import pallas as pl
from jax.experimental.pallas import tpu as pltpu
from jax.sharding import PartitionSpec as P

LANES = 128
RIM = 16
COST = 1024
F32 = jnp.float32
BF16 = jnp.bfloat16
VMEM_LIMIT = 24 * 1024 * 1024


def pairwise(axis, step):
    return [(source, source ^ step) for source in range(lax.axis_size(axis))]


def shifted(value, axis, steps):
    count = lax.axis_size(axis)
    initial, last = (max(0, -steps), min(count, count - steps))
    return lax.ppermute(value, axis, [(source, source + steps) for source in range(initial, last)])


def call(body, name, outs, scratch=(), scalars=0, far=0, operands=0, cost=COST):
    specs = [pl.BlockSpec(memory_space=pltpu.SMEM)] * scalars
    specs += [pl.BlockSpec(memory_space=pltpu.HBM)] * far
    specs += [pl.BlockSpec(memory_space=pltpu.VMEM)] * operands
    return pl.pallas_call(
        body,
        out_shape=outs,
        in_specs=specs,
        out_specs=jax.tree.map(lambda _: pl.BlockSpec(memory_space=pltpu.VMEM), outs),
        scratch_shapes=scratch,
        compiler_params=pltpu.CompilerParams(vmem_limit_bytes=VMEM_LIMIT),
        cost_estimate=pl.CostEstimate(flops=0, transcendentals=0, bytes_accessed=cost),
        name=name,
    )


def shape(dims, dtype):
    return jax.ShapeDtypeStruct(dims, dtype)


def each_tile(chans, body):
    def step(j, carry):
        body(j, pl.ds(pl.multiple_of(j * LANES, LANES), LANES))
        return carry

    lax.fori_loop(0, chans // LANES, step, 0)


def feature(ext_ref, taps_ref, lanes, part, start, rows):
    total = taps_ref[0, part : part + 1, lanes] * ext_ref[part, 8 + start : 8 + start + rows, :]
    for lag in range(1, 3):
        first = 8 + start - lag
        tap = taps_ref[lag, part : part + 1, lanes]
        total = total + tap * ext_ref[part, first : first + rows, :]
    return total


def group_of_lane(rows, group):
    return lax.broadcasted_iota(jnp.int32, (rows, LANES), 1) // group


def square(axis):
    return lax.broadcasted_iota(jnp.int32, (LANES, LANES), axis)


def fill_table(table_ref, taps, forward):
    early = (square(1) > square(0)) if forward else (square(1) >= square(0))
    for g in range(taps.shape[0]):
        wide = jnp.broadcast_to(taps[g : g + 1, :], (LANES, LANES))
        ring = pltpu.roll(wide, 0, 1, stride=1, stride_axis=0)
        table_ref[g * LANES : (g + 1) * LANES, 0:LANES] = jnp.where(early, ring, 0.0).astype(BF16)
        table_ref[g * LANES : (g + 1) * LANES, LANES:] = jnp.where(early, 0.0, ring).astype(BF16)


def pick_groups(wide, group, blocks):
    lane = group_of_lane(LANES, group)
    outs = []
    for b in range(blocks):
        total = wide[0:LANES, b * LANES : (b + 1) * LANES]
        for g in range(1, LANES // group):
            part = wide[g * LANES : (g + 1) * LANES, b * LANES : (b + 1) * LANES]
            total = jnp.where(lane == g, part, total)
        outs.append(total)
    return jnp.concatenate(outs, axis=0)


def side_by_side(ref, blocks, lanes):
    return jnp.concatenate([ref[b * LANES : (b + 2) * LANES, lanes] for b in range(blocks)], axis=1)


def spread_taps(filt, group, reverse):
    count = filt.shape[0]
    owner = (
        group_of_lane(count, group) == lax.broadcasted_iota(jnp.int32, (count, LANES), 0)
    ).astype(BF16)
    if reverse:
        flip = (square(0) + square(1) == LANES - 1).astype(BF16)
        filt = jnp.dot(filt, flip, preferred_element_type=F32).astype(BF16)
    return lax.dot_general(filt, owner, (((0,), (0,)), ((), ())), preferred_element_type=F32)


def tail_kernel(
    x_hbm, taps_hbm, filt_hbm, sent_ref, x_ref, taps_ref, filt_ref, ext, sems
):
    _, rows, chans = x_ref.shape
    first = rows - LANES - RIM
    near = (pl.ds(1, 2), pl.ds(first, LANES + RIM))
    copies = [
        pltpu.make_async_copy(taps_hbm, taps_ref, sems.at[0]),
        pltpu.make_async_copy(x_hbm.at[near], x_ref.at[near], sems.at[1]),
        pltpu.make_async_copy(x_hbm.at[0], x_ref.at[0], sems.at[2]),
        pltpu.make_async_copy(
            x_hbm.at[1:3, 0:first], x_ref.at[1:3, 0:first], sems.at[3]
        ),
        pltpu.make_async_copy(filt_hbm, filt_ref, sems.at[4]),
    ]
    for copy in copies:
        copy.start()
    for copy in copies[:3]:
        copy.wait()

    def tile(j, lanes):
        for part in range(3):
            ext[part, 8:, :] = x_ref[part, first:, lanes].astype(F32)
        keyed = feature(ext, taps_ref, lanes, 1, RIM, LANES)
        valued = feature(ext, taps_ref, lanes, 2, RIM, LANES)
        sent_ref[0:LANES, lanes] = (keyed * valued).astype(BF16)
        end = 8 + RIM + LANES
        rim = [ext[part, end - 2 : end, :] for part in range(3)]
        rim.append(jnp.zeros((RIM - 6, LANES), F32))
        sent_ref[LANES:, lanes] = jnp.concatenate(rim, axis=0).astype(BF16)

    each_tile(chans, tile)
    for copy in copies[3:]:
        copy.wait()


def grad_gate_kernel(
    c_hbm, w_hbm, x_ref, taps_ref, gg_ref, back_ref, w_ref, c_ref, ext, c_sem, w_sems
):
    chans = w_ref.shape[0]
    chunks = w_sems.shape[0]
    wide = chans // chunks
    span = LANES + RIM

    def chunk(j):
        rows = pl.ds(pl.multiple_of(j * wide, wide), wide)
        return pltpu.make_async_copy(w_hbm.at[rows], w_ref.at[rows], w_sems.at[j])

    load = pltpu.make_async_copy(c_hbm, c_ref, c_sem)
    load.start()
    for j in range(chunks):
        chunk(j).start()
    load.wait()

    def product(j, carry):
        chunk(j).wait()
        cols = pl.ds(pl.multiple_of(j * wide, wide), wide)
        gg_ref[:, cols] = lax.dot_general(
            c_ref[...], w_ref[cols, :], (((1,), (1,)), ((), ())), preferred_element_type=F32
        )
        return carry

    lax.fori_loop(0, chunks, product, 0)

    def tile(j, lanes):
        ext[0, 0:8, :] = jnp.zeros((8, LANES), F32)
        ext[0, 8:, :] = x_ref[0, 0:span, lanes].astype(F32)
        query = feature(ext, taps_ref, lanes, 0, 0, span)
        back_ref[0:span, lanes] = (gg_ref[0:span, lanes] * query).astype(BF16)
        grad = gg_ref[0:2, lanes]
        high = grad.astype(BF16).astype(F32)
        rim = [x_ref[part, 0:RIM, lanes].astype(F32)[0:2] for part in range(3)]
        rim += [high, grad - high, jnp.zeros((RIM - 10, LANES), F32)]
        back_ref[span:, lanes] = jnp.concatenate(rim, axis=0).astype(BF16)

    each_tile(chans, tile)


def forward_kernel(
    group, which_ref, x_ref, taps_ref, filt_ref, halo_ref, w_ref,
    send_ref, gate_ref, mixed_ref, gext_ref, ext, table,
):
    _, rows, chans = x_ref.shape
    blocks = rows // LANES
    count = LANES // group

    def tile(j, lanes):
        for part in range(3):
            at = LANES + 2 * part
            ext[part, 6:8, :] = halo_ref[at : at + 2, lanes].astype(F32)
            ext[part, 8:, :] = x_ref[part, :, lanes].astype(F32)
        keyed = feature(ext, taps_ref, lanes, 1, 0, rows)
        valued = feature(ext, taps_ref, lanes, 2, 0, rows)
        gext_ref[0:LANES, lanes] = halo_ref[0:LANES, lanes]
        gext_ref[LANES:, lanes] = (keyed * valued).astype(BF16)
        filt = filt_ref[pl.ds(pl.multiple_of(j * count, count), count), :]
        turned = ((square(0) + square(1)) % LANES == 0).astype(BF16)
        fill_table(table, jnp.dot(filt, turned, preferred_element_type=F32), True)
        wide = jnp.dot(
            table[...], side_by_side(gext_ref, blocks, lanes), preferred_element_type=F32
        )
        mixed = pick_groups(wide, group, blocks)
        mixed_ref[:, lanes] = mixed
        query = feature(ext, taps_ref, lanes, 0, 0, rows)
        gate_ref[:, lanes] = (query * mixed).astype(BF16)

    each_tile(chans, tile)
    half = w_ref.shape[1] // 2
    cols = pl.ds(pl.multiple_of(which_ref[0] * half, half), half)
    send_ref[...] = jnp.dot(
        gate_ref[...], w_ref[:, cols], preferred_element_type=F32
    ).astype(BF16)


def keep_kernel(which_ref, gate_ref, w_ref, keep_ref):
    half = w_ref.shape[1] // 2
    cols = pl.ds(pl.multiple_of(which_ref[0] * half, half), half)
    keep_ref[...] = jnp.dot(
        gate_ref[...], w_ref[:, cols], preferred_element_type=F32
    ).astype(BF16)


def backward_kernel(
    group, x_ref, taps_ref, filt_ref, halo_ref, gg_ref, mixed_ref, gext_ref, back_ref,
    gin_ref, sums_ref, ext, mext, gf, table, left,
):
    _, rows, chans = x_ref.shape
    blocks = rows // LANES
    count = LANES // group
    span = LANES + RIM

    def tile(j, lanes):
        for part in range(3):
            at = LANES + 2 * part
            ext[part, 6:8, :] = halo_ref[at : at + 2, lanes].astype(F32)
            ext[part, 8 : 8 + rows, :] = x_ref[part, :, lanes].astype(F32)
            at = span + 2 * part
            ext[part, 8 + rows : 10 + rows, :] = back_ref[at : at + 2, lanes].astype(F32)
        query = feature(ext, taps_ref, lanes, 0, 0, rows)
        keyed = feature(ext, taps_ref, lanes, 1, 0, rows)
        valued = feature(ext, taps_ref, lanes, 2, 0, rows)
        query_next = feature(ext, taps_ref, lanes, 0, rows, 2)
        keyed_next = feature(ext, taps_ref, lanes, 1, rows, 2)
        valued_next = feature(ext, taps_ref, lanes, 2, rows, 2)
        gg_next = back_ref[span + 6 : span + 8, lanes].astype(F32) + back_ref[
            span + 8 : span + 10, lanes
        ].astype(F32)
        grad_mixed = (gg_ref[:, lanes] * query).astype(BF16)
        head = back_ref[0:span, lanes].astype(F32)
        mixed_next = (gg_next * query_next).astype(BF16).astype(F32)
        head = jnp.concatenate([mixed_next, head[2:]], axis=0)
        mext[0:rows, :] = grad_mixed
        mext[rows:, :] = head[0:LANES].astype(BF16)
        filt = filt_ref[pl.ds(pl.multiple_of(j * count, count), count), :]
        fill_table(table, filt.astype(F32), False)
        wide = jnp.dot(
            table[...], side_by_side(mext, blocks, slice(None)), preferred_element_type=F32
        )
        grad_gated = pick_groups(wide, group, blocks)
        taps = spread_taps(filt, group, False)
        taps_turned = spread_taps(filt, group, True)
        recent = gext_ref[rows:, lanes].astype(F32)
        gated_next = (keyed_next * valued_next).astype(BF16).astype(F32)
        recent = jnp.concatenate([recent, gated_next], axis=0)
        grads_next, mixes_next = [], []
        for t in range(2):
            grads_next.append(jnp.sum(taps * head[t : t + LANES], axis=0, keepdims=True))
            mixes_next.append(
                jnp.sum(taps_turned * recent[t + 1 : t + 1 + LANES], axis=0, keepdims=True)
            )
        grad_next = jnp.concatenate(grads_next, axis=0)
        mix_next = jnp.concatenate(mixes_next, axis=0)
        parts = (
            (gg_ref[:, lanes] * mixed_ref[:, lanes]).astype(BF16).astype(F32),
            (grad_gated * valued).astype(BF16).astype(F32),
            (grad_gated * keyed).astype(BF16).astype(F32),
        )
        following = (gg_next * mix_next, grad_next * valued_next, grad_next * keyed_next)
        short_rows = [[None] * 3 for _ in range(3)]
        for part in range(3):
            gf[part, 0:rows, :] = parts[part]
            gf[part, rows : rows + 2, :] = following[part].astype(BF16).astype(F32)
            total = taps_ref[0, part : part + 1, lanes] * parts[part]
            for lag in range(1, 3):
                tap = taps_ref[lag, part : part + 1, lanes]
                total = total + tap * gf[part, lag : lag + rows, :]
            gin_ref[part, :, lanes] = total.astype(BF16)
            for lag in range(3):
                short_rows[lag][part] = jnp.sum(
                    parts[part] * ext[part, 8 - lag : 8 - lag + rows, :], axis=0, keepdims=True
                )
        lane = group_of_lane(LANES, group)
        for g in range(count):
            for b in range(blocks):
                left[g * LANES : (g + 1) * LANES, b * LANES : (b + 1) * LANES] = jnp.where(
                    lane == g, grad_mixed[b * LANES : (b + 1) * LANES, :], jnp.zeros((), BF16)
                )
        ends = [gext_ref[b * LANES : (b + 1) * LANES, lanes] for b in range(blocks + 1)]
        flip = (square(0) + square(1) == LANES - 1).astype(BF16)
        upside = jnp.dot(
            flip, jnp.concatenate(ends, axis=1), preferred_element_type=F32
        ).astype(BF16)
        right = jnp.concatenate([upside[:, 0 : blocks * LANES], upside[:, LANES:]], axis=0)
        products = lax.dot_general(
            left[...], right, (((1,), (1,)), ((), ())), preferred_element_type=F32
        )
        early = square(0) + square(1) < LANES - 1
        lag_rows = []
        for g in range(count):
            own = products[g * LANES : (g + 1) * LANES, :]
            ring = jnp.where(early, own[:, 0:LANES], own[:, LANES:])
            ring = pltpu.roll(ring, 0, 1, stride=1, stride_axis=0)
            lag_rows.append(jnp.sum(ring, axis=0, keepdims=True))
        sums_ref[0:8, lanes] = pltpu.roll(jnp.concatenate(lag_rows, axis=0), 1, 1)
        flat = [short_rows[lag][part] for lag in range(3) for part in range(3)]
        flat.append(jnp.zeros((7, LANES), F32))
        sums_ref[8:24, lanes] = jnp.concatenate(flat, axis=0)

    each_tile(chans, tile)


def unpack_kernel(group, short_scale, long_scale, a_ref, b_ref, short_ref, long_ref):
    chans = a_ref.shape[1]
    count = LANES // group
    total = a_ref[...] + b_ref[...]
    for j in range(chans // LANES):
        long_ref[j * count : (j + 1) * count, :] = (
            total[0:8, j * LANES : (j + 1) * LANES] * long_scale
        )
    for lag in range(3):
        for part in range(3):
            at = 8 + 3 * lag + part
            short_ref[lag, part : part + 1, :] = total[at : at + 1] * short_scale


def local(inputs, short_filter, long_filter, out_weight, out_cotangent):
    rows, _, chans = inputs.shape
    groups, span = long_filter.shape
    width = out_weight.shape[1]
    group = chans // groups
    count = LANES // group
    tokens_all = rows * lax.axis_size("ctx")
    n_tp = lax.axis_size("tp")
    signal = inputs.transpose(1, 0, 2)
    signal, short_filter, long_filter, out_weight, out_cotangent = [
        pltpu.with_memory_space_constraint(value, pltpu.HBM)
        for value in (signal, short_filter, long_filter, out_weight, out_cotangent)
    ]
    table = pltpu.VMEM((count * LANES, 2 * LANES), BF16)

    sent, signal, short_filter, long_filter = call(
        tail_kernel,
        "tail",
        (
            shape((LANES + RIM, chans), BF16),
            shape(signal.shape, BF16),
            shape(short_filter.shape, F32),
            shape(long_filter.shape, BF16),
        ),
        [pltpu.VMEM((3, 8 + RIM + LANES, LANES), F32), pltpu.SemaphoreType.DMA((5,))],
        far=3,
    )(signal, short_filter, long_filter)
    halo = shifted(sent, "ctx", 1)
    grad_gate, sent_back, out_weight = call(
        grad_gate_kernel,
        "grad_gate",
        (
            shape((rows, chans), F32),
            shape((LANES + 2 * RIM, chans), BF16),
            shape(out_weight.shape, BF16),
        ),
        [
            pltpu.VMEM(out_cotangent.shape, BF16),
            pltpu.VMEM((1, 8 + RIM + LANES, LANES), F32),
            pltpu.SemaphoreType.DMA,
            pltpu.SemaphoreType.DMA((max(1, chans // 256),)),
        ],
        far=2,
        operands=2,
    )(out_cotangent, out_weight, signal, short_filter)
    back = shifted(sent_back, "ctx", -1)
    core = lax.rem(lax.axis_index("tp"), 2)
    other, gate_out, mixed, gated = call(
        functools.partial(forward_kernel, group),
        "forward",
        (
            shape((rows, width // 2), BF16),
            shape((rows, chans), BF16),
            shape((rows, chans), F32),
            shape((LANES + rows, chans), BF16),
        ),
        [pltpu.VMEM((3, 8 + rows, LANES), F32), table],
        scalars=1,
        operands=5,
    )(jnp.reshape(1 - core, (1,)), signal, short_filter, long_filter, halo, out_weight)
    theirs = lax.ppermute(other, "tp", pairwise("tp", 1))
    mine = call(keep_kernel, "keep", shape((rows, width // 2), BF16), scalars=1, operands=2)(
        jnp.reshape(core, (1,)), gate_out, out_weight
    )
    theirs, back = lax.optimization_barrier((theirs, back))
    mine = (mine.astype(F32) + theirs.astype(F32)).astype(BF16)
    step = 2
    got = lax.ppermute(mine, "tp", pairwise("tp", step))

    grad_in, sums = call(
        functools.partial(backward_kernel, group),
        "backward",
        (shape((3, rows, chans), BF16), shape((24, chans), F32)),
        [
            pltpu.VMEM((3, rows + 16, LANES), F32),
            pltpu.VMEM((rows + LANES, LANES), BF16),
            pltpu.VMEM((3, rows + 8, LANES), F32),
            table,
            pltpu.VMEM((count * LANES, (rows // LANES) * LANES), BF16),
        ],
        operands=8,
        cost=200_000_000,
    )(signal, short_filter, long_filter, halo, grad_gate, mixed, gated, back)

    n_ctx = lax.axis_size("ctx")
    if n_ctx & (n_ctx - 1) == 0:
        hop = 1
        rest = jnp.zeros_like(sums)
        while hop < n_ctx:
            rest = lax.ppermute(sums, "ctx", pairwise("ctx", hop))
            hop *= 2
            if hop < n_ctx:
                sums = sums + rest
    else:
        sums = lax.psum(sums, "ctx")
        rest = jnp.zeros_like(sums)
    got, sums, rest = lax.optimization_barrier((got, sums, rest))
    mine = (mine.astype(F32) + got.astype(F32)).astype(BF16)
    step *= 2
    while step < n_tp:
        got = lax.ppermute(mine, "tp", pairwise("tp", step))
        mine = (mine.astype(F32) + got.astype(F32)).astype(BF16)
        step *= 2
    sibling = lax.ppermute(mine, "tp", pairwise("tp", 1))
    result = jnp.where(
        core == 0,
        jnp.concatenate([mine, sibling], axis=1),
        jnp.concatenate([sibling, mine], axis=1),
    )
    grad_short, grad_long = call(
        functools.partial(
            unpack_kernel, group, float(tokens_all) ** (-0.5), float(tokens_all * group) ** (-0.5)
        ),
        "unpack",
        (shape((3, 3, chans), F32), shape((groups, span), F32)),
        operands=2,
    )(sums, rest)
    return (result, grad_in.transpose(1, 0, 2), grad_short, grad_long)


def solution(mesh):
    in_specs = (
        P("ctx", None, "tp"),
        P(None, None, "tp"),
        P("tp", None),
        P("tp", None),
        P("ctx", None),
    )
    out_specs = (P("ctx", None), P("ctx", None, "tp"), P(None, None, "tp"), P("tp", None))
    return jax.shard_map(local, mesh=mesh, in_specs=in_specs, out_specs=out_specs, check_vma=False)
```

```python
import functools

import jax
import jax.numpy as jnp
from jax import lax
from jax.experimental import pallas as pl
from jax.experimental.pallas import tpu as pltpu
from jax.sharding import PartitionSpec as P

LANES = 128
RIM = 16
COST = 1024
PIECES = 2
F32 = jnp.float32
BF16 = jnp.bfloat16
VMEM_LIMIT = 12 * 1024 * 1024


def pairwise(axis, step):
    return [(source, source ^ step) for source in range(lax.axis_size(axis))]


def shifted(value, axis, steps):
    count = lax.axis_size(axis)
    initial, last = (max(0, -steps), min(count, count - steps))
    return lax.ppermute(value, axis, [(source, source + steps) for source in range(initial, last)])


def call(body, name, outs, scratch=(), scalars=0, far=0, operands=0, cost=COST):
    specs = [pl.BlockSpec(memory_space=pltpu.SMEM)] * scalars
    specs += [pl.BlockSpec(memory_space=pltpu.HBM)] * far
    specs += [pl.BlockSpec(memory_space=pltpu.VMEM)] * operands
    return pl.pallas_call(
        body,
        out_shape=outs,
        in_specs=specs,
        out_specs=jax.tree.map(lambda _: pl.BlockSpec(memory_space=pltpu.VMEM), outs),
        scratch_shapes=scratch,
        compiler_params=pltpu.CompilerParams(vmem_limit_bytes=VMEM_LIMIT),
        cost_estimate=pl.CostEstimate(flops=0, transcendentals=0, bytes_accessed=cost),
        name=name,
    )


def shape(dims, dtype):
    return jax.ShapeDtypeStruct(dims, dtype)


def each_tile(chans, body):
    def step(j, carry):
        body(j, pl.ds(pl.multiple_of(j * LANES, LANES), LANES))
        return carry

    lax.fori_loop(0, chans // LANES, step, 0, unroll=2)


def feature(ext_ref, taps_ref, lanes, part, start, rows):
    total = taps_ref[0, part : part + 1, lanes] * ext_ref[part, 8 + start : 8 + start + rows, :]
    for lag in range(1, 3):
        first = 8 + start - lag
        tap = taps_ref[lag, part : part + 1, lanes]
        total = total + tap * ext_ref[part, first : first + rows, :]
    return total


def group_of_lane(rows, group):
    return lax.broadcasted_iota(jnp.int32, (rows, LANES), 1) // group


def square(axis):
    return lax.broadcasted_iota(jnp.int32, (LANES, LANES), axis)


def fill_table(table_ref, taps, forward):
    early = (square(1) > square(0)) if forward else (square(1) >= square(0))
    for g in range(taps.shape[0]):
        wide = jnp.broadcast_to(taps[g : g + 1, :], (LANES, LANES))
        ring = pltpu.roll(wide, 0, 1, stride=1, stride_axis=0)
        table_ref[g * LANES : (g + 1) * LANES, 0:LANES] = jnp.where(early, ring, 0.0).astype(BF16)
        table_ref[g * LANES : (g + 1) * LANES, LANES:] = jnp.where(early, 0.0, ring).astype(BF16)


def pick_groups(wide, group, blocks):
    lane = group_of_lane(LANES, group)
    outs = []
    for b in range(blocks):
        total = wide[0:LANES, b * LANES : (b + 1) * LANES]
        for g in range(1, LANES // group):
            part = wide[g * LANES : (g + 1) * LANES, b * LANES : (b + 1) * LANES]
            total = jnp.where(lane == g, part, total)
        outs.append(total)
    return jnp.concatenate(outs, axis=0)


def side_by_side(ref, blocks, lanes):
    return jnp.concatenate([ref[b * LANES : (b + 2) * LANES, lanes] for b in range(blocks)], axis=1)


def spread_taps(filt, group, reverse):
    count = filt.shape[0]
    owner = (
        group_of_lane(count, group) == lax.broadcasted_iota(jnp.int32, (count, LANES), 0)
    ).astype(BF16)
    if reverse:
        flip = (square(0) + square(1) == LANES - 1).astype(BF16)
        filt = jnp.dot(filt, flip, preferred_element_type=F32).astype(BF16)
    return lax.dot_general(filt, owner, (((0,), (0,)), ((), ())), preferred_element_type=F32)


def tail_kernel(
    x_hbm, taps_hbm, filt_hbm, sent_ref, x_ref, taps_ref, filt_ref, ext, sems
):
    _, rows, chans = x_ref.shape
    first = rows - LANES - RIM
    near = (pl.ds(1, 2), pl.ds(first, LANES + RIM))
    copies = [
        pltpu.make_async_copy(taps_hbm, taps_ref, sems.at[0]),
        pltpu.make_async_copy(x_hbm.at[near], x_ref.at[near], sems.at[1]),
        pltpu.make_async_copy(x_hbm.at[0], x_ref.at[0], sems.at[2]),
        pltpu.make_async_copy(
            x_hbm.at[1:3, 0:first], x_ref.at[1:3, 0:first], sems.at[3]
        ),
        pltpu.make_async_copy(filt_hbm, filt_ref, sems.at[4]),
    ]
    for copy in copies:
        copy.start()
    for copy in copies[:3]:
        copy.wait()

    def tile(j, lanes):
        for part in range(3):
            ext[part, 8:, :] = x_ref[part, first:, lanes].astype(F32)
        keyed = feature(ext, taps_ref, lanes, 1, RIM, LANES)
        valued = feature(ext, taps_ref, lanes, 2, RIM, LANES)
        sent_ref[0:LANES, lanes] = (keyed * valued).astype(BF16)
        end = 8 + RIM + LANES
        rim = [ext[part, end - 2 : end, :] for part in range(3)]
        rim.append(jnp.zeros((RIM - 6, LANES), F32))
        sent_ref[LANES:, lanes] = jnp.concatenate(rim, axis=0).astype(BF16)

    each_tile(chans, tile)
    for copy in copies[3:]:
        copy.wait()


def grad_gate_kernel(
    c_hbm, w_hbm, x_ref, taps_ref, gg_ref, back_ref, w_ref, c_ref, ext, c_sem, w_sems
):
    chans = w_ref.shape[0]
    chunks = w_sems.shape[0]
    wide = chans // chunks
    span = LANES + RIM

    def chunk(j):
        rows = pl.ds(pl.multiple_of(j * wide, wide), wide)
        return pltpu.make_async_copy(w_hbm.at[rows], w_ref.at[rows], w_sems.at[j])

    load = pltpu.make_async_copy(c_hbm, c_ref, c_sem)
    load.start()
    for j in range(min(2, chunks)):
        chunk(j).start()
    load.wait()

    def product(j, carry):
        chunk(j).wait()

        @pl.when(j + 2 < chunks)
        def _():
            chunk(j + 2).start()

        cols = pl.ds(pl.multiple_of(j * wide, wide), wide)
        gg_ref[:, cols] = lax.dot_general(
            c_ref[...], w_ref[cols, :], (((1,), (1,)), ((), ())), preferred_element_type=F32
        )
        return carry

    lax.fori_loop(0, chunks, product, 0)

    def tile(j, lanes):
        ext[0, 0:8, :] = jnp.zeros((8, LANES), F32)
        ext[0, 8:, :] = x_ref[0, 0:span, lanes].astype(F32)
        query = feature(ext, taps_ref, lanes, 0, 0, span)
        back_ref[0:span, lanes] = (gg_ref[0:span, lanes] * query).astype(BF16)
        grad = gg_ref[0:2, lanes]
        high = grad.astype(BF16).astype(F32)
        rim = [x_ref[part, 0:RIM, lanes].astype(F32)[0:2] for part in range(3)]
        rim += [high, grad - high, jnp.zeros((RIM - 10, LANES), F32)]
        back_ref[span:, lanes] = jnp.concatenate(rim, axis=0).astype(BF16)

    each_tile(chans, tile)


def forward_kernel(
    group, which_ref, x_ref, taps_ref, filt_ref, halo_ref, w_ref,
    *refs,
):
    sends, (gate_ref, mixed_ref, feat_ref, gext_ref, ext, table) = refs[:PIECES], refs[PIECES:]
    _, rows, chans = x_ref.shape
    blocks = rows // LANES
    count = LANES // group

    def tile(j, lanes):
        for part in range(3):
            at = LANES + 2 * part
            ext[part, 6:8, :] = halo_ref[at : at + 2, lanes].astype(F32)
            ext[part, 8:, :] = x_ref[part, :, lanes].astype(F32)
        keyed = feature(ext, taps_ref, lanes, 1, 0, rows)
        valued = feature(ext, taps_ref, lanes, 2, 0, rows)
        feat_ref[1, :, lanes] = keyed
        feat_ref[2, :, lanes] = valued
        gext_ref[0:LANES, lanes] = halo_ref[0:LANES, lanes]
        gext_ref[LANES:, lanes] = (keyed * valued).astype(BF16)
        filt = filt_ref[pl.ds(pl.multiple_of(j * count, count), count), :]
        turned = ((square(0) + square(1)) % LANES == 0).astype(BF16)
        fill_table(table, jnp.dot(filt, turned, preferred_element_type=F32), True)
        wide = jnp.dot(
            table[...], side_by_side(gext_ref, blocks, lanes), preferred_element_type=F32
        )
        mixed = pick_groups(wide, group, blocks)
        mixed_ref[:, lanes] = mixed
        query = feature(ext, taps_ref, lanes, 0, 0, rows)
        feat_ref[0, :, lanes] = query
        gate_ref[:, lanes] = (query * mixed).astype(BF16)

    each_tile(chans, tile)
    project(which_ref[0], gate_ref, w_ref, sends)


def project(which, gate_ref, w_ref, out_refs):
    half = w_ref.shape[1] // 2
    part = half // len(out_refs)
    for i, out_ref in enumerate(out_refs):
        cols = pl.ds(pl.multiple_of(which * half + i * part, part), part)
        out_ref[...] = jnp.dot(
            gate_ref[...], w_ref[:, cols], preferred_element_type=F32
        ).astype(BF16)


def keep_kernel(which_ref, gate_ref, w_ref, *keep_refs):
    project(which_ref[0], gate_ref, w_ref, keep_refs)


def lags_kernel(group, filt_ref, gg_ref, feat_ref, gext_ref, gm_ref, lags_ref, tables_ref, left):
    rows, chans = gg_ref.shape
    blocks = rows // LANES
    count = LANES // group

    def tile(j, lanes):
        filt = filt_ref[pl.ds(pl.multiple_of(j * count, count), count), :]
        fill_table(tables_ref.at[j], filt.astype(F32), False)
        grad_mixed = (gg_ref[:, lanes] * feat_ref[0, :, lanes]).astype(BF16)
        gm_ref[:, lanes] = grad_mixed
        lane = group_of_lane(LANES, group)
        for g in range(count):
            for b in range(blocks):
                left[g * LANES : (g + 1) * LANES, b * LANES : (b + 1) * LANES] = jnp.where(
                    lane == g, grad_mixed[b * LANES : (b + 1) * LANES, :], jnp.zeros((), BF16)
                )
        ends = [gext_ref[b * LANES : (b + 1) * LANES, lanes] for b in range(blocks + 1)]
        flip = (square(0) + square(1) == LANES - 1).astype(BF16)
        upside = jnp.dot(
            flip, jnp.concatenate(ends, axis=1), preferred_element_type=F32
        ).astype(BF16)
        right = jnp.concatenate([upside[:, 0 : blocks * LANES], upside[:, LANES:]], axis=0)
        products = lax.dot_general(
            left[...], right, (((1,), (1,)), ((), ())), preferred_element_type=F32
        )
        early = square(0) + square(1) < LANES - 1
        lag_rows = []
        for g in range(count):
            own = products[g * LANES : (g + 1) * LANES, :]
            ring = jnp.where(early, own[:, 0:LANES], own[:, LANES:])
            ring = pltpu.roll(ring, 0, 1, stride=1, stride_axis=0)
            lag_rows.append(jnp.sum(ring, axis=0, keepdims=True))
        lags_ref[:, lanes] = pltpu.roll(jnp.concatenate(lag_rows, axis=0), 1, 1)

    each_tile(chans, tile)


def backward_kernel(
    group, x_ref, taps_ref, filt_ref, halo_ref, gg_ref, mixed_ref, feat_ref, gext_ref, back_ref,
    gm_ref, lags_ref, tables_ref, gin_ref, sums_ref, ext, mext, gf,
):
    _, rows, chans = x_ref.shape
    blocks = rows // LANES
    count = LANES // group
    span = LANES + RIM

    def tile(j, lanes):
        for part in range(3):
            at = LANES + 2 * part
            ext[part, 6:8, :] = halo_ref[at : at + 2, lanes].astype(F32)
            ext[part, 8 : 8 + rows, :] = x_ref[part, :, lanes].astype(F32)
            at = span + 2 * part
            ext[part, 8 + rows : 10 + rows, :] = back_ref[at : at + 2, lanes].astype(F32)
        keyed = feat_ref[1, :, lanes]
        valued = feat_ref[2, :, lanes]
        query_next = feature(ext, taps_ref, lanes, 0, rows, 2)
        keyed_next = feature(ext, taps_ref, lanes, 1, rows, 2)
        valued_next = feature(ext, taps_ref, lanes, 2, rows, 2)
        gg_next = back_ref[span + 6 : span + 8, lanes].astype(F32) + back_ref[
            span + 8 : span + 10, lanes
        ].astype(F32)
        head = back_ref[0:span, lanes].astype(F32)
        mixed_next = (gg_next * query_next).astype(BF16).astype(F32)
        head = jnp.concatenate([mixed_next, head[2:]], axis=0)
        mext[0:rows, :] = gm_ref[:, lanes]
        mext[rows:, :] = head[0:LANES].astype(BF16)
        wide = jnp.dot(
            tables_ref[j], side_by_side(mext, blocks, slice(None)), preferred_element_type=F32
        )
        grad_gated = pick_groups(wide, group, blocks)
        filt = filt_ref[pl.ds(pl.multiple_of(j * count, count), count), :]
        taps = spread_taps(filt, group, False)
        taps_turned = spread_taps(filt, group, True)
        recent = gext_ref[rows:, lanes].astype(F32)
        gated_next = (keyed_next * valued_next).astype(BF16).astype(F32)
        recent = jnp.concatenate([recent, gated_next], axis=0)
        grads_next, mixes_next = [], []
        for t in range(2):
            grads_next.append(jnp.sum(taps * head[t : t + LANES], axis=0, keepdims=True))
            mixes_next.append(
                jnp.sum(taps_turned * recent[t + 1 : t + 1 + LANES], axis=0, keepdims=True)
            )
        grad_next = jnp.concatenate(grads_next, axis=0)
        mix_next = jnp.concatenate(mixes_next, axis=0)
        parts = (
            (gg_ref[:, lanes] * mixed_ref[:, lanes]).astype(BF16).astype(F32),
            (grad_gated * valued).astype(BF16).astype(F32),
            (grad_gated * keyed).astype(BF16).astype(F32),
        )
        following = (gg_next * mix_next, grad_next * valued_next, grad_next * keyed_next)
        short_rows = [[None] * 3 for _ in range(3)]
        for part in range(3):
            gf[part, 0:rows, :] = parts[part]
            gf[part, rows : rows + 2, :] = following[part].astype(BF16).astype(F32)
            total = taps_ref[0, part : part + 1, lanes] * parts[part]
            for lag in range(1, 3):
                tap = taps_ref[lag, part : part + 1, lanes]
                total = total + tap * gf[part, lag : lag + rows, :]
            gin_ref[part, :, lanes] = total.astype(BF16)
            for lag in range(3):
                short_rows[lag][part] = jnp.sum(
                    parts[part] * ext[part, 8 - lag : 8 - lag + rows, :], axis=0, keepdims=True
                )
        flat = [lags_ref[:, lanes]] + [short_rows[lag][part] for lag in range(3) for part in range(3)]
        flat.append(jnp.zeros((15, LANES), F32))
        sums_ref[:, lanes] = jnp.concatenate(flat, axis=0).astype(sums_ref.dtype)

    each_tile(chans, tile)


def unpack_kernel(group, short_scale, long_scale, *refs):
    short_ref, long_ref = refs[-2:]
    totals = [ref[...].astype(F32) for ref in refs[:-2]]
    while len(totals) > 1:
        totals = [sum(totals[i : i + 2]) for i in range(0, len(totals), 2)]
    total = totals[0]
    count = LANES // group
    for j in range(total.shape[1] // LANES):
        long_ref[j * count : (j + 1) * count, :] = (
            total[0:count, j * LANES : (j + 1) * LANES] * long_scale
        )
    for lag in range(3):
        for part in range(3):
            at = count + 3 * lag + part
            short_ref[lag, part : part + 1, :] = total[at : at + 1] * short_scale


def local(inputs, short_filter, long_filter, out_weight, out_cotangent):
    rows, _, chans = inputs.shape
    groups, span = long_filter.shape
    width = out_weight.shape[1]
    group = chans // groups
    count = LANES // group
    tokens_all = rows * lax.axis_size("ctx")
    n_tp = lax.axis_size("tp")
    signal = inputs.transpose(1, 0, 2)
    signal, short_filter, long_filter, out_weight, out_cotangent = [
        pltpu.with_memory_space_constraint(value, pltpu.HBM)
        for value in (signal, short_filter, long_filter, out_weight, out_cotangent)
    ]
    table = pltpu.VMEM((count * LANES, 2 * LANES), BF16)

    sent, signal, short_filter, long_filter = call(
        tail_kernel,
        "tail",
        (
            shape((LANES + RIM, chans), BF16),
            shape(signal.shape, BF16),
            shape(short_filter.shape, F32),
            shape(long_filter.shape, BF16),
        ),
        [pltpu.VMEM((3, 8 + RIM + LANES, LANES), F32), pltpu.SemaphoreType.DMA((5,))],
        far=3,
    )(signal, short_filter, long_filter)
    halo = shifted(sent, "ctx", 1)
    grad_gate, sent_back, out_weight = call(
        grad_gate_kernel,
        "grad_gate",
        (
            shape((rows, chans), F32),
            shape((LANES + 2 * RIM, chans), BF16),
            shape(out_weight.shape, BF16),
        ),
        [
            pltpu.VMEM(out_cotangent.shape, BF16),
            pltpu.VMEM((1, 8 + RIM + LANES, LANES), F32),
            pltpu.SemaphoreType.DMA,
            pltpu.SemaphoreType.DMA((max(1, chans // 256),)),
        ],
        far=2,
        operands=2,
    )(out_cotangent, out_weight, signal, short_filter)
    back = shifted(sent_back, "ctx", -1)
    core = lax.rem(lax.axis_index("tp"), 2)
    piece = shape((rows, width // 2 // PIECES), BF16)
    *other, gate_out, mixed, feat, gated = call(
        functools.partial(forward_kernel, group),
        "forward",
        (piece,) * PIECES
        + (
            shape((rows, chans), BF16),
            shape((rows, chans), F32),
            shape((3, rows, chans), F32),
            shape((LANES + rows, chans), BF16),
        ),
        [pltpu.VMEM((3, 8 + rows, LANES), F32), table],
        scalars=1,
        operands=5,
    )(jnp.reshape(1 - core, (1,)), signal, short_filter, long_filter, halo, out_weight)
    theirs = [lax.ppermute(value, "tp", pairwise("tp", 1)) for value in other]
    kept = call(keep_kernel, "keep", (piece,) * PIECES, scalars=1, operands=2)(
        jnp.reshape(core, (1,)), gate_out, out_weight
    )
    mine = [
        (a.astype(F32) + b.astype(F32)).astype(BF16) for a, b in zip(kept, theirs, strict=True)
    ]
    step = 2
    got = [lax.ppermute(value, "tp", pairwise("tp", step)) for value in mine]

    grad_mixed, lags, tables = call(
        functools.partial(lags_kernel, group),
        "lags",
        (
            shape((rows, chans), BF16),
            shape((count, chans), F32),
            shape((chans // LANES, count * LANES, 2 * LANES), BF16),
        ),
        [pltpu.VMEM((count * LANES, (rows // LANES) * LANES), BF16)],
        operands=4,
    )(long_filter, grad_gate, feat, gated)
    n_ctx = lax.axis_size("ctx")
    by_pairs = n_ctx & (n_ctx - 1) == 0
    grad_in, sums = call(
        functools.partial(backward_kernel, group),
        "backward",
        (shape((3, rows, chans), BF16), shape((32, chans), BF16 if by_pairs else F32)),
        [
            pltpu.VMEM((3, rows + 16, LANES), F32),
            pltpu.VMEM((rows + LANES, LANES), BF16),
            pltpu.VMEM((3, rows + 8, LANES), F32),
        ],
        operands=12,
    )(
        signal, short_filter, long_filter, halo, grad_gate, mixed, feat, gated, back,
        grad_mixed, lags, tables,
    )
    if by_pairs:
        hop = 1
        while hop < max(2, n_ctx // 4):
            rest = lax.ppermute(sums, "ctx", pairwise("ctx", hop))
            sums = (sums.astype(F32) + rest.astype(F32)).astype(BF16)
            hop *= 2
        terms = [sums]
        for other_hop in range(hop, n_ctx, hop):
            terms.append(lax.ppermute(sums, "ctx", pairwise("ctx", other_hop)))
    else:
        terms = [lax.psum(sums, "ctx")]
    got, terms[:4] = lax.optimization_barrier((got, terms[:4]))
    mine = [
        (a.astype(F32) + b.astype(F32)).astype(BF16) for a, b in zip(mine, got, strict=True)
    ]
    step *= 2
    while step < n_tp:
        got = [lax.ppermute(value, "tp", pairwise("tp", step)) for value in mine]
        mine = [
            (a.astype(F32) + b.astype(F32)).astype(BF16) for a, b in zip(mine, got, strict=True)
        ]
        step *= 2
    sibling = [lax.ppermute(value, "tp", pairwise("tp", 1)) for value in mine]
    result = jnp.where(
        core == 0,
        jnp.concatenate(mine + sibling, axis=1),
        jnp.concatenate(sibling + mine, axis=1),
    )
    grad_short, grad_long = call(
        functools.partial(
            unpack_kernel, group, float(tokens_all) ** (-0.5), float(tokens_all * group) ** (-0.5)
        ),
        "unpack",
        (shape((3, 3, chans), F32), shape((groups, span), F32)),
        operands=len(terms),
    )(*terms)
    return (result, grad_in.transpose(1, 0, 2), grad_short, grad_long)


def solution(mesh):
    in_specs = (
        P("ctx", None, "tp"),
        P(None, None, "tp"),
        P("tp", None),
        P("tp", None),
        P("ctx", None),
    )
    out_specs = (P("ctx", None), P("ctx", None, "tp"), P(None, None, "tp"), P("tp", None))
    return jax.shard_map(local, mesh=mesh, in_specs=in_specs, out_specs=out_specs, check_vma=False)
```

```python
import functools

import jax
import jax.numpy as jnp
from jax import lax
from jax.experimental import pallas as pl
from jax.experimental.pallas import tpu as pltpu
from jax.sharding import PartitionSpec as P

LANES = 128
RIM = 16
COST = 1024
PIECES = 2
F32 = jnp.float32
BF16 = jnp.bfloat16
VMEM_LIMIT = 12 * 1024 * 1024


def pairwise(axis, step):
    return [(source, source ^ step) for source in range(lax.axis_size(axis))]


def shifted(value, axis, steps):
    count = lax.axis_size(axis)
    initial, last = (max(0, -steps), min(count, count - steps))
    return lax.ppermute(value, axis, [(source, source + steps) for source in range(initial, last)])


def call(body, name, outs, scratch=(), scalars=0, far=0, operands=0, cost=COST):
    specs = [pl.BlockSpec(memory_space=pltpu.SMEM)] * scalars
    specs += [pl.BlockSpec(memory_space=pltpu.HBM)] * far
    specs += [pl.BlockSpec(memory_space=pltpu.VMEM)] * operands
    return pl.pallas_call(
        body,
        out_shape=outs,
        in_specs=specs,
        out_specs=jax.tree.map(lambda _: pl.BlockSpec(memory_space=pltpu.VMEM), outs),
        scratch_shapes=scratch,
        compiler_params=pltpu.CompilerParams(vmem_limit_bytes=VMEM_LIMIT),
        cost_estimate=pl.CostEstimate(flops=0, transcendentals=0, bytes_accessed=cost),
        name=name,
    )


def shape(dims, dtype):
    return jax.ShapeDtypeStruct(dims, dtype)


def each_tile(chans, body):
    def step(j, carry):
        body(j, pl.ds(pl.multiple_of(j * LANES, LANES), LANES))
        return carry

    lax.fori_loop(0, chans // LANES, step, 0, unroll=2)


def feature(ext_ref, taps_ref, lanes, part, start, rows):
    total = taps_ref[0, part : part + 1, lanes] * ext_ref[part, 8 + start : 8 + start + rows, :]
    for lag in range(1, 3):
        first = 8 + start - lag
        tap = taps_ref[lag, part : part + 1, lanes]
        total = total + tap * ext_ref[part, first : first + rows, :]
    return total


def group_of_lane(rows, group):
    return lax.broadcasted_iota(jnp.int32, (rows, LANES), 1) // group


def square(axis):
    return lax.broadcasted_iota(jnp.int32, (LANES, LANES), axis)


def fill_table(table_ref, taps, forward):
    early = (square(1) > square(0)) if forward else (square(1) >= square(0))
    for g in range(taps.shape[0]):
        wide = jnp.broadcast_to(taps[g : g + 1, :], (LANES, LANES))
        ring = pltpu.roll(wide, 0, 1, stride=1, stride_axis=0)
        table_ref[g * LANES : (g + 1) * LANES, 0:LANES] = jnp.where(early, ring, 0.0).astype(BF16)
        table_ref[g * LANES : (g + 1) * LANES, LANES:] = jnp.where(early, 0.0, ring).astype(BF16)


def pick_groups(wide, group, blocks):
    lane = group_of_lane(LANES, group)
    outs = []
    for b in range(blocks):
        total = wide[0:LANES, b * LANES : (b + 1) * LANES]
        for g in range(1, LANES // group):
            part = wide[g * LANES : (g + 1) * LANES, b * LANES : (b + 1) * LANES]
            total = jnp.where(lane == g, part, total)
        outs.append(total)
    return jnp.concatenate(outs, axis=0)


def side_by_side(ref, blocks, lanes):
    return jnp.concatenate([ref[b * LANES : (b + 2) * LANES, lanes] for b in range(blocks)], axis=1)


def spread_taps(filt, group, reverse):
    count = filt.shape[0]
    owner = (
        group_of_lane(count, group) == lax.broadcasted_iota(jnp.int32, (count, LANES), 0)
    ).astype(BF16)
    if reverse:
        flip = (square(0) + square(1) == LANES - 1).astype(BF16)
        filt = jnp.dot(filt, flip, preferred_element_type=F32).astype(BF16)
    return lax.dot_general(filt, owner, (((0,), (0,)), ((), ())), preferred_element_type=F32)


def tail_kernel(
    x_hbm, taps_hbm, filt_hbm, sent_ref, x_ref, taps_ref, filt_ref, ext, sems
):
    _, rows, chans = x_ref.shape
    first = rows - LANES - RIM
    near = (pl.ds(1, 2), pl.ds(first, LANES + RIM))
    copies = [
        pltpu.make_async_copy(taps_hbm, taps_ref, sems.at[0]),
        pltpu.make_async_copy(x_hbm.at[near], x_ref.at[near], sems.at[1]),
        pltpu.make_async_copy(x_hbm.at[0], x_ref.at[0], sems.at[2]),
        pltpu.make_async_copy(
            x_hbm.at[1:3, 0:first], x_ref.at[1:3, 0:first], sems.at[3]
        ),
        pltpu.make_async_copy(filt_hbm, filt_ref, sems.at[4]),
    ]
    for copy in copies:
        copy.start()
    for copy in copies[:3]:
        copy.wait()

    def tile(j, lanes):
        for part in range(3):
            ext[part, 8:, :] = x_ref[part, first:, lanes].astype(F32)
        keyed = feature(ext, taps_ref, lanes, 1, RIM, LANES)
        valued = feature(ext, taps_ref, lanes, 2, RIM, LANES)
        sent_ref[0:LANES, lanes] = (keyed * valued).astype(BF16)
        end = 8 + RIM + LANES
        rim = [ext[part, end - 2 : end, :] for part in range(3)]
        rim.append(jnp.zeros((RIM - 6, LANES), F32))
        sent_ref[LANES:, lanes] = jnp.concatenate(rim, axis=0).astype(BF16)

    each_tile(chans, tile)
    for copy in copies[3:]:
        copy.wait()


def grad_gate_kernel(
    c_hbm, w_hbm, x_ref, taps_ref, gg_ref, back_ref, w_ref, c_ref, ext, c_sem, w_sems
):
    chans = w_ref.shape[0]
    chunks = w_sems.shape[0]
    wide = chans // chunks
    span = LANES + RIM

    def chunk(j):
        rows = pl.ds(pl.multiple_of(j * wide, wide), wide)
        return pltpu.make_async_copy(w_hbm.at[rows], w_ref.at[rows], w_sems.at[j])

    load = pltpu.make_async_copy(c_hbm, c_ref, c_sem)
    load.start()
    for j in range(min(2, chunks)):
        chunk(j).start()
    load.wait()

    def product(j, carry):
        chunk(j).wait()

        @pl.when(j + 2 < chunks)
        def _():
            chunk(j + 2).start()

        cols = pl.ds(pl.multiple_of(j * wide, wide), wide)
        gg_ref[:, cols] = lax.dot_general(
            c_ref[...], w_ref[cols, :], (((1,), (1,)), ((), ())), preferred_element_type=F32
        )
        return carry

    lax.fori_loop(0, chunks, product, 0)

    def tile(j, lanes):
        ext[0, 0:8, :] = jnp.zeros((8, LANES), F32)
        ext[0, 8:, :] = x_ref[0, 0:span, lanes].astype(F32)
        query = feature(ext, taps_ref, lanes, 0, 0, span)
        back_ref[0:span, lanes] = (gg_ref[0:span, lanes] * query).astype(BF16)
        grad = gg_ref[0:2, lanes]
        high = grad.astype(BF16).astype(F32)
        rim = [x_ref[part, 0:RIM, lanes].astype(F32)[0:2] for part in range(3)]
        rim += [high, grad - high, jnp.zeros((RIM - 10, LANES), F32)]
        back_ref[span:, lanes] = jnp.concatenate(rim, axis=0).astype(BF16)

    each_tile(chans, tile)


def forward_kernel(
    group, which_ref, x_ref, taps_ref, filt_ref, halo_ref, w_ref,
    *refs,
):
    sends, (gate_ref, mixed_ref, feat_ref, gext_ref, ext, table) = refs[:PIECES], refs[PIECES:]
    _, rows, chans = x_ref.shape
    blocks = rows // LANES
    count = LANES // group

    def tile(j, lanes):
        for part in range(3):
            at = LANES + 2 * part
            ext[part, 6:8, :] = halo_ref[at : at + 2, lanes].astype(F32)
            ext[part, 8:, :] = x_ref[part, :, lanes].astype(F32)
        keyed = feature(ext, taps_ref, lanes, 1, 0, rows)
        valued = feature(ext, taps_ref, lanes, 2, 0, rows)
        feat_ref[1, :, lanes] = keyed
        feat_ref[2, :, lanes] = valued
        gext_ref[0:LANES, lanes] = halo_ref[0:LANES, lanes]
        gext_ref[LANES:, lanes] = (keyed * valued).astype(BF16)
        filt = filt_ref[pl.ds(pl.multiple_of(j * count, count), count), :]
        turned = ((square(0) + square(1)) % LANES == 0).astype(BF16)
        fill_table(table, jnp.dot(filt, turned, preferred_element_type=F32), True)
        wide = jnp.dot(
            table[...], side_by_side(gext_ref, blocks, lanes), preferred_element_type=F32
        )
        mixed = pick_groups(wide, group, blocks)
        mixed_ref[:, lanes] = mixed
        query = feature(ext, taps_ref, lanes, 0, 0, rows)
        feat_ref[0, :, lanes] = query
        gate_ref[:, lanes] = (query * mixed).astype(BF16)

    each_tile(chans, tile)
    project(which_ref[0], gate_ref, w_ref, sends)


def project(which, gate_ref, w_ref, out_refs):
    half = w_ref.shape[1] // 2
    part = half // len(out_refs)
    for i, out_ref in enumerate(out_refs):
        cols = pl.ds(pl.multiple_of(which * half + i * part, part), part)
        out_ref[...] = jnp.dot(
            gate_ref[...], w_ref[:, cols], preferred_element_type=F32
        ).astype(BF16)


def keep_kernel(which_ref, gate_ref, w_ref, *keep_refs):
    project(which_ref[0], gate_ref, w_ref, keep_refs)


def short_sums(grad, ext_ref, part):
    rows = grad.shape[0]
    return [
        jnp.sum(grad * ext_ref[part, 8 - lag : 8 - lag + rows, :], axis=0, keepdims=True)
        for lag in range(3)
    ]


def lags_kernel(
    group, filt_ref, x_ref, halo_ref, gg_ref, mixed_ref, feat_ref, gext_ref,
    gm_ref, gq_ref, lags_ref, tables_ref, left, ext,
):
    rows, chans = gg_ref.shape
    blocks = rows // LANES
    count = LANES // group

    def tile(j, lanes):
        filt = filt_ref[pl.ds(pl.multiple_of(j * count, count), count), :]
        fill_table(tables_ref.at[j], filt.astype(F32), False)
        grad_mixed = (gg_ref[:, lanes] * feat_ref[0, :, lanes]).astype(BF16)
        gm_ref[:, lanes] = grad_mixed
        grad_query = (gg_ref[:, lanes] * mixed_ref[:, lanes]).astype(BF16)
        gq_ref[:, lanes] = grad_query
        ext[0, 6:8, :] = halo_ref[LANES : LANES + 2, lanes].astype(F32)
        ext[0, 8:, :] = x_ref[0, :, lanes].astype(F32)
        sums = short_sums(grad_query.astype(F32), ext, 0)
        lane = group_of_lane(LANES, group)
        for g in range(count):
            for b in range(blocks):
                left[g * LANES : (g + 1) * LANES, b * LANES : (b + 1) * LANES] = jnp.where(
                    lane == g, grad_mixed[b * LANES : (b + 1) * LANES, :], jnp.zeros((), BF16)
                )
        ends = [gext_ref[b * LANES : (b + 1) * LANES, lanes] for b in range(blocks + 1)]
        flip = (square(0) + square(1) == LANES - 1).astype(BF16)
        upside = jnp.dot(
            flip, jnp.concatenate(ends, axis=1), preferred_element_type=F32
        ).astype(BF16)
        right = jnp.concatenate([upside[:, 0 : blocks * LANES], upside[:, LANES:]], axis=0)
        products = lax.dot_general(
            left[...], right, (((1,), (1,)), ((), ())), preferred_element_type=F32
        )
        early = square(0) + square(1) < LANES - 1
        lag_rows = []
        for g in range(count):
            own = products[g * LANES : (g + 1) * LANES, :]
            ring = jnp.where(early, own[:, 0:LANES], own[:, LANES:])
            ring = pltpu.roll(ring, 0, 1, stride=1, stride_axis=0)
            lag_rows.append(jnp.sum(ring, axis=0, keepdims=True))
        lags = pltpu.roll(jnp.concatenate(lag_rows, axis=0), 1, 1)
        sums.append(jnp.zeros((16 - count - 3, LANES), F32))
        lags_ref[:, lanes] = jnp.concatenate([lags] + sums, axis=0)

    each_tile(chans, tile)


def next_rows(ext_ref, taps_ref, x_ref, back_ref, lanes, parts):
    rows = x_ref.shape[1]
    span = LANES + RIM
    outs = []
    for part in parts:
        recent = x_ref[part, rows - RIM :, lanes].astype(F32)
        at = span + 2 * part
        ext_ref[part, 0:8, :] = recent[RIM - 8 :]
        ext_ref[part, 8:10, :] = back_ref[at : at + 2, lanes].astype(F32)
        outs.append(feature(ext_ref, taps_ref, lanes, part, 0, 2))
    high = back_ref[span + 6 : span + 8, lanes].astype(F32)
    low = back_ref[span + 8 : span + 10, lanes].astype(F32)
    return outs, high + low


def next_mixed(back_ref, lanes, grad, query):
    head = back_ref[0 : LANES + RIM, lanes].astype(F32)
    first = (grad * query).astype(BF16).astype(F32)
    return jnp.concatenate([first, head[2:]], axis=0)


def backward_kernel(
    group, x_ref, taps_ref, halo_ref, feat_ref, back_ref, gm_ref, lags_ref, tables_ref,
    gkv_ref, sums_ref, ext, mext, near,
):
    _, rows, chans = x_ref.shape
    blocks = rows // LANES
    count = LANES // group

    def tile(j, lanes):
        for part in range(1, 3):
            at = LANES + 2 * part
            ext[part, 6:8, :] = halo_ref[at : at + 2, lanes].astype(F32)
            ext[part, 8:, :] = x_ref[part, :, lanes].astype(F32)
        (query_next,), gg_next = next_rows(near, taps_ref, x_ref, back_ref, lanes, (0,))
        head = next_mixed(back_ref, lanes, gg_next, query_next)
        mext[0:rows, :] = gm_ref[:, lanes]
        mext[rows:, :] = head[0:LANES].astype(BF16)
        wide = jnp.dot(
            tables_ref[j], side_by_side(mext, blocks, slice(None)), preferred_element_type=F32
        )
        grad_gated = pick_groups(wide, group, blocks)
        sums = [None] * 3
        for part in range(1, 3):
            grad = (grad_gated * feat_ref[3 - part, :, lanes]).astype(BF16)
            gkv_ref[part - 1, :, lanes] = grad
            sums[part] = short_sums(grad.astype(F32), ext, part)
        early = lags_ref[:, lanes]
        flat = [early[0:count]]
        for lag in range(3):
            flat += [early[count + lag : count + lag + 1], sums[1][lag], sums[2][lag]]
        flat.append(jnp.zeros((32 - count - 9, LANES), F32))
        sums_ref[:, lanes] = jnp.concatenate(flat, axis=0).astype(sums_ref.dtype)

    each_tile(chans, tile)


def inputs_kernel(
    group, x_ref, taps_ref, filt_ref, gext_ref, back_ref, gq_ref, gkv_ref, gin_ref, near, gf
):
    _, rows, chans = x_ref.shape
    count = LANES // group

    def tile(j, lanes):
        (query, keyed, valued), grad = next_rows(
            near, taps_ref, x_ref, back_ref, lanes, (0, 1, 2)
        )
        head = next_mixed(back_ref, lanes, grad, query)
        filt = filt_ref[pl.ds(pl.multiple_of(j * count, count), count), :]
        taps = spread_taps(filt, group, False)
        taps_turned = spread_taps(filt, group, True)
        recent = gext_ref[rows:, lanes].astype(F32)
        recent = jnp.concatenate([recent, (keyed * valued).astype(BF16).astype(F32)], axis=0)
        gated, mixed = [], []
        for t in range(2):
            gated.append(jnp.sum(taps * head[t : t + LANES], axis=0, keepdims=True))
            mixed.append(
                jnp.sum(taps_turned * recent[t + 1 : t + 1 + LANES], axis=0, keepdims=True)
            )
        gated, mixed = jnp.concatenate(gated, axis=0), jnp.concatenate(mixed, axis=0)
        following = (grad * mixed, gated * valued, gated * keyed)
        for part in range(3):
            own = gq_ref[:, lanes] if part == 0 else gkv_ref[part - 1, :, lanes]
            gf[part, 0:rows, :] = own.astype(F32)
            gf[part, rows : rows + 2, :] = following[part].astype(BF16).astype(F32)
            total = taps_ref[0, part : part + 1, lanes] * gf[part, 0:rows, :]
            for lag in range(1, 3):
                tap = taps_ref[lag, part : part + 1, lanes]
                total = total + tap * gf[part, lag : lag + rows, :]
            gin_ref[part, :, lanes] = total.astype(BF16)

    each_tile(chans, tile)


def unpack_kernel(group, short_scale, long_scale, *refs):
    short_ref, long_ref = refs[-2:]
    totals = [ref[...].astype(F32) for ref in refs[:-2]]
    while len(totals) > 1:
        totals = [sum(totals[i : i + 2]) for i in range(0, len(totals), 2)]
    total = totals[0]
    count = LANES // group
    for j in range(total.shape[1] // LANES):
        long_ref[j * count : (j + 1) * count, :] = (
            total[0:count, j * LANES : (j + 1) * LANES] * long_scale
        )
    for lag in range(3):
        for part in range(3):
            at = count + 3 * lag + part
            short_ref[lag, part : part + 1, :] = total[at : at + 1] * short_scale


def local(inputs, short_filter, long_filter, out_weight, out_cotangent):
    rows, _, chans = inputs.shape
    groups, span = long_filter.shape
    width = out_weight.shape[1]
    group = chans // groups
    count = LANES // group
    tokens_all = rows * lax.axis_size("ctx")
    n_tp = lax.axis_size("tp")
    signal = inputs.transpose(1, 0, 2)
    signal, short_filter, long_filter, out_weight, out_cotangent = [
        pltpu.with_memory_space_constraint(value, pltpu.HBM)
        for value in (signal, short_filter, long_filter, out_weight, out_cotangent)
    ]
    table = pltpu.VMEM((count * LANES, 2 * LANES), BF16)

    sent, signal, short_filter, long_filter = call(
        tail_kernel,
        "tail",
        (
            shape((LANES + RIM, chans), BF16),
            shape(signal.shape, BF16),
            shape(short_filter.shape, F32),
            shape(long_filter.shape, BF16),
        ),
        [pltpu.VMEM((3, 8 + RIM + LANES, LANES), F32), pltpu.SemaphoreType.DMA((5,))],
        far=3,
    )(signal, short_filter, long_filter)
    halo = shifted(sent, "ctx", 1)
    grad_gate, sent_back, out_weight = call(
        grad_gate_kernel,
        "grad_gate",
        (
            shape((rows, chans), F32),
            shape((LANES + 2 * RIM, chans), BF16),
            shape(out_weight.shape, BF16),
        ),
        [
            pltpu.VMEM(out_cotangent.shape, BF16),
            pltpu.VMEM((1, 8 + RIM + LANES, LANES), F32),
            pltpu.SemaphoreType.DMA,
            pltpu.SemaphoreType.DMA((max(1, chans // 256),)),
        ],
        far=2,
        operands=2,
    )(out_cotangent, out_weight, signal, short_filter)
    back = shifted(sent_back, "ctx", -1)
    core = lax.rem(lax.axis_index("tp"), 2)
    piece = shape((rows, width // 2 // PIECES), BF16)
    *other, gate_out, mixed, feat, gated = call(
        functools.partial(forward_kernel, group),
        "forward",
        (piece,) * PIECES
        + (
            shape((rows, chans), BF16),
            shape((rows, chans), F32),
            shape((3, rows, chans), F32),
            shape((LANES + rows, chans), BF16),
        ),
        [pltpu.VMEM((3, 8 + rows, LANES), F32), table],
        scalars=1,
        operands=5,
    )(jnp.reshape(1 - core, (1,)), signal, short_filter, long_filter, halo, out_weight)
    theirs = [lax.ppermute(value, "tp", pairwise("tp", 1)) for value in other]
    kept = call(keep_kernel, "keep", (piece,) * PIECES, scalars=1, operands=2)(
        jnp.reshape(core, (1,)), gate_out, out_weight
    )
    mine = [
        (a.astype(F32) + b.astype(F32)).astype(BF16) for a, b in zip(kept, theirs, strict=True)
    ]
    step = 2
    got = [lax.ppermute(value, "tp", pairwise("tp", step)) for value in mine]

    ext = pltpu.VMEM((3, rows + 8, LANES), F32)
    near = pltpu.VMEM((3, 16, LANES), F32)
    grad_mixed, grad_query, lags, tables = call(
        functools.partial(lags_kernel, group),
        "lags",
        (
            shape((rows, chans), BF16),
            shape((rows, chans), BF16),
            shape((16, chans), F32),
            shape((chans // LANES, count * LANES, 2 * LANES), BF16),
        ),
        [pltpu.VMEM((count * LANES, (rows // LANES) * LANES), BF16), ext],
        operands=7,
    )(long_filter, signal, halo, grad_gate, mixed, feat, gated)
    n_ctx = lax.axis_size("ctx")
    by_pairs = n_ctx & (n_ctx - 1) == 0
    grad_rest, sums = call(
        functools.partial(backward_kernel, group),
        "backward",
        (shape((2, rows, chans), BF16), shape((32, chans), BF16 if by_pairs else F32)),
        [ext, pltpu.VMEM((rows + LANES, LANES), BF16), near],
        operands=8,
    )(signal, short_filter, halo, feat, back, grad_mixed, lags, tables)
    grad_in = call(
        functools.partial(inputs_kernel, group),
        "inputs",
        shape((3, rows, chans), BF16),
        [near, pltpu.VMEM((3, rows + 8, LANES), F32)],
        operands=7,
    )(signal, short_filter, long_filter, gated, back, grad_query, grad_rest)
    if by_pairs:
        hop = 1
        terms = [sums]
        while hop < n_ctx:
            if len(terms) > 1:
                pairs = [a.astype(F32) + b.astype(F32) for a, b in zip(terms[::2], terms[1::2])]
                terms = [sum(pairs).astype(BF16)]
            radix = min(4, n_ctx // hop)
            terms += [
                lax.ppermute(terms[0], "ctx", pairwise("ctx", i * hop)) for i in range(1, radix)
            ]
            hop *= radix
    else:
        terms = [lax.psum(sums, "ctx")]
    got, terms, grad_in = lax.optimization_barrier((got, terms, grad_in))
    mine = [
        (a.astype(F32) + b.astype(F32)).astype(BF16) for a, b in zip(mine, got, strict=True)
    ]
    step *= 2
    while step < n_tp:
        got = [lax.ppermute(value, "tp", pairwise("tp", step)) for value in mine]
        mine = [
            (a.astype(F32) + b.astype(F32)).astype(BF16) for a, b in zip(mine, got, strict=True)
        ]
        step *= 2
    sibling = [lax.ppermute(value, "tp", pairwise("tp", 1)) for value in mine]
    result = jnp.where(
        core == 0,
        jnp.concatenate(mine + sibling, axis=1),
        jnp.concatenate(sibling + mine, axis=1),
    )
    grad_short, grad_long = call(
        functools.partial(
            unpack_kernel, group, float(tokens_all) ** (-0.5), float(tokens_all * group) ** (-0.5)
        ),
        "unpack",
        (shape((3, 3, chans), F32), shape((groups, span), F32)),
        operands=len(terms),
    )(*terms)
    return (result, grad_in.transpose(1, 0, 2), grad_short, grad_long)


def solution(mesh):
    in_specs = (
        P("ctx", None, "tp"),
        P(None, None, "tp"),
        P("tp", None),
        P("tp", None),
        P("ctx", None),
    )
    out_specs = (P("ctx", None), P("ctx", None, "tp"), P(None, None, "tp"), P("tp", None))
    return jax.shard_map(local, mesh=mesh, in_specs=in_specs, out_specs=out_specs, check_vma=False)
```

```python
import functools

import jax
import jax.numpy as jnp
from jax import lax
from jax.experimental import pallas as pl
from jax.experimental.pallas import tpu as pltpu
from jax.sharding import PartitionSpec as P

LANES = 128
RIM = 16
SUB = 32
COST = 1024
PIECES = 2
F32 = jnp.float32
BF16 = jnp.bfloat16
VMEM_LIMIT = 12 * 1024 * 1024


def pairwise(axis, step):
    return [(source, source ^ step) for source in range(lax.axis_size(axis))]


def shifted(value, axis, steps):
    count = lax.axis_size(axis)
    initial, last = (max(0, -steps), min(count, count - steps))
    return lax.ppermute(value, axis, [(source, source + steps) for source in range(initial, last)])


def call(body, name, outs, scratch=(), scalars=0, far=0, operands=0, cost=COST):
    specs = [pl.BlockSpec(memory_space=pltpu.SMEM)] * scalars
    specs += [pl.BlockSpec(memory_space=pltpu.HBM)] * far
    specs += [pl.BlockSpec(memory_space=pltpu.VMEM)] * operands
    return pl.pallas_call(
        body,
        out_shape=outs,
        in_specs=specs,
        out_specs=jax.tree.map(lambda _: pl.BlockSpec(memory_space=pltpu.VMEM), outs),
        scratch_shapes=scratch,
        compiler_params=pltpu.CompilerParams(vmem_limit_bytes=VMEM_LIMIT),
        cost_estimate=pl.CostEstimate(flops=0, transcendentals=0, bytes_accessed=cost),
        name=name,
    )


def shape(dims, dtype):
    return jax.ShapeDtypeStruct(dims, dtype)


def each_tile(chans, body, *scratch):
    for j in range(chans // LANES):
        body(j, slice(j * LANES, (j + 1) * LANES), *[ref.at[j] for ref in scratch])


def feature(ext_ref, taps_ref, lanes, part, start, rows):
    total = taps_ref[0, part : part + 1, lanes] * ext_ref[part, 8 + start : 8 + start + rows, :]
    for lag in range(1, 3):
        first = 8 + start - lag
        tap = taps_ref[lag, part : part + 1, lanes]
        total = total + tap * ext_ref[part, first : first + rows, :]
    return total


def group_of_lane(rows, group):
    return lax.broadcasted_iota(jnp.int32, (rows, LANES), 1) // group


def grid_of(rows, axis):
    return lax.broadcasted_iota(jnp.int32, (rows, LANES), axis)


def fill_table(table_ref, taps, forward):
    row, col = grid_of(SUB, 0), grid_of(SUB, 1)
    early = (col > row) if forward else (col >= row)
    for g in range(taps.shape[0]):
        wide = jnp.broadcast_to(taps[g : g + 1, :], (SUB, LANES))
        ring = pltpu.roll(wide, 0, 1, stride=1, stride_axis=0)
        rows = slice(g * SUB, (g + 1) * SUB)
        table_ref[rows, 0:LANES] = jnp.where(early, ring, 0.0).astype(BF16)
        table_ref[rows, LANES:] = jnp.where(early, 0.0, ring)[:, 0:SUB].astype(BF16)


def pick_groups(wide, group, blocks):
    lane = group_of_lane(SUB, group)
    outs = []
    for b in range(blocks):
        cols = slice(b * LANES, (b + 1) * LANES)
        total = wide[0:SUB, cols]
        for g in range(1, LANES // group):
            total = jnp.where(lane == g, wide[g * SUB : (g + 1) * SUB, cols], total)
        outs.append(total)
    return jnp.concatenate(outs, axis=0)


def windows(ref, blocks, lanes):
    return jnp.concatenate(
        [ref[b * SUB : (b + 1) * SUB + LANES, lanes] for b in range(blocks)], axis=1
    )


def spread_taps(filt, group, reverse):
    count = filt.shape[0]
    owner = (
        group_of_lane(count, group) == lax.broadcasted_iota(jnp.int32, (count, LANES), 0)
    ).astype(BF16)
    if reverse:
        flip = (grid_of(LANES, 0) + grid_of(LANES, 1) == LANES - 1).astype(BF16)
        filt = jnp.dot(filt, flip, preferred_element_type=F32).astype(BF16)
    return lax.dot_general(filt, owner, (((0,), (0,)), ((), ())), preferred_element_type=F32)


def tail_kernel(
    x_hbm, taps_hbm, filt_hbm, sent_ref, x_ref, taps_ref, filt_ref, ext_ref, sems
):
    _, rows, chans = x_ref.shape
    first = rows - LANES - RIM
    near = (pl.ds(1, 2), pl.ds(first, LANES + RIM))
    copies = [
        pltpu.make_async_copy(taps_hbm, taps_ref, sems.at[0]),
        pltpu.make_async_copy(x_hbm.at[near], x_ref.at[near], sems.at[1]),
        pltpu.make_async_copy(x_hbm.at[0], x_ref.at[0], sems.at[2]),
        pltpu.make_async_copy(
            x_hbm.at[1:3, 0:first], x_ref.at[1:3, 0:first], sems.at[3]
        ),
        pltpu.make_async_copy(filt_hbm, filt_ref, sems.at[4]),
    ]
    for copy in copies:
        copy.start()
    for copy in copies[:3]:
        copy.wait()

    def tile(j, lanes, ext):
        for part in range(3):
            ext[part, 8:, :] = x_ref[part, first:, lanes].astype(F32)
        keyed = feature(ext, taps_ref, lanes, 1, RIM, LANES)
        valued = feature(ext, taps_ref, lanes, 2, RIM, LANES)
        sent_ref[0:LANES, lanes] = (keyed * valued).astype(BF16)
        end = 8 + RIM + LANES
        rim = [ext[part, end - 2 : end, :] for part in range(3)]
        rim.append(jnp.zeros((RIM - 6, LANES), F32))
        sent_ref[LANES:, lanes] = jnp.concatenate(rim, axis=0).astype(BF16)

    each_tile(chans, tile, ext_ref)
    for copy in copies[3:]:
        copy.wait()


def grad_gate_kernel(
    c_hbm, w_hbm, x_ref, taps_ref, gg_ref, back_ref, w_ref, c_ref, ext_ref, c_sem, w_sems
):
    chans = w_ref.shape[0]
    chunks = w_sems.shape[0]
    wide = chans // chunks
    span = LANES + RIM

    def chunk(j):
        rows = pl.ds(pl.multiple_of(j * wide, wide), wide)
        return pltpu.make_async_copy(w_hbm.at[rows], w_ref.at[rows], w_sems.at[j])

    load = pltpu.make_async_copy(c_hbm, c_ref, c_sem)
    load.start()
    for j in range(min(2, chunks)):
        chunk(j).start()
    load.wait()

    def product(j, carry):
        chunk(j).wait()

        @pl.when(j + 2 < chunks)
        def _():
            chunk(j + 2).start()

        cols = pl.ds(pl.multiple_of(j * wide, wide), wide)
        gg_ref[:, cols] = lax.dot_general(
            c_ref[...], w_ref[cols, :], (((1,), (1,)), ((), ())), preferred_element_type=F32
        )
        return carry

    lax.fori_loop(0, chunks, product, 0)

    def tile(j, lanes, ext):
        ext[0, 0:8, :] = jnp.zeros((8, LANES), F32)
        ext[0, 8:, :] = x_ref[0, 0:span, lanes].astype(F32)
        query = feature(ext, taps_ref, lanes, 0, 0, span)
        back_ref[0:span, lanes] = (gg_ref[0:span, lanes] * query).astype(BF16)
        grad = gg_ref[0:2, lanes]
        high = grad.astype(BF16).astype(F32)
        rim = [x_ref[part, 0:RIM, lanes].astype(F32)[0:2] for part in range(3)]
        rim += [high, grad - high, jnp.zeros((RIM - 10, LANES), F32)]
        back_ref[span:, lanes] = jnp.concatenate(rim, axis=0).astype(BF16)

    each_tile(chans, tile, ext_ref)


def forward_kernel(
    group, which_ref, x_ref, taps_ref, filt_ref, halo_ref, w_ref,
    *refs,
):
    sends, (gate_ref, mixed_ref, feat_ref, gext_ref, ext_ref, table_ref) = refs[:PIECES], refs[PIECES:]
    _, rows, chans = x_ref.shape
    blocks = rows // SUB
    count = LANES // group

    def tile(j, lanes, ext, table):
        for part in range(3):
            at = LANES + 2 * part
            ext[part, 6:8, :] = halo_ref[at : at + 2, lanes].astype(F32)
            ext[part, 8:, :] = x_ref[part, :, lanes].astype(F32)
        keyed = feature(ext, taps_ref, lanes, 1, 0, rows)
        valued = feature(ext, taps_ref, lanes, 2, 0, rows)
        feat_ref[1, :, lanes] = keyed
        feat_ref[2, :, lanes] = valued
        gext_ref[0:LANES, lanes] = halo_ref[0:LANES, lanes]
        gext_ref[LANES:, lanes] = (keyed * valued).astype(BF16)
        filt = filt_ref[j * count : (j + 1) * count, :]
        turned = ((grid_of(LANES, 0) + grid_of(LANES, 1)) % LANES == 0).astype(BF16)
        fill_table(table, jnp.dot(filt, turned, preferred_element_type=F32), True)
        wide = jnp.dot(
            table[...], windows(gext_ref, blocks, lanes), preferred_element_type=F32
        )
        mixed = pick_groups(wide, group, blocks)
        mixed_ref[:, lanes] = mixed
        query = feature(ext, taps_ref, lanes, 0, 0, rows)
        feat_ref[0, :, lanes] = query
        gate_ref[:, lanes] = (query * mixed).astype(BF16)

    each_tile(chans, tile, ext_ref, table_ref)
    project(which_ref[0], gate_ref, w_ref, sends)


def project(which, gate_ref, w_ref, out_refs):
    half = w_ref.shape[1] // 2
    part = half // len(out_refs)
    for i, out_ref in enumerate(out_refs):
        cols = pl.ds(pl.multiple_of(which * half + i * part, part), part)
        out_ref[...] = jnp.dot(
            gate_ref[...], w_ref[:, cols], preferred_element_type=F32
        ).astype(BF16)


def keep_kernel(which_ref, gate_ref, w_ref, *keep_refs):
    project(which_ref[0], gate_ref, w_ref, keep_refs)


def short_sums(grad, ext_ref, part):
    rows = grad.shape[0]
    return [
        jnp.sum(grad * ext_ref[part, 8 - lag : 8 - lag + rows, :], axis=0, keepdims=True)
        for lag in range(3)
    ]


def lags_kernel(
    group, filt_ref, x_ref, halo_ref, gg_ref, mixed_ref, feat_ref, gext_ref,
    gm_ref, gq_ref, lags_ref, tables_ref, left_ref, upside_ref, ext_ref,
):
    rows, chans = gg_ref.shape
    blocks = rows // SUB
    count = LANES // group

    def tile(j, lanes, left, upside, ext):
        filt = filt_ref[j * count : (j + 1) * count, :]
        fill_table(tables_ref.at[j], filt.astype(F32), False)
        grad_mixed = (gg_ref[:, lanes] * feat_ref[0, :, lanes]).astype(BF16)
        gm_ref[:, lanes] = grad_mixed
        grad_query = (gg_ref[:, lanes] * mixed_ref[:, lanes]).astype(BF16)
        gq_ref[:, lanes] = grad_query
        ext[0, 6:8, :] = halo_ref[LANES : LANES + 2, lanes].astype(F32)
        ext[0, 8:, :] = x_ref[0, :, lanes].astype(F32)
        sums = short_sums(grad_query.astype(F32), ext, 0)
        lane = group_of_lane(SUB, group)
        for g in range(count):
            for b in range(blocks):
                left[g * SUB : (g + 1) * SUB, b * LANES : (b + 1) * LANES] = jnp.where(
                    lane == g, grad_mixed[b * SUB : (b + 1) * SUB, :], jnp.zeros((), BF16)
                )
        ends = rows // LANES + 1
        flip = (grid_of(LANES, 0) + grid_of(LANES, 1) == LANES - 1).astype(BF16)
        turned = jnp.dot(
            flip,
            jnp.concatenate(
                [gext_ref[b * LANES : (b + 1) * LANES, lanes] for b in range(ends)], axis=1
            ),
            preferred_element_type=F32,
        ).astype(BF16)
        upside[0:LANES, :] = jnp.zeros((LANES, LANES), BF16)
        for b in range(ends):
            upside[LANES * (ends - b) : LANES * (ends - b + 1), :] = turned[
                :, b * LANES : (b + 1) * LANES
            ]
        rights = []
        for b in range(blocks):
            at = rows + LANES - b * SUB
            rights.append(
                jnp.concatenate([upside[at : at + LANES], upside[at - LANES : at]], axis=0)
            )
        products = lax.dot_general(
            left[...],
            jnp.concatenate(rights, axis=1),
            (((1,), (1,)), ((), ())),
            preferred_element_type=F32,
        )
        early = grid_of(SUB, 0) + grid_of(SUB, 1) < LANES - 1
        lag_rows = []
        for g in range(count):
            own = products[g * SUB : (g + 1) * SUB, :]
            ring = jnp.where(early, own[:, 0:LANES], own[:, LANES:])
            ring = pltpu.roll(ring, 0, 1, stride=1, stride_axis=0)
            lag_rows.append(jnp.sum(ring, axis=0, keepdims=True))
        lags = pltpu.roll(jnp.concatenate(lag_rows, axis=0), 1, 1)
        sums.append(jnp.zeros((16 - count - 3, LANES), F32))
        lags_ref[:, lanes] = jnp.concatenate([lags] + sums, axis=0)

    each_tile(chans, tile, left_ref, upside_ref, ext_ref)


def next_rows(ext_ref, taps_ref, x_ref, back_ref, lanes, parts):
    rows = x_ref.shape[1]
    span = LANES + RIM
    outs = []
    for part in parts:
        recent = x_ref[part, rows - RIM :, lanes].astype(F32)
        at = span + 2 * part
        ext_ref[part, 0:8, :] = recent[RIM - 8 :]
        ext_ref[part, 8:10, :] = back_ref[at : at + 2, lanes].astype(F32)
        outs.append(feature(ext_ref, taps_ref, lanes, part, 0, 2))
    high = back_ref[span + 6 : span + 8, lanes].astype(F32)
    low = back_ref[span + 8 : span + 10, lanes].astype(F32)
    return outs, high + low


def next_mixed(back_ref, lanes, grad, query):
    head = back_ref[0 : LANES + RIM, lanes].astype(F32)
    first = (grad * query).astype(BF16).astype(F32)
    return jnp.concatenate([first, head[2:]], axis=0)


def backward_kernel(
    group, x_ref, taps_ref, halo_ref, feat_ref, back_ref, gm_ref, lags_ref, tables_ref,
    gkv_ref, sums_ref, ext_ref, mext_ref, near_ref,
):
    _, rows, chans = x_ref.shape
    blocks = rows // SUB
    count = LANES // group

    def tile(j, lanes, ext, mext, near):
        for part in range(1, 3):
            at = LANES + 2 * part
            ext[part, 6:8, :] = halo_ref[at : at + 2, lanes].astype(F32)
            ext[part, 8:, :] = x_ref[part, :, lanes].astype(F32)
        (query_next,), gg_next = next_rows(near, taps_ref, x_ref, back_ref, lanes, (0,))
        head = next_mixed(back_ref, lanes, gg_next, query_next)
        mext[0:rows, :] = gm_ref[:, lanes]
        mext[rows:, :] = head[0:LANES].astype(BF16)
        wide = jnp.dot(
            tables_ref[j], windows(mext, blocks, slice(None)), preferred_element_type=F32
        )
        grad_gated = pick_groups(wide, group, blocks)
        sums = [None] * 3
        for part in range(1, 3):
            grad = (grad_gated * feat_ref[3 - part, :, lanes]).astype(BF16)
            gkv_ref[part - 1, :, lanes] = grad
            sums[part] = short_sums(grad.astype(F32), ext, part)
        early = lags_ref[:, lanes]
        flat = [early[0:count]]
        for lag in range(3):
            flat += [early[count + lag : count + lag + 1], sums[1][lag], sums[2][lag]]
        flat.append(jnp.zeros((32 - count - 9, LANES), F32))
        sums_ref[:, lanes] = jnp.concatenate(flat, axis=0).astype(sums_ref.dtype)

    each_tile(chans, tile, ext_ref, mext_ref, near_ref)


def inputs_kernel(
    group, x_ref, taps_ref, filt_ref, gext_ref, back_ref, gq_ref, gkv_ref, gin_ref, near_ref, gf_ref
):
    _, rows, chans = x_ref.shape
    count = LANES // group

    def tile(j, lanes, near, gf):
        (query, keyed, valued), grad = next_rows(
            near, taps_ref, x_ref, back_ref, lanes, (0, 1, 2)
        )
        head = next_mixed(back_ref, lanes, grad, query)
        filt = filt_ref[j * count : (j + 1) * count, :]
        taps = spread_taps(filt, group, False)
        taps_turned = spread_taps(filt, group, True)
        recent = gext_ref[rows:, lanes].astype(F32)
        recent = jnp.concatenate([recent, (keyed * valued).astype(BF16).astype(F32)], axis=0)
        gated, mixed = [], []
        for t in range(2):
            gated.append(jnp.sum(taps * head[t : t + LANES], axis=0, keepdims=True))
            mixed.append(
                jnp.sum(taps_turned * recent[t + 1 : t + 1 + LANES], axis=0, keepdims=True)
            )
        gated, mixed = jnp.concatenate(gated, axis=0), jnp.concatenate(mixed, axis=0)
        following = (grad * mixed, gated * valued, gated * keyed)
        for part in range(3):
            own = gq_ref[:, lanes] if part == 0 else gkv_ref[part - 1, :, lanes]
            gf[part, 0:rows, :] = own.astype(F32)
            gf[part, rows : rows + 2, :] = following[part].astype(BF16).astype(F32)
            total = taps_ref[0, part : part + 1, lanes] * gf[part, 0:rows, :]
            for lag in range(1, 3):
                tap = taps_ref[lag, part : part + 1, lanes]
                total = total + tap * gf[part, lag : lag + rows, :]
            gin_ref[part, :, lanes] = total.astype(BF16)

    each_tile(chans, tile, near_ref, gf_ref)


def unpack_kernel(group, short_scale, long_scale, *refs):
    short_ref, long_ref = refs[-2:]
    totals = [ref[...].astype(F32) for ref in refs[:-2]]
    while len(totals) > 1:
        totals = [sum(totals[i : i + 2]) for i in range(0, len(totals), 2)]
    total = totals[0]
    count = LANES // group
    for j in range(total.shape[1] // LANES):
        long_ref[j * count : (j + 1) * count, :] = (
            total[0:count, j * LANES : (j + 1) * LANES] * long_scale
        )
    for lag in range(3):
        for part in range(3):
            at = count + 3 * lag + part
            short_ref[lag, part : part + 1, :] = total[at : at + 1] * short_scale


def local(inputs, short_filter, long_filter, out_weight, out_cotangent):
    rows, _, chans = inputs.shape
    groups, span = long_filter.shape
    width = out_weight.shape[1]
    group = chans // groups
    count = LANES // group
    tiles = chans // LANES
    tokens_all = rows * lax.axis_size("ctx")
    n_tp = lax.axis_size("tp")
    signal = inputs.transpose(1, 0, 2)
    signal, short_filter, long_filter, out_weight, out_cotangent = [
        pltpu.with_memory_space_constraint(value, pltpu.HBM)
        for value in (signal, short_filter, long_filter, out_weight, out_cotangent)
    ]
    table = pltpu.VMEM((tiles, count * SUB, LANES + SUB), BF16)

    sent, signal, short_filter, long_filter = call(
        tail_kernel,
        "tail",
        (
            shape((LANES + RIM, chans), BF16),
            shape(signal.shape, BF16),
            shape(short_filter.shape, F32),
            shape(long_filter.shape, BF16),
        ),
        [pltpu.VMEM((tiles, 3, 8 + RIM + LANES, LANES), F32), pltpu.SemaphoreType.DMA((5,))],
        far=3,
    )(signal, short_filter, long_filter)
    halo = shifted(sent, "ctx", 1)
    grad_gate, sent_back, out_weight = call(
        grad_gate_kernel,
        "grad_gate",
        (
            shape((rows, chans), F32),
            shape((LANES + 2 * RIM, chans), BF16),
            shape(out_weight.shape, BF16),
        ),
        [
            pltpu.VMEM(out_cotangent.shape, BF16),
            pltpu.VMEM((tiles, 1, 8 + RIM + LANES, LANES), F32),
            pltpu.SemaphoreType.DMA,
            pltpu.SemaphoreType.DMA((max(1, chans // 256),)),
        ],
        far=2,
        operands=2,
    )(out_cotangent, out_weight, signal, short_filter)
    back = shifted(sent_back, "ctx", -1)
    core = lax.rem(lax.axis_index("tp"), 2)
    piece = shape((rows, width // 2 // PIECES), BF16)
    *other, gate_out, mixed, feat, gated = call(
        functools.partial(forward_kernel, group),
        "forward",
        (piece,) * PIECES
        + (
            shape((rows, chans), BF16),
            shape((rows, chans), F32),
            shape((3, rows, chans), F32),
            shape((LANES + rows, chans), BF16),
        ),
        [pltpu.VMEM((tiles, 3, 8 + rows, LANES), F32), table],
        scalars=1,
        operands=5,
    )(jnp.reshape(1 - core, (1,)), signal, short_filter, long_filter, halo, out_weight)
    theirs = [lax.ppermute(value, "tp", pairwise("tp", 1)) for value in other]
    kept = call(keep_kernel, "keep", (piece,) * PIECES, scalars=1, operands=2)(
        jnp.reshape(core, (1,)), gate_out, out_weight
    )
    mine = [
        (a.astype(F32) + b.astype(F32)).astype(BF16) for a, b in zip(kept, theirs, strict=True)
    ]
    step = 2
    got = [lax.ppermute(value, "tp", pairwise("tp", step)) for value in mine]

    ext = pltpu.VMEM((tiles, 3, rows + 8, LANES), F32)
    near = pltpu.VMEM((tiles, 3, 16, LANES), F32)
    grad_mixed, grad_query, lags, tables = call(
        functools.partial(lags_kernel, group),
        "lags",
        (
            shape((rows, chans), BF16),
            shape((rows, chans), BF16),
            shape((16, chans), F32),
            shape((chans // LANES, count * SUB, LANES + SUB), BF16),
        ),
        [
            pltpu.VMEM((tiles, count * SUB, rows // SUB * LANES), BF16),
            pltpu.VMEM((tiles, rows + 2 * LANES, LANES), BF16),
            ext,
        ],
        operands=7,
    )(long_filter, signal, halo, grad_gate, mixed, feat, gated)
    n_ctx = lax.axis_size("ctx")
    by_pairs = n_ctx & (n_ctx - 1) == 0
    grad_rest, sums = call(
        functools.partial(backward_kernel, group),
        "backward",
        (shape((2, rows, chans), BF16), shape((32, chans), BF16 if by_pairs else F32)),
        [ext, pltpu.VMEM((tiles, rows + LANES, LANES), BF16), near],
        operands=8,
    )(signal, short_filter, halo, feat, back, grad_mixed, lags, tables)
    grad_in = call(
        functools.partial(inputs_kernel, group),
        "inputs",
        shape((3, rows, chans), BF16),
        [near, pltpu.VMEM((tiles, 3, rows + 8, LANES), F32)],
        operands=7,
    )(signal, short_filter, long_filter, gated, back, grad_query, grad_rest)
    if by_pairs:
        hop = 1
        terms = [sums]
        while hop < n_ctx:
            if len(terms) > 1:
                pairs = [a.astype(F32) + b.astype(F32) for a, b in zip(terms[::2], terms[1::2])]
                terms = [sum(pairs).astype(BF16)]
            radix = min(4, n_ctx // hop)
            terms += [
                lax.ppermute(terms[0], "ctx", pairwise("ctx", i * hop)) for i in range(1, radix)
            ]
            hop *= radix
    else:
        terms = [lax.psum(sums, "ctx")]
    got, terms, grad_in = lax.optimization_barrier((got, terms, grad_in))
    mine = [
        (a.astype(F32) + b.astype(F32)).astype(BF16) for a, b in zip(mine, got, strict=True)
    ]
    step *= 2
    while step < n_tp:
        got = [lax.ppermute(value, "tp", pairwise("tp", step)) for value in mine]
        mine = [
            (a.astype(F32) + b.astype(F32)).astype(BF16) for a, b in zip(mine, got, strict=True)
        ]
        step *= 2
    sibling = [lax.ppermute(value, "tp", pairwise("tp", 1)) for value in mine]
    result = jnp.where(
        core == 0,
        jnp.concatenate(mine + sibling, axis=1),
        jnp.concatenate(sibling + mine, axis=1),
    )
    grad_short, grad_long = call(
        functools.partial(
            unpack_kernel, group, float(tokens_all) ** (-0.5), float(tokens_all * group) ** (-0.5)
        ),
        "unpack",
        (shape((3, 3, chans), F32), shape((groups, span), F32)),
        operands=len(terms),
    )(*terms)
    return (result, grad_in.transpose(1, 0, 2), grad_short, grad_long)


def solution(mesh):
    in_specs = (
        P("ctx", None, "tp"),
        P(None, None, "tp"),
        P("tp", None),
        P("tp", None),
        P("ctx", None),
    )
    out_specs = (P("ctx", None), P("ctx", None, "tp"), P(None, None, "tp"), P("tp", None))
    return jax.shard_map(local, mesh=mesh, in_specs=in_specs, out_specs=out_specs, check_vma=False)
```

```python
import functools

import jax
import jax.numpy as jnp
from jax import lax
from jax.experimental import pallas as pl
from jax.experimental.pallas import tpu as pltpu
from jax.sharding import PartitionSpec as P

LANES = 128
RIM = 16
EDGE = 8
SUB = 32
COST = 1024
PIECES = 2
F32 = jnp.float32
BF16 = jnp.bfloat16
VMEM_LIMIT = 12 * 1024 * 1024


def pairwise(axis, step):
    return [(source, source ^ step) for source in range(lax.axis_size(axis))]


def shifted(value, axis, steps):
    count = lax.axis_size(axis)
    initial, last = (max(0, -steps), min(count, count - steps))
    return lax.ppermute(value, axis, [(source, source + steps) for source in range(initial, last)])


def call(body, name, outs, scratch=(), scalars=0, far=0, operands=0, cost=COST):
    specs = [pl.BlockSpec(memory_space=pltpu.SMEM)] * scalars
    specs += [pl.BlockSpec(memory_space=pltpu.HBM)] * far
    specs += [pl.BlockSpec(memory_space=pltpu.VMEM)] * operands
    return pl.pallas_call(
        body,
        out_shape=outs,
        in_specs=specs,
        out_specs=jax.tree.map(lambda _: pl.BlockSpec(memory_space=pltpu.VMEM), outs),
        scratch_shapes=scratch,
        compiler_params=pltpu.CompilerParams(vmem_limit_bytes=VMEM_LIMIT),
        cost_estimate=pl.CostEstimate(flops=0, transcendentals=0, bytes_accessed=cost),
        name=name,
    )


def shape(dims, dtype):
    return jax.ShapeDtypeStruct(dims, dtype)


def each_tile(chans, body, *scratch):
    for j in range(chans // LANES):
        body(j, slice(j * LANES, (j + 1) * LANES), *[ref.at[j] for ref in scratch])


def feature(ext_ref, taps_ref, lanes, part, start, rows):
    total = taps_ref[0, part : part + 1, lanes] * ext_ref[part, 8 + start : 8 + start + rows, :]
    for lag in range(1, 3):
        first = 8 + start - lag
        tap = taps_ref[lag, part : part + 1, lanes]
        total = total + tap * ext_ref[part, first : first + rows, :]
    return total


def group_of_lane(rows, group):
    return lax.broadcasted_iota(jnp.int32, (rows, LANES), 1) // group


def grid_of(rows, axis):
    return lax.broadcasted_iota(jnp.int32, (rows, LANES), axis)


def fill_table(table_ref, taps, forward):
    row, col = grid_of(SUB, 0), grid_of(SUB, 1)
    early = (col > row) if forward else (col >= row)
    for g in range(taps.shape[0]):
        wide = jnp.broadcast_to(taps[g : g + 1, :], (SUB, LANES))
        ring = pltpu.roll(wide, 0, 1, stride=1, stride_axis=0)
        rows = slice(g * SUB, (g + 1) * SUB)
        table_ref[rows, 0:LANES] = jnp.where(early, ring, 0.0).astype(BF16)
        table_ref[rows, LANES:] = jnp.where(early, 0.0, ring)[:, 0:SUB].astype(BF16)


def pick_groups(wide, group, blocks):
    lane = group_of_lane(SUB, group)
    outs = []
    for b in range(blocks):
        cols = slice(b * LANES, (b + 1) * LANES)
        total = wide[0:SUB, cols]
        for g in range(1, LANES // group):
            total = jnp.where(lane == g, wide[g * SUB : (g + 1) * SUB, cols], total)
        outs.append(total)
    return jnp.concatenate(outs, axis=0)


def windows(ref, blocks, lanes):
    return jnp.concatenate(
        [ref[b * SUB : (b + 1) * SUB + LANES, lanes] for b in range(blocks)], axis=1
    )


def spread_taps(filt, group, reverse):
    count = filt.shape[0]
    owner = (
        group_of_lane(count, group) == lax.broadcasted_iota(jnp.int32, (count, LANES), 0)
    ).astype(BF16)
    if reverse:
        flip = (grid_of(LANES, 0) + grid_of(LANES, 1) == LANES - 1).astype(BF16)
        filt = jnp.dot(filt, flip, preferred_element_type=F32).astype(BF16)
    return lax.dot_general(filt, owner, (((0,), (0,)), ((), ())), preferred_element_type=F32)


def tail_kernel(
    x_hbm, taps_hbm, filt_hbm, sent_ref, x_ref, taps_ref, filt_ref, ext_ref, sems
):
    _, rows, chans = x_ref.shape
    first = rows - LANES - RIM
    regions = (
        (pl.ds(1, 2), pl.ds(first, LANES + RIM)),
        (pl.ds(0, 1), pl.ds(rows - RIM, RIM)),
        (pl.ds(0, 1), pl.ds(0, rows - RIM)),
        (pl.ds(1, 2), pl.ds(0, first)),
    )
    copies = [pltpu.make_async_copy(taps_hbm, taps_ref, sems.at[0])]
    for i, region in enumerate(regions):
        copies.append(
            pltpu.make_async_copy(x_hbm.at[region], x_ref.at[region], sems.at[1 + i])
        )
    copies.append(pltpu.make_async_copy(filt_hbm, filt_ref, sems.at[5]))
    for copy in copies:
        copy.start()
    for copy in copies[:3]:
        copy.wait()

    def tile(j, lanes, ext):
        for part in range(1, 3):
            ext[part, 8:, :] = x_ref[part, first:, lanes].astype(F32)
        keyed = feature(ext, taps_ref, lanes, 1, RIM, LANES)
        valued = feature(ext, taps_ref, lanes, 2, RIM, LANES)
        sent_ref[0:LANES, lanes] = (keyed * valued).astype(BF16)
        rim = [x_ref[part, rows - RIM :, lanes].astype(F32)[RIM - 2 :] for part in range(3)]
        rim.append(jnp.zeros((EDGE - 6, LANES), F32))
        sent_ref[LANES:, lanes] = jnp.concatenate(rim, axis=0).astype(BF16)

    each_tile(chans, tile, ext_ref)
    for copy in copies[3:]:
        copy.wait()


def grad_gate_kernel(
    c_hbm, w_hbm, x_ref, taps_ref, gg_ref, back_ref, w_ref, c_ref, ext_ref, c_sem, w_sems
):
    chans = w_ref.shape[0]
    chunks = w_sems.shape[0]
    wide = chans // chunks
    span = LANES + RIM

    def chunk(j):
        rows = pl.ds(pl.multiple_of(j * wide, wide), wide)
        return pltpu.make_async_copy(w_hbm.at[rows], w_ref.at[rows], w_sems.at[j])

    load = pltpu.make_async_copy(c_hbm, c_ref, c_sem)
    load.start()
    for j in range(min(2, chunks)):
        chunk(j).start()
    load.wait()

    def product(j, carry):
        chunk(j).wait()

        @pl.when(j + 2 < chunks)
        def _():
            chunk(j + 2).start()

        cols = pl.ds(pl.multiple_of(j * wide, wide), wide)
        gg_ref[:, cols] = lax.dot_general(
            c_ref[...], w_ref[cols, :], (((1,), (1,)), ((), ())), preferred_element_type=F32
        )
        for i in range(wide // LANES):
            at = pl.multiple_of(j * wide + i * LANES, LANES)
            tile(pl.ds(at, LANES), ext_ref.at[i])
        return carry

    def tile(lanes, ext):
        ext[0, 0:8, :] = jnp.zeros((8, LANES), F32)
        ext[0, 8:, :] = x_ref[0, 0:span, lanes].astype(F32)
        query = feature(ext, taps_ref, lanes, 0, 0, span)
        grad_mixed = (gg_ref[0:span, lanes] * query).astype(BF16).astype(F32)
        back_ref[0:LANES, lanes] = grad_mixed[0:LANES].astype(BF16)
        grad = gg_ref[0:2, lanes]
        high = grad.astype(BF16).astype(F32)
        rim = [x_ref[part, 0:RIM, lanes].astype(F32)[0:2] for part in range(3)]
        rim += [high, grad - high, jnp.zeros((RIM - 11, LANES), F32)]
        rim.insert(0, grad_mixed[LANES : LANES + 1])
        back_ref[LANES:, lanes] = jnp.concatenate(rim, axis=0).astype(BF16)

    lax.fori_loop(0, chunks, product, 0)


def forward_kernel(
    group, which_ref, x_ref, taps_ref, filt_ref, halo_ref, w_ref,
    *refs,
):
    sends, (gate_ref, mixed_ref, feat_ref, gext_ref, ext_ref, table_ref) = refs[:PIECES], refs[PIECES:]
    _, rows, chans = x_ref.shape
    blocks = rows // SUB
    count = LANES // group

    def tile(j, lanes, ext, table):
        for part in range(3):
            at = LANES + 2 * part
            ext[part, 6:8, :] = halo_ref[at : at + 2, lanes].astype(F32)
            ext[part, 8:, :] = x_ref[part, :, lanes].astype(F32)
        keyed = feature(ext, taps_ref, lanes, 1, 0, rows)
        valued = feature(ext, taps_ref, lanes, 2, 0, rows)
        feat_ref[1, :, lanes] = keyed
        feat_ref[2, :, lanes] = valued
        gext_ref[0:LANES, lanes] = halo_ref[0:LANES, lanes]
        gext_ref[LANES:, lanes] = (keyed * valued).astype(BF16)
        filt = filt_ref[j * count : (j + 1) * count, :]
        turned = ((grid_of(LANES, 0) + grid_of(LANES, 1)) % LANES == 0).astype(BF16)
        fill_table(table, jnp.dot(filt, turned, preferred_element_type=F32), True)
        wide = jnp.dot(
            table[...], windows(gext_ref, blocks, lanes), preferred_element_type=F32
        )
        mixed = pick_groups(wide, group, blocks)
        mixed_ref[:, lanes] = mixed
        query = feature(ext, taps_ref, lanes, 0, 0, rows)
        feat_ref[0, :, lanes] = query
        gate_ref[:, lanes] = (query * mixed).astype(BF16)

    each_tile(chans, tile, ext_ref, table_ref)
    project(which_ref[0], gate_ref, w_ref, sends)


def project(which, gate_ref, w_ref, out_refs):
    half = w_ref.shape[1] // 2
    part = half // len(out_refs)
    for i, out_ref in enumerate(out_refs):
        cols = pl.ds(pl.multiple_of(which * half + i * part, part), part)
        out_ref[...] = jnp.dot(
            gate_ref[...], w_ref[:, cols], preferred_element_type=F32
        ).astype(BF16)


def keep_kernel(which_ref, gate_ref, w_ref, *keep_refs):
    project(which_ref[0], gate_ref, w_ref, keep_refs)


def short_sums(grad, ext_ref, part):
    rows = grad.shape[0]
    return [
        jnp.sum(grad * ext_ref[part, 8 - lag : 8 - lag + rows, :], axis=0, keepdims=True)
        for lag in range(3)
    ]


def lags_kernel(
    group, filt_ref, x_ref, halo_ref, gg_ref, mixed_ref, feat_ref, gext_ref,
    gm_ref, gq_ref, lags_ref, tables_ref, left_ref, upside_ref, ext_ref,
):
    rows, chans = gg_ref.shape
    blocks = rows // SUB
    count = LANES // group

    def tile(j, lanes, left, upside, ext):
        filt = filt_ref[j * count : (j + 1) * count, :]
        fill_table(tables_ref.at[j], filt.astype(F32), False)
        grad_mixed = (gg_ref[:, lanes] * feat_ref[0, :, lanes]).astype(BF16)
        gm_ref[:, lanes] = grad_mixed
        grad_query = (gg_ref[:, lanes] * mixed_ref[:, lanes]).astype(BF16)
        gq_ref[:, lanes] = grad_query
        ext[0, 6:8, :] = halo_ref[LANES : LANES + 2, lanes].astype(F32)
        ext[0, 8:, :] = x_ref[0, :, lanes].astype(F32)
        sums = short_sums(grad_query.astype(F32), ext, 0)
        lane = group_of_lane(SUB, group)
        for g in range(count):
            for b in range(blocks):
                left[g * SUB : (g + 1) * SUB, b * LANES : (b + 1) * LANES] = jnp.where(
                    lane == g, grad_mixed[b * SUB : (b + 1) * SUB, :], jnp.zeros((), BF16)
                )
        ends = rows // LANES + 1
        flip = (grid_of(LANES, 0) + grid_of(LANES, 1) == LANES - 1).astype(BF16)
        turned = jnp.dot(
            flip,
            jnp.concatenate(
                [gext_ref[b * LANES : (b + 1) * LANES, lanes] for b in range(ends)], axis=1
            ),
            preferred_element_type=F32,
        ).astype(BF16)
        upside[0:LANES, :] = jnp.zeros((LANES, LANES), BF16)
        for b in range(ends):
            upside[LANES * (ends - b) : LANES * (ends - b + 1), :] = turned[
                :, b * LANES : (b + 1) * LANES
            ]
        rights = []
        for b in range(blocks):
            at = rows + LANES - b * SUB
            rights.append(
                jnp.concatenate([upside[at : at + LANES], upside[at - LANES : at]], axis=0)
            )
        products = lax.dot_general(
            left[...],
            jnp.concatenate(rights, axis=1),
            (((1,), (1,)), ((), ())),
            preferred_element_type=F32,
        )
        early = grid_of(SUB, 0) + grid_of(SUB, 1) < LANES - 1
        lag_rows = []
        for g in range(count):
            own = products[g * SUB : (g + 1) * SUB, :]
            ring = jnp.where(early, own[:, 0:LANES], own[:, LANES:])
            ring = pltpu.roll(ring, 0, 1, stride=1, stride_axis=0)
            lag_rows.append(jnp.sum(ring, axis=0, keepdims=True))
        lags = pltpu.roll(jnp.concatenate(lag_rows, axis=0), 1, 1)
        sums.append(jnp.zeros((16 - count - 3, LANES), F32))
        lags_ref[:, lanes] = jnp.concatenate([lags] + sums, axis=0)

    each_tile(chans, tile, left_ref, upside_ref, ext_ref)


def next_rows(ext_ref, taps_ref, x_ref, back_ref, lanes, parts):
    rows = x_ref.shape[1]
    rim = back_ref[LANES:, lanes].astype(F32)
    outs = []
    for part in parts:
        recent = x_ref[part, rows - RIM :, lanes].astype(F32)
        ext_ref[part, 0:8, :] = recent[RIM - 8 :]
        ext_ref[part, 8:10, :] = rim[1 + 2 * part : 3 + 2 * part]
        outs.append(feature(ext_ref, taps_ref, lanes, part, 0, 2))
    return outs, rim[7:9] + rim[9:11]


def next_mixed(back_ref, lanes, grad, query):
    head = back_ref[0 : LANES + RIM, lanes].astype(F32)
    first = (grad * query).astype(BF16).astype(F32)
    return jnp.concatenate([first, head[2:]], axis=0)


def backward_kernel(
    group, x_ref, taps_ref, halo_ref, feat_ref, back_ref, gm_ref, lags_ref, tables_ref,
    gkv_ref, sums_ref, ext_ref, mext_ref, near_ref,
):
    _, rows, chans = x_ref.shape
    blocks = rows // SUB
    count = LANES // group

    def tile(j, lanes, ext, mext, near):
        for part in range(1, 3):
            at = LANES + 2 * part
            ext[part, 6:8, :] = halo_ref[at : at + 2, lanes].astype(F32)
            ext[part, 8:, :] = x_ref[part, :, lanes].astype(F32)
        (query_next,), gg_next = next_rows(near, taps_ref, x_ref, back_ref, lanes, (0,))
        head = next_mixed(back_ref, lanes, gg_next, query_next)
        mext[0:rows, :] = gm_ref[:, lanes]
        mext[rows:, :] = head[0:LANES].astype(BF16)
        wide = jnp.dot(
            tables_ref[j], windows(mext, blocks, slice(None)), preferred_element_type=F32
        )
        grad_gated = pick_groups(wide, group, blocks)
        sums = [None] * 3
        for part in range(1, 3):
            grad = (grad_gated * feat_ref[3 - part, :, lanes]).astype(BF16)
            gkv_ref[part - 1, :, lanes] = grad
            sums[part] = short_sums(grad.astype(F32), ext, part)
        early = lags_ref[:, lanes]
        flat = [early[0:count]]
        for lag in range(3):
            flat += [early[count + lag : count + lag + 1], sums[1][lag], sums[2][lag]]
        flat.append(jnp.zeros((32 - count - 9, LANES), F32))
        sums_ref[:, lanes] = jnp.concatenate(flat, axis=0).astype(sums_ref.dtype)

    each_tile(chans, tile, ext_ref, mext_ref, near_ref)


def inputs_kernel(
    group, x_ref, taps_ref, filt_ref, gext_ref, back_ref, gq_ref, gkv_ref, gin_ref, near_ref, gf_ref
):
    _, rows, chans = x_ref.shape
    count = LANES // group

    def tile(j, lanes, near, gf):
        (query, keyed, valued), grad = next_rows(
            near, taps_ref, x_ref, back_ref, lanes, (0, 1, 2)
        )
        head = next_mixed(back_ref, lanes, grad, query)
        filt = filt_ref[j * count : (j + 1) * count, :]
        taps = spread_taps(filt, group, False)
        taps_turned = spread_taps(filt, group, True)
        recent = gext_ref[rows:, lanes].astype(F32)
        recent = jnp.concatenate([recent, (keyed * valued).astype(BF16).astype(F32)], axis=0)
        gated, mixed = [], []
        for t in range(2):
            gated.append(jnp.sum(taps * head[t : t + LANES], axis=0, keepdims=True))
            mixed.append(
                jnp.sum(taps_turned * recent[t + 1 : t + 1 + LANES], axis=0, keepdims=True)
            )
        gated, mixed = jnp.concatenate(gated, axis=0), jnp.concatenate(mixed, axis=0)
        following = (grad * mixed, gated * valued, gated * keyed)
        for part in range(3):
            own = gq_ref[:, lanes] if part == 0 else gkv_ref[part - 1, :, lanes]
            gf[part, 0:rows, :] = own.astype(F32)
            gf[part, rows : rows + 2, :] = following[part].astype(BF16).astype(F32)
            total = taps_ref[0, part : part + 1, lanes] * gf[part, 0:rows, :]
            for lag in range(1, 3):
                tap = taps_ref[lag, part : part + 1, lanes]
                total = total + tap * gf[part, lag : lag + rows, :]
            gin_ref[part, :, lanes] = total.astype(BF16)

    each_tile(chans, tile, near_ref, gf_ref)


def unpack_kernel(group, short_scale, long_scale, *refs):
    short_ref, long_ref = refs[-2:]
    totals = [ref[...].astype(F32) for ref in refs[:-2]]
    while len(totals) > 1:
        totals = [sum(totals[i : i + 2]) for i in range(0, len(totals), 2)]
    total = totals[0]
    count = LANES // group
    for j in range(total.shape[1] // LANES):
        long_ref[j * count : (j + 1) * count, :] = (
            total[0:count, j * LANES : (j + 1) * LANES] * long_scale
        )
    for lag in range(3):
        for part in range(3):
            at = count + 3 * lag + part
            short_ref[lag, part : part + 1, :] = total[at : at + 1] * short_scale


def place_kernel(first, which_ref, own_ref, sibling_ref, *refs):
    out_ref, sems = refs[-2:]
    half = out_ref.shape[1] // 2
    copies = []
    for i, ref in enumerate((own_ref, sibling_ref)):
        side = which_ref[0] if i == 0 else 1 - which_ref[0]
        cols = pl.ds(pl.multiple_of(side * half + first, LANES), ref.shape[1])
        copies.append(pltpu.make_async_copy(ref, out_ref.at[:, cols], sems.at[i]))
    for copy in copies:
        copy.start()
    for copy in copies:
        copy.wait()


def place(result, which, own, sibling, first, width):
    far = pl.BlockSpec(memory_space=pltpu.HBM)
    near = pl.BlockSpec(memory_space=pltpu.VMEM)
    operands = (which, own, sibling) + (() if result is None else (result,))
    return pl.pallas_call(
        functools.partial(place_kernel, first),
        out_shape=shape((own.shape[0], width), BF16),
        in_specs=[pl.BlockSpec(memory_space=pltpu.SMEM), near, near, far][: len(operands)],
        out_specs=far,
        scratch_shapes=[pltpu.SemaphoreType.DMA((2,))],
        compiler_params=pltpu.CompilerParams(vmem_limit_bytes=VMEM_LIMIT),
        input_output_aliases={} if result is None else {3: 0},
        name="place",
    )(*operands)


def local(inputs, short_filter, long_filter, out_weight, out_cotangent):
    rows, _, chans = inputs.shape
    groups, span = long_filter.shape
    width = out_weight.shape[1]
    group = chans // groups
    count = LANES // group
    tiles = chans // LANES
    tokens_all = rows * lax.axis_size("ctx")
    n_tp = lax.axis_size("tp")
    signal = inputs.transpose(1, 0, 2)
    signal, short_filter, long_filter, out_weight, out_cotangent = [
        pltpu.with_memory_space_constraint(value, pltpu.HBM)
        for value in (signal, short_filter, long_filter, out_weight, out_cotangent)
    ]
    table = pltpu.VMEM((tiles, count * SUB, LANES + SUB), BF16)

    sent, signal, short_filter, long_filter = call(
        tail_kernel,
        "tail",
        (
            shape((LANES + EDGE, chans), BF16),
            shape(signal.shape, BF16),
            shape(short_filter.shape, F32),
            shape(long_filter.shape, BF16),
        ),
        [pltpu.VMEM((tiles, 3, 8 + RIM + LANES, LANES), F32), pltpu.SemaphoreType.DMA((6,))],
        far=3,
    )(signal, short_filter, long_filter)
    halo = shifted(sent, "ctx", 1)
    grad_gate, sent_back, out_weight = call(
        grad_gate_kernel,
        "grad_gate",
        (
            shape((rows, chans), F32),
            shape((LANES + RIM, chans), BF16),
            shape(out_weight.shape, BF16),
        ),
        [
            pltpu.VMEM(out_cotangent.shape, BF16),
            pltpu.VMEM((tiles, 1, 8 + RIM + LANES, LANES), F32),
            pltpu.SemaphoreType.DMA,
            pltpu.SemaphoreType.DMA((max(1, chans // 256),)),
        ],
        far=2,
        operands=2,
    )(out_cotangent, out_weight, signal, short_filter)
    back = shifted(sent_back, "ctx", -1)
    core = lax.rem(lax.axis_index("tp"), 2)
    piece = shape((rows, width // 2 // PIECES), BF16)
    *other, gate_out, mixed, feat, gated = call(
        functools.partial(forward_kernel, group),
        "forward",
        (piece,) * PIECES
        + (
            shape((rows, chans), BF16),
            shape((rows, chans), F32),
            shape((3, rows, chans), F32),
            shape((LANES + rows, chans), BF16),
        ),
        [pltpu.VMEM((tiles, 3, 8 + rows, LANES), F32), table],
        scalars=1,
        operands=5,
    )(jnp.reshape(1 - core, (1,)), signal, short_filter, long_filter, halo, out_weight)
    theirs = [lax.ppermute(value, "tp", pairwise("tp", 1)) for value in other]
    kept = call(keep_kernel, "keep", (piece,) * PIECES, scalars=1, operands=2)(
        jnp.reshape(core, (1,)), gate_out, out_weight
    )
    mine = [
        (a.astype(F32) + b.astype(F32)).astype(BF16) for a, b in zip(kept, theirs, strict=True)
    ]
    step = 2
    got = [lax.ppermute(value, "tp", pairwise("tp", step)) for value in mine]

    ext = pltpu.VMEM((tiles, 3, rows + 8, LANES), F32)
    near = pltpu.VMEM((tiles, 3, 16, LANES), F32)
    grad_mixed, grad_query, lags, tables = call(
        functools.partial(lags_kernel, group),
        "lags",
        (
            shape((rows, chans), BF16),
            shape((rows, chans), BF16),
            shape((16, chans), F32),
            shape((chans // LANES, count * SUB, LANES + SUB), BF16),
        ),
        [
            pltpu.VMEM((tiles, count * SUB, rows // SUB * LANES), BF16),
            pltpu.VMEM((tiles, rows + 2 * LANES, LANES), BF16),
            ext,
        ],
        operands=7,
    )(long_filter, signal, halo, grad_gate, mixed, feat, gated)
    n_ctx = lax.axis_size("ctx")
    by_pairs = n_ctx & (n_ctx - 1) == 0
    grad_rest, sums = call(
        functools.partial(backward_kernel, group),
        "backward",
        (shape((2, rows, chans), BF16), shape((32, chans), BF16 if by_pairs else F32)),
        [ext, pltpu.VMEM((tiles, rows + LANES, LANES), BF16), near],
        operands=8,
    )(signal, short_filter, halo, feat, back, grad_mixed, lags, tables)
    grad_in = call(
        functools.partial(inputs_kernel, group),
        "inputs",
        shape((3, rows, chans), BF16),
        [near, pltpu.VMEM((tiles, 3, rows + 8, LANES), F32)],
        operands=7,
    )(signal, short_filter, long_filter, gated, back, grad_query, grad_rest)
    if by_pairs:
        hop = 1
        terms = [sums]
        while hop < n_ctx:
            if len(terms) > 1:
                pairs = [a.astype(F32) + b.astype(F32) for a, b in zip(terms[::2], terms[1::2])]
                terms = [sum(pairs).astype(BF16)]
            radix = min(4, n_ctx // hop)
            terms += [
                lax.ppermute(terms[0], "ctx", pairwise("ctx", i * hop)) for i in range(1, radix)
            ]
            if hop == 1:
                terms, grad_in = lax.optimization_barrier((terms, grad_in))
            hop *= radix
    else:
        terms = [lax.psum(sums, "ctx")]
    got, terms = lax.optimization_barrier((got, terms))
    mine = [
        (a.astype(F32) + b.astype(F32)).astype(BF16) for a, b in zip(mine, got, strict=True)
    ]
    step *= 2
    while step < n_tp:
        got = [lax.ppermute(value, "tp", pairwise("tp", step)) for value in mine]
        mine = [
            (a.astype(F32) + b.astype(F32)).astype(BF16) for a, b in zip(mine, got, strict=True)
        ]
        step *= 2
    sibling = [lax.ppermute(value, "tp", pairwise("tp", 1)) for value in mine]
    result = None
    for i in reversed(range(PIECES)):
        result = place(
            result, jnp.reshape(core, (1,)), mine[i], sibling[i], i * (width // 2 // PIECES), width
        )
    grad_short, grad_long = call(
        functools.partial(
            unpack_kernel, group, float(tokens_all) ** (-0.5), float(tokens_all * group) ** (-0.5)
        ),
        "unpack",
        (shape((3, 3, chans), F32), shape((groups, span), F32)),
        operands=len(terms),
    )(*terms)
    return (result, grad_in.transpose(1, 0, 2), grad_short, grad_long)


def solution(mesh):
    in_specs = (
        P("ctx", None, "tp"),
        P(None, None, "tp"),
        P("tp", None),
        P("tp", None),
        P("ctx", None),
    )
    out_specs = (P("ctx", None), P("ctx", None, "tp"), P(None, None, "tp"), P("tp", None))
    return jax.shard_map(local, mesh=mesh, in_specs=in_specs, out_specs=out_specs, check_vma=False)
```

```python
import functools

import jax
import jax.numpy as jnp
from jax import lax
from jax.experimental import pallas as pl
from jax.experimental.pallas import tpu as pltpu
from jax.sharding import PartitionSpec as P

LANES = 128
RIM = 16
EDGE = 8
SUB = 32
COST = 1024
PIECES = 2
F32 = jnp.float32
BF16 = jnp.bfloat16
VMEM_LIMIT = 12 * 1024 * 1024


def pairwise(axis, step):
    return [(source, source ^ step) for source in range(lax.axis_size(axis))]


def shifted(value, axis, steps):
    count = lax.axis_size(axis)
    initial, last = (max(0, -steps), min(count, count - steps))
    return lax.ppermute(value, axis, [(source, source + steps) for source in range(initial, last)])


def call(body, name, outs, scratch=(), scalars=0, far=0, operands=0, cost=COST):
    specs = [pl.BlockSpec(memory_space=pltpu.SMEM)] * scalars
    specs += [pl.BlockSpec(memory_space=pltpu.HBM)] * far
    specs += [pl.BlockSpec(memory_space=pltpu.VMEM)] * operands
    return pl.pallas_call(
        body,
        out_shape=outs,
        in_specs=specs,
        out_specs=jax.tree.map(lambda _: pl.BlockSpec(memory_space=pltpu.VMEM), outs),
        scratch_shapes=scratch,
        compiler_params=pltpu.CompilerParams(vmem_limit_bytes=VMEM_LIMIT),
        cost_estimate=pl.CostEstimate(flops=0, transcendentals=0, bytes_accessed=cost),
        name=name,
    )


def shape(dims, dtype):
    return jax.ShapeDtypeStruct(dims, dtype)


def each_tile(chans, body, *scratch):
    for j in range(chans // LANES):
        body(j, slice(j * LANES, (j + 1) * LANES), *[ref.at[j] for ref in scratch])


def feature(ext_ref, taps_ref, lanes, part, start, rows):
    total = taps_ref[0, part : part + 1, lanes] * ext_ref[part, 8 + start : 8 + start + rows, :]
    for lag in range(1, 3):
        first = 8 + start - lag
        tap = taps_ref[lag, part : part + 1, lanes]
        total = total + tap * ext_ref[part, first : first + rows, :]
    return total


def group_of_lane(rows, group):
    return lax.broadcasted_iota(jnp.int32, (rows, LANES), 1) // group


def grid_of(rows, axis):
    return lax.broadcasted_iota(jnp.int32, (rows, LANES), axis)


def fill_table(table_ref, taps, forward):
    row, col = grid_of(SUB, 0), grid_of(SUB, 1)
    early = (col > row) if forward else (col >= row)
    for g in range(taps.shape[0]):
        wide = jnp.broadcast_to(taps[g : g + 1, :], (SUB, LANES))
        ring = pltpu.roll(wide, 0, 1, stride=1, stride_axis=0)
        rows = slice(g * SUB, (g + 1) * SUB)
        table_ref[rows, 0:LANES] = jnp.where(early, ring, 0.0).astype(BF16)
        table_ref[rows, LANES:] = jnp.where(early, 0.0, ring)[:, 0:SUB].astype(BF16)


def pick_groups(wide, group, blocks):
    lane = group_of_lane(SUB, group)
    outs = []
    for b in range(blocks):
        cols = slice(b * LANES, (b + 1) * LANES)
        total = wide[0:SUB, cols]
        for g in range(1, LANES // group):
            total = jnp.where(lane == g, wide[g * SUB : (g + 1) * SUB, cols], total)
        outs.append(total)
    return jnp.concatenate(outs, axis=0)


def windows(ref, blocks, lanes):
    return jnp.concatenate(
        [ref[b * SUB : (b + 1) * SUB + LANES, lanes] for b in range(blocks)], axis=1
    )


def spread_taps(filt, group, reverse):
    count = filt.shape[0]
    owner = (
        group_of_lane(count, group) == lax.broadcasted_iota(jnp.int32, (count, LANES), 0)
    ).astype(BF16)
    if reverse:
        flip = (grid_of(LANES, 0) + grid_of(LANES, 1) == LANES - 1).astype(BF16)
        filt = jnp.dot(filt, flip, preferred_element_type=F32).astype(BF16)
    return lax.dot_general(filt, owner, (((0,), (0,)), ((), ())), preferred_element_type=F32)


def tail_kernel(
    x_hbm, taps_hbm, filt_hbm, sent_ref, x_ref, taps_ref, filt_ref, ext_ref, sems
):
    _, rows, chans = x_ref.shape
    first = rows - LANES - RIM
    regions = (
        (pl.ds(1, 2), pl.ds(first, LANES + RIM)),
        (pl.ds(0, 1), pl.ds(rows - RIM, RIM)),
        (pl.ds(0, 1), pl.ds(0, rows - RIM)),
        (pl.ds(1, 2), pl.ds(0, first)),
    )
    copies = [pltpu.make_async_copy(taps_hbm, taps_ref, sems.at[0])]
    for i, region in enumerate(regions):
        copies.append(
            pltpu.make_async_copy(x_hbm.at[region], x_ref.at[region], sems.at[1 + i])
        )
    copies.append(pltpu.make_async_copy(filt_hbm, filt_ref, sems.at[5]))
    for copy in copies:
        copy.start()
    for copy in copies[:3]:
        copy.wait()

    def tile(j, lanes, ext):
        for part in range(1, 3):
            ext[part, 8:, :] = x_ref[part, first:, lanes].astype(F32)
        keyed = feature(ext, taps_ref, lanes, 1, RIM, LANES)
        valued = feature(ext, taps_ref, lanes, 2, RIM, LANES)
        sent_ref[0:LANES, lanes] = (keyed * valued).astype(BF16)
        rim = [x_ref[part, rows - RIM :, lanes].astype(F32)[RIM - 2 :] for part in range(3)]
        rim.append(jnp.zeros((EDGE - 6, LANES), F32))
        sent_ref[LANES:, lanes] = jnp.concatenate(rim, axis=0).astype(BF16)

    each_tile(chans, tile, ext_ref)
    for copy in copies[3:]:
        copy.wait()


def grad_gate_kernel(
    c_hbm, w_hbm, x_ref, taps_ref, gg_ref, back_ref, w_ref, c_ref, ext_ref, c_sem, w_sems
):
    chans = w_ref.shape[0]
    chunks = w_sems.shape[0]
    wide = chans // chunks
    span = LANES + RIM

    def chunk(j):
        rows = pl.ds(pl.multiple_of(j * wide, wide), wide)
        return pltpu.make_async_copy(w_hbm.at[rows], w_ref.at[rows], w_sems.at[j])

    load = pltpu.make_async_copy(c_hbm, c_ref, c_sem)
    load.start()
    for j in range(min(2, chunks)):
        chunk(j).start()
    load.wait()

    def product(j, carry):
        chunk(j).wait()

        @pl.when(j + 2 < chunks)
        def _():
            chunk(j + 2).start()

        cols = pl.ds(pl.multiple_of(j * wide, wide), wide)
        gg_ref[:, cols] = lax.dot_general(
            c_ref[...], w_ref[cols, :], (((1,), (1,)), ((), ())), preferred_element_type=F32
        )
        for i in range(wide // LANES):
            at = pl.multiple_of(j * wide + i * LANES, LANES)
            tile(pl.ds(at, LANES), ext_ref.at[i])
        return carry

    def tile(lanes, ext):
        ext[0, 0:8, :] = jnp.zeros((8, LANES), F32)
        ext[0, 8:, :] = x_ref[0, 0:span, lanes].astype(F32)
        query = feature(ext, taps_ref, lanes, 0, 0, span)
        grad_mixed = (gg_ref[0:span, lanes] * query).astype(BF16).astype(F32)
        back_ref[0:LANES, lanes] = grad_mixed[0:LANES].astype(BF16)
        grad = gg_ref[0:2, lanes]
        high = grad.astype(BF16).astype(F32)
        rim = [x_ref[part, 0:RIM, lanes].astype(F32)[0:2] for part in range(3)]
        rim += [high, grad - high, jnp.zeros((RIM - 11, LANES), F32)]
        rim.insert(0, grad_mixed[LANES : LANES + 1])
        back_ref[LANES:, lanes] = jnp.concatenate(rim, axis=0).astype(BF16)

    lax.fori_loop(0, chunks, product, 0)


def forward_kernel(
    group, which_ref, x_ref, taps_ref, filt_ref, halo_ref, w_ref,
    *refs,
):
    sends, (gate_ref, mixed_ref, gext_ref, ext_ref, table_ref) = refs[:PIECES], refs[PIECES:]
    _, rows, chans = x_ref.shape
    blocks = rows // SUB
    count = LANES // group

    def tile(j, lanes, ext, table):
        for part in range(3):
            at = LANES + 2 * part
            ext[part, 6:8, :] = halo_ref[at : at + 2, lanes].astype(F32)
            ext[part, 8:, :] = x_ref[part, :, lanes].astype(F32)
        keyed = feature(ext, taps_ref, lanes, 1, 0, rows)
        valued = feature(ext, taps_ref, lanes, 2, 0, rows)
        gext_ref[0:LANES, lanes] = halo_ref[0:LANES, lanes]
        gext_ref[LANES:, lanes] = (keyed * valued).astype(BF16)
        filt = filt_ref[j * count : (j + 1) * count, :]
        turned = ((grid_of(LANES, 0) + grid_of(LANES, 1)) % LANES == 0).astype(BF16)
        fill_table(table, jnp.dot(filt, turned, preferred_element_type=F32), True)
        wide = jnp.dot(
            table[...], windows(gext_ref, blocks, lanes), preferred_element_type=F32
        )
        mixed = pick_groups(wide, group, blocks)
        mixed_ref[:, lanes] = mixed
        query = feature(ext, taps_ref, lanes, 0, 0, rows)
        gate_ref[:, lanes] = (query * mixed).astype(BF16)

    each_tile(chans, tile, ext_ref, table_ref)
    project(which_ref[0], gate_ref, w_ref, sends)


def project(which, gate_ref, w_ref, out_refs):
    half = w_ref.shape[1] // 2
    part = half // len(out_refs)
    for i, out_ref in enumerate(out_refs):
        cols = pl.ds(pl.multiple_of(which * half + i * part, part), part)
        out_ref[...] = jnp.dot(
            gate_ref[...], w_ref[:, cols], preferred_element_type=F32
        ).astype(BF16)


def keep_kernel(which_ref, gate_ref, w_ref, *keep_refs):
    project(which_ref[0], gate_ref, w_ref, keep_refs)


def short_sums(grad, ext_ref, part):
    rows = grad.shape[0]
    return [
        jnp.sum(grad * ext_ref[part, 8 - lag : 8 - lag + rows, :], axis=0, keepdims=True)
        for lag in range(3)
    ]


def lags_kernel(
    group, filt_ref, x_ref, taps_ref, halo_ref, gg_ref, mixed_ref, gext_ref,
    gm_ref, gq_ref, lags_ref, tables_ref, left_ref, upside_ref, ext_ref,
):
    rows, chans = gg_ref.shape
    blocks = rows // SUB
    count = LANES // group

    def tile(j, lanes, left, upside, ext):
        filt = filt_ref[j * count : (j + 1) * count, :]
        fill_table(tables_ref.at[j], filt.astype(F32), False)
        ext[0, 6:8, :] = halo_ref[LANES : LANES + 2, lanes].astype(F32)
        ext[0, 8:, :] = x_ref[0, :, lanes].astype(F32)
        query = feature(ext, taps_ref, lanes, 0, 0, rows)
        grad_mixed = (gg_ref[:, lanes] * query).astype(BF16)
        gm_ref[:, lanes] = grad_mixed
        grad_query = (gg_ref[:, lanes] * mixed_ref[:, lanes]).astype(BF16)
        gq_ref[:, lanes] = grad_query
        sums = short_sums(grad_query.astype(F32), ext, 0)
        lane = group_of_lane(SUB, group)
        for g in range(count):
            for b in range(blocks):
                left[g * SUB : (g + 1) * SUB, b * LANES : (b + 1) * LANES] = jnp.where(
                    lane == g, grad_mixed[b * SUB : (b + 1) * SUB, :], jnp.zeros((), BF16)
                )
        ends = rows // LANES + 1
        flip = (grid_of(LANES, 0) + grid_of(LANES, 1) == LANES - 1).astype(BF16)
        turned = jnp.dot(
            flip,
            jnp.concatenate(
                [gext_ref[b * LANES : (b + 1) * LANES, lanes] for b in range(ends)], axis=1
            ),
            preferred_element_type=F32,
        ).astype(BF16)
        upside[0:LANES, :] = jnp.zeros((LANES, LANES), BF16)
        for b in range(ends):
            upside[LANES * (ends - b) : LANES * (ends - b + 1), :] = turned[
                :, b * LANES : (b + 1) * LANES
            ]
        rights = []
        for b in range(blocks):
            at = rows + LANES - b * SUB
            rights.append(
                jnp.concatenate([upside[at : at + LANES], upside[at - LANES : at]], axis=0)
            )
        products = lax.dot_general(
            left[...],
            jnp.concatenate(rights, axis=1),
            (((1,), (1,)), ((), ())),
            preferred_element_type=F32,
        )
        early = grid_of(SUB, 0) + grid_of(SUB, 1) < LANES - 1
        lag_rows = []
        for g in range(count):
            own = products[g * SUB : (g + 1) * SUB, :]
            ring = jnp.where(early, own[:, 0:LANES], own[:, LANES:])
            ring = pltpu.roll(ring, 0, 1, stride=1, stride_axis=0)
            lag_rows.append(jnp.sum(ring, axis=0, keepdims=True))
        lags = pltpu.roll(jnp.concatenate(lag_rows, axis=0), 1, 1)
        sums.append(jnp.zeros((16 - count - 3, LANES), F32))
        lags_ref[:, lanes] = jnp.concatenate([lags] + sums, axis=0)

    each_tile(chans, tile, left_ref, upside_ref, ext_ref)


def next_rows(ext_ref, taps_ref, x_ref, back_ref, lanes, parts):
    rows = x_ref.shape[1]
    rim = back_ref[LANES:, lanes].astype(F32)
    outs = []
    for part in parts:
        recent = x_ref[part, rows - RIM :, lanes].astype(F32)
        ext_ref[part, 0:8, :] = recent[RIM - 8 :]
        ext_ref[part, 8:10, :] = rim[1 + 2 * part : 3 + 2 * part]
        outs.append(feature(ext_ref, taps_ref, lanes, part, 0, 2))
    return outs, rim[7:9] + rim[9:11]


def next_mixed(back_ref, lanes, grad, query):
    head = back_ref[0 : LANES + RIM, lanes].astype(F32)
    first = (grad * query).astype(BF16).astype(F32)
    return jnp.concatenate([first, head[2:]], axis=0)


def backward_kernel(
    group, x_ref, taps_ref, halo_ref, back_ref, gm_ref, lags_ref, tables_ref,
    gkv_ref, sums_ref, ext_ref, mext_ref, near_ref,
):
    _, rows, chans = x_ref.shape
    blocks = rows // SUB
    count = LANES // group

    def tile(j, lanes, ext, mext, near):
        for part in range(1, 3):
            at = LANES + 2 * part
            ext[part, 6:8, :] = halo_ref[at : at + 2, lanes].astype(F32)
            ext[part, 8:, :] = x_ref[part, :, lanes].astype(F32)
        (query_next,), gg_next = next_rows(near, taps_ref, x_ref, back_ref, lanes, (0,))
        head = next_mixed(back_ref, lanes, gg_next, query_next)
        mext[0:rows, :] = gm_ref[:, lanes]
        mext[rows:, :] = head[0:LANES].astype(BF16)
        wide = jnp.dot(
            tables_ref[j], windows(mext, blocks, slice(None)), preferred_element_type=F32
        )
        grad_gated = pick_groups(wide, group, blocks)
        sums = [None] * 3
        for part in range(1, 3):
            grad = (grad_gated * feature(ext, taps_ref, lanes, 3 - part, 0, rows)).astype(BF16)
            gkv_ref[part - 1, :, lanes] = grad
            sums[part] = short_sums(grad.astype(F32), ext, part)
        early = lags_ref[:, lanes]
        flat = [early[0:count]]
        for lag in range(3):
            flat += [early[count + lag : count + lag + 1], sums[1][lag], sums[2][lag]]
        flat.append(jnp.zeros((32 - count - 9, LANES), F32))
        sums_ref[:, lanes] = jnp.concatenate(flat, axis=0).astype(sums_ref.dtype)

    each_tile(chans, tile, ext_ref, mext_ref, near_ref)


def inputs_kernel(
    group, x_ref, taps_ref, filt_ref, gext_ref, back_ref, gq_ref, gkv_ref, gin_ref, near_ref, gf_ref
):
    _, rows, chans = x_ref.shape
    count = LANES // group

    def tile(j, lanes, near, gf):
        (query, keyed, valued), grad = next_rows(
            near, taps_ref, x_ref, back_ref, lanes, (0, 1, 2)
        )
        head = next_mixed(back_ref, lanes, grad, query)
        filt = filt_ref[j * count : (j + 1) * count, :]
        taps = spread_taps(filt, group, False)
        taps_turned = spread_taps(filt, group, True)
        recent = gext_ref[rows:, lanes].astype(F32)
        recent = jnp.concatenate([recent, (keyed * valued).astype(BF16).astype(F32)], axis=0)
        gated, mixed = [], []
        for t in range(2):
            gated.append(jnp.sum(taps * head[t : t + LANES], axis=0, keepdims=True))
            mixed.append(
                jnp.sum(taps_turned * recent[t + 1 : t + 1 + LANES], axis=0, keepdims=True)
            )
        gated, mixed = jnp.concatenate(gated, axis=0), jnp.concatenate(mixed, axis=0)
        following = (grad * mixed, gated * valued, gated * keyed)
        for part in range(3):
            own = gq_ref[:, lanes] if part == 0 else gkv_ref[part - 1, :, lanes]
            gf[part, 0:rows, :] = own.astype(F32)
            gf[part, rows : rows + 2, :] = following[part].astype(BF16).astype(F32)
            total = taps_ref[0, part : part + 1, lanes] * gf[part, 0:rows, :]
            for lag in range(1, 3):
                tap = taps_ref[lag, part : part + 1, lanes]
                total = total + tap * gf[part, lag : lag + rows, :]
            gin_ref[part, :, lanes] = total.astype(BF16)

    each_tile(chans, tile, near_ref, gf_ref)


def unpack_kernel(group, short_scale, long_scale, *refs):
    short_ref, long_ref = refs[-2:]
    totals = [ref[...].astype(F32) for ref in refs[:-2]]
    while len(totals) > 1:
        totals = [sum(totals[i : i + 2]) for i in range(0, len(totals), 2)]
    total = totals[0]
    count = LANES // group
    for j in range(total.shape[1] // LANES):
        long_ref[j * count : (j + 1) * count, :] = (
            total[0:count, j * LANES : (j + 1) * LANES] * long_scale
        )
    for lag in range(3):
        for part in range(3):
            at = count + 3 * lag + part
            short_ref[lag, part : part + 1, :] = total[at : at + 1] * short_scale


def place_kernel(first, which_ref, own_ref, sibling_ref, *refs):
    out_ref, sems = refs[-2:]
    half = out_ref.shape[1] // 2
    copies = []
    for i, ref in enumerate((own_ref, sibling_ref)):
        side = which_ref[0] if i == 0 else 1 - which_ref[0]
        cols = pl.ds(pl.multiple_of(side * half + first, LANES), ref.shape[1])
        copies.append(pltpu.make_async_copy(ref, out_ref.at[:, cols], sems.at[i]))
    for copy in copies:
        copy.start()
    for copy in copies:
        copy.wait()


def place(result, which, own, sibling, first, width):
    far = pl.BlockSpec(memory_space=pltpu.HBM)
    near = pl.BlockSpec(memory_space=pltpu.VMEM)
    operands = (which, own, sibling) + (() if result is None else (result,))
    return pl.pallas_call(
        functools.partial(place_kernel, first),
        out_shape=shape((own.shape[0], width), BF16),
        in_specs=[pl.BlockSpec(memory_space=pltpu.SMEM), near, near, far][: len(operands)],
        out_specs=far,
        scratch_shapes=[pltpu.SemaphoreType.DMA((2,))],
        compiler_params=pltpu.CompilerParams(vmem_limit_bytes=VMEM_LIMIT),
        input_output_aliases={} if result is None else {3: 0},
        name="place",
    )(*operands)


def local(inputs, short_filter, long_filter, out_weight, out_cotangent):
    rows, _, chans = inputs.shape
    groups, span = long_filter.shape
    width = out_weight.shape[1]
    group = chans // groups
    count = LANES // group
    tiles = chans // LANES
    tokens_all = rows * lax.axis_size("ctx")
    n_tp = lax.axis_size("tp")
    signal = inputs.transpose(1, 0, 2)
    signal, short_filter, long_filter, out_weight, out_cotangent = [
        pltpu.with_memory_space_constraint(value, pltpu.HBM)
        for value in (signal, short_filter, long_filter, out_weight, out_cotangent)
    ]
    table = pltpu.VMEM((tiles, count * SUB, LANES + SUB), BF16)

    sent, signal, short_filter, long_filter = call(
        tail_kernel,
        "tail",
        (
            shape((LANES + EDGE, chans), BF16),
            shape(signal.shape, BF16),
            shape(short_filter.shape, F32),
            shape(long_filter.shape, BF16),
        ),
        [pltpu.VMEM((tiles, 3, 8 + RIM + LANES, LANES), F32), pltpu.SemaphoreType.DMA((6,))],
        far=3,
    )(signal, short_filter, long_filter)
    halo = shifted(sent, "ctx", 1)
    grad_gate, sent_back, out_weight = call(
        grad_gate_kernel,
        "grad_gate",
        (
            shape((rows, chans), F32),
            shape((LANES + RIM, chans), BF16),
            shape(out_weight.shape, BF16),
        ),
        [
            pltpu.VMEM(out_cotangent.shape, BF16),
            pltpu.VMEM((tiles, 1, 8 + RIM + LANES, LANES), F32),
            pltpu.SemaphoreType.DMA,
            pltpu.SemaphoreType.DMA((max(1, chans // 256),)),
        ],
        far=2,
        operands=2,
    )(out_cotangent, out_weight, signal, short_filter)
    back = shifted(sent_back, "ctx", -1)
    core = lax.rem(lax.axis_index("tp"), 2)
    piece = shape((rows, width // 2 // PIECES), BF16)
    *other, gate_out, mixed, gated = call(
        functools.partial(forward_kernel, group),
        "forward",
        (piece,) * PIECES
        + (
            shape((rows, chans), BF16),
            shape((rows, chans), F32),
            shape((LANES + rows, chans), BF16),
        ),
        [pltpu.VMEM((tiles, 3, 8 + rows, LANES), F32), table],
        scalars=1,
        operands=5,
    )(jnp.reshape(1 - core, (1,)), signal, short_filter, long_filter, halo, out_weight)
    theirs = [lax.ppermute(value, "tp", pairwise("tp", 1)) for value in other]
    kept = call(keep_kernel, "keep", (piece,) * PIECES, scalars=1, operands=2)(
        jnp.reshape(core, (1,)), gate_out, out_weight
    )
    mine = [
        (a.astype(F32) + b.astype(F32)).astype(BF16) for a, b in zip(kept, theirs, strict=True)
    ]
    step = 2
    got = [lax.ppermute(value, "tp", pairwise("tp", step)) for value in mine]

    ext = pltpu.VMEM((tiles, 3, rows + 8, LANES), F32)
    near = pltpu.VMEM((tiles, 3, 16, LANES), F32)
    grad_mixed, grad_query, lags, tables = call(
        functools.partial(lags_kernel, group),
        "lags",
        (
            shape((rows, chans), BF16),
            shape((rows, chans), BF16),
            shape((16, chans), F32),
            shape((chans // LANES, count * SUB, LANES + SUB), BF16),
        ),
        [
            pltpu.VMEM((tiles, count * SUB, rows // SUB * LANES), BF16),
            pltpu.VMEM((tiles, rows + 2 * LANES, LANES), BF16),
            ext,
        ],
        operands=7,
    )(long_filter, signal, short_filter, halo, grad_gate, mixed, gated)
    n_ctx = lax.axis_size("ctx")
    by_pairs = n_ctx & (n_ctx - 1) == 0
    grad_rest, sums = call(
        functools.partial(backward_kernel, group),
        "backward",
        (shape((2, rows, chans), BF16), shape((32, chans), BF16 if by_pairs else F32)),
        [ext, pltpu.VMEM((tiles, rows + LANES, LANES), BF16), near],
        operands=7,
    )(signal, short_filter, halo, back, grad_mixed, lags, tables)
    grad_in = call(
        functools.partial(inputs_kernel, group),
        "inputs",
        shape((3, rows, chans), BF16),
        [near, pltpu.VMEM((tiles, 3, rows + 8, LANES), F32)],
        operands=7,
    )(signal, short_filter, long_filter, gated, back, grad_query, grad_rest)
    if by_pairs:
        hop = 1
        terms = [sums]
        while hop < n_ctx:
            if len(terms) > 1:
                pairs = [a.astype(F32) + b.astype(F32) for a, b in zip(terms[::2], terms[1::2])]
                terms = [sum(pairs).astype(BF16)]
            radix = min(4, n_ctx // hop)
            terms += [
                lax.ppermute(terms[0], "ctx", pairwise("ctx", i * hop)) for i in range(1, radix)
            ]
            if hop == 1:
                terms, grad_in = lax.optimization_barrier((terms, grad_in))
            hop *= radix
    else:
        terms = [lax.psum(sums, "ctx")]
    got, terms = lax.optimization_barrier((got, terms))
    mine = [
        (a.astype(F32) + b.astype(F32)).astype(BF16) for a, b in zip(mine, got, strict=True)
    ]
    step *= 2
    while step < n_tp:
        got = [lax.ppermute(value, "tp", pairwise("tp", step)) for value in mine]
        mine = [
            (a.astype(F32) + b.astype(F32)).astype(BF16) for a, b in zip(mine, got, strict=True)
        ]
        step *= 2
    sibling = [lax.ppermute(value, "tp", pairwise("tp", 1)) for value in mine]
    result = None
    for i in reversed(range(PIECES)):
        result = place(
            result, jnp.reshape(core, (1,)), mine[i], sibling[i], i * (width // 2 // PIECES), width
        )
    grad_short, grad_long = call(
        functools.partial(
            unpack_kernel, group, float(tokens_all) ** (-0.5), float(tokens_all * group) ** (-0.5)
        ),
        "unpack",
        (shape((3, 3, chans), F32), shape((groups, span), F32)),
        operands=len(terms),
    )(*terms)
    return (result, grad_in.transpose(1, 0, 2), grad_short, grad_long)


def solution(mesh):
    in_specs = (
        P("ctx", None, "tp"),
        P(None, None, "tp"),
        P("tp", None),
        P("tp", None),
        P("ctx", None),
    )
    out_specs = (P("ctx", None), P("ctx", None, "tp"), P(None, None, "tp"), P("tp", None))
    return jax.shard_map(local, mesh=mesh, in_specs=in_specs, out_specs=out_specs, check_vma=False)
```

```python
import functools

import jax
import jax.numpy as jnp
from jax import lax
from jax.experimental import pallas as pl
from jax.experimental.pallas import tpu as pltpu
from jax.sharding import PartitionSpec as P

LANES = 128
RIM = 16
EDGE = 8
SUB = 32
COST = 1024
PIECES = 2
F32 = jnp.float32
BF16 = jnp.bfloat16
VMEM_LIMIT = 12 * 1024 * 1024


def pairwise(axis, step):
    return [(source, source ^ step) for source in range(lax.axis_size(axis))]


def shifted(value, axis, steps):
    count = lax.axis_size(axis)
    initial, last = (max(0, -steps), min(count, count - steps))
    return lax.ppermute(value, axis, [(source, source + steps) for source in range(initial, last)])


def call(body, name, outs, scratch=(), scalars=0, far=0, operands=0, cost=COST):
    specs = [pl.BlockSpec(memory_space=pltpu.SMEM)] * scalars
    specs += [pl.BlockSpec(memory_space=pltpu.HBM)] * far
    specs += [pl.BlockSpec(memory_space=pltpu.VMEM)] * operands
    return pl.pallas_call(
        body,
        out_shape=outs,
        in_specs=specs,
        out_specs=jax.tree.map(lambda _: pl.BlockSpec(memory_space=pltpu.VMEM), outs),
        scratch_shapes=scratch,
        compiler_params=pltpu.CompilerParams(vmem_limit_bytes=VMEM_LIMIT),
        cost_estimate=pl.CostEstimate(flops=0, transcendentals=0, bytes_accessed=cost),
        name=name,
    )


def shape(dims, dtype):
    return jax.ShapeDtypeStruct(dims, dtype)


def each_tile(chans, body, *scratch):
    for j in range(chans // LANES):
        body(j, slice(j * LANES, (j + 1) * LANES), *[ref.at[j] for ref in scratch])


def feature(ext_ref, taps_ref, lanes, part, start, rows):
    total = taps_ref[0, part : part + 1, lanes] * ext_ref[part, 8 + start : 8 + start + rows, :]
    for lag in range(1, 3):
        first = 8 + start - lag
        tap = taps_ref[lag, part : part + 1, lanes]
        total = total + tap * ext_ref[part, first : first + rows, :]
    return total


def group_of_lane(rows, group):
    return lax.broadcasted_iota(jnp.int32, (rows, LANES), 1) // group


def grid_of(rows, axis):
    return lax.broadcasted_iota(jnp.int32, (rows, LANES), axis)


def fill_table(table_ref, taps, forward):
    row, col = grid_of(SUB, 0), grid_of(SUB, 1)
    early = (col > row) if forward else (col >= row)
    for g in range(taps.shape[0]):
        wide = jnp.broadcast_to(taps[g : g + 1, :], (SUB, LANES))
        ring = pltpu.roll(wide, 0, 1, stride=1, stride_axis=0)
        rows = slice(g * SUB, (g + 1) * SUB)
        table_ref[rows, 0:LANES] = jnp.where(early, ring, 0.0).astype(BF16)
        table_ref[rows, LANES:] = jnp.where(early, 0.0, ring)[:, 0:SUB].astype(BF16)


def pick_groups(wide, group, blocks):
    lane = group_of_lane(SUB, group)
    outs = []
    for b in range(blocks):
        cols = slice(b * LANES, (b + 1) * LANES)
        total = wide[0:SUB, cols]
        for g in range(1, LANES // group):
            total = jnp.where(lane == g, wide[g * SUB : (g + 1) * SUB, cols], total)
        outs.append(total)
    return jnp.concatenate(outs, axis=0)


def windows(ref, blocks, lanes):
    return jnp.concatenate(
        [ref[b * SUB : (b + 1) * SUB + LANES, lanes] for b in range(blocks)], axis=1
    )


def spread_taps(filt, group, reverse):
    count = filt.shape[0]
    owner = (
        group_of_lane(count, group) == lax.broadcasted_iota(jnp.int32, (count, LANES), 0)
    ).astype(BF16)
    if reverse:
        flip = (grid_of(LANES, 0) + grid_of(LANES, 1) == LANES - 1).astype(BF16)
        filt = jnp.dot(filt, flip, preferred_element_type=F32).astype(BF16)
    return lax.dot_general(filt, owner, (((0,), (0,)), ((), ())), preferred_element_type=F32)


def tail_kernel(
    x_hbm, taps_hbm, filt_hbm, sent_ref, x_ref, taps_ref, filt_ref, ext_ref, sems
):
    _, rows, chans = x_ref.shape
    first = rows - LANES - RIM
    regions = (
        (pl.ds(1, 2), pl.ds(first, LANES + RIM)),
        (pl.ds(0, 1), pl.ds(rows - RIM, RIM)),
        (pl.ds(0, 1), pl.ds(0, rows - RIM)),
        (pl.ds(1, 2), pl.ds(0, first)),
    )
    copies = [pltpu.make_async_copy(taps_hbm, taps_ref, sems.at[0])]
    for i, region in enumerate(regions):
        copies.append(
            pltpu.make_async_copy(x_hbm.at[region], x_ref.at[region], sems.at[1 + i])
        )
    copies.append(pltpu.make_async_copy(filt_hbm, filt_ref, sems.at[5]))
    for copy in copies:
        copy.start()
    for copy in copies[:3]:
        copy.wait()

    def tile(j, lanes, ext):
        for part in range(1, 3):
            ext[part, 8:, :] = x_ref[part, first:, lanes].astype(F32)
        keyed = feature(ext, taps_ref, lanes, 1, RIM, LANES)
        valued = feature(ext, taps_ref, lanes, 2, RIM, LANES)
        sent_ref[0:LANES, lanes] = (keyed * valued).astype(BF16)
        rim = [x_ref[part, rows - RIM :, lanes].astype(F32)[RIM - 2 :] for part in range(3)]
        rim.append(jnp.zeros((EDGE - 6, LANES), F32))
        sent_ref[LANES:, lanes] = jnp.concatenate(rim, axis=0).astype(BF16)

    each_tile(chans, tile, ext_ref)
    for copy in copies[3:]:
        copy.wait()


def grad_gate_kernel(
    c_hbm, w_hbm, x_ref, taps_ref, gg_ref, back_ref, w_ref, c_ref, ext_ref, c_sem, w_sems
):
    chans = w_ref.shape[0]
    chunks = w_sems.shape[0]
    wide = chans // chunks
    span = LANES + RIM

    def chunk(j):
        rows = pl.ds(pl.multiple_of(j * wide, wide), wide)
        return pltpu.make_async_copy(w_hbm.at[rows], w_ref.at[rows], w_sems.at[j])

    load = pltpu.make_async_copy(c_hbm, c_ref, c_sem)
    load.start()
    for j in range(min(2, chunks)):
        chunk(j).start()
    load.wait()

    def product(j, carry):
        chunk(j).wait()

        @pl.when(j + 2 < chunks)
        def _():
            chunk(j + 2).start()

        cols = pl.ds(pl.multiple_of(j * wide, wide), wide)
        gg_ref[:, cols] = lax.dot_general(
            c_ref[...], w_ref[cols, :], (((1,), (1,)), ((), ())), preferred_element_type=F32
        )
        for i in range(wide // LANES):
            at = pl.multiple_of(j * wide + i * LANES, LANES)
            tile(pl.ds(at, LANES), ext_ref.at[i])
        return carry

    def tile(lanes, ext):
        ext[0, 0:8, :] = jnp.zeros((8, LANES), F32)
        ext[0, 8:, :] = x_ref[0, 0:span, lanes].astype(F32)
        query = feature(ext, taps_ref, lanes, 0, 0, span)
        grad_mixed = (gg_ref[0:span, lanes] * query).astype(BF16).astype(F32)
        back_ref[0:LANES, lanes] = grad_mixed[0:LANES].astype(BF16)
        grad = gg_ref[0:2, lanes]
        high = grad.astype(BF16).astype(F32)
        rim = [x_ref[part, 0:RIM, lanes].astype(F32)[0:2] for part in range(3)]
        rim += [high, grad - high, jnp.zeros((RIM - 11, LANES), F32)]
        rim.insert(0, grad_mixed[LANES : LANES + 1])
        back_ref[LANES:, lanes] = jnp.concatenate(rim, axis=0).astype(BF16)

    lax.fori_loop(0, chunks, product, 0)


def forward_kernel(
    group, which_ref, x_ref, taps_ref, filt_ref, halo_ref, w_ref,
    *refs,
):
    sends, (gate_ref, mixed_ref, gext_ref, ext_ref, table_ref) = refs[:PIECES], refs[PIECES:]
    _, rows, chans = x_ref.shape
    blocks = rows // SUB
    count = LANES // group

    def tile(j, lanes, ext, table):
        for part in range(3):
            at = LANES + 2 * part
            ext[part, 6:8, :] = halo_ref[at : at + 2, lanes].astype(F32)
            ext[part, 8:, :] = x_ref[part, :, lanes].astype(F32)
        keyed = feature(ext, taps_ref, lanes, 1, 0, rows)
        valued = feature(ext, taps_ref, lanes, 2, 0, rows)
        gext_ref[0:LANES, lanes] = halo_ref[0:LANES, lanes]
        gext_ref[LANES:, lanes] = (keyed * valued).astype(BF16)
        filt = filt_ref[j * count : (j + 1) * count, :]
        turned = ((grid_of(LANES, 0) + grid_of(LANES, 1)) % LANES == 0).astype(BF16)
        fill_table(table, jnp.dot(filt, turned, preferred_element_type=F32), True)
        wide = jnp.dot(
            table[...], windows(gext_ref, blocks, lanes), preferred_element_type=F32
        )
        mixed = pick_groups(wide, group, blocks)
        mixed_ref[:, lanes] = mixed
        query = feature(ext, taps_ref, lanes, 0, 0, rows)
        gate_ref[:, lanes] = (query * mixed).astype(BF16)

    each_tile(chans, tile, ext_ref, table_ref)
    project(which_ref[0], gate_ref, w_ref, sends)


def project(which, gate_ref, w_ref, out_refs, theirs=None):
    half = w_ref.shape[1] // 2
    part = half // len(out_refs)
    for i, out_ref in enumerate(out_refs):
        cols = pl.ds(pl.multiple_of(which * half + i * part, part), part)
        total = jnp.dot(gate_ref[...], w_ref[:, cols], preferred_element_type=F32)
        if theirs is not None:
            total = total.astype(BF16).astype(F32) + theirs[i][...].astype(F32)
        out_ref[...] = total.astype(BF16)


def keep_kernel(which_ref, gate_ref, w_ref, *refs):
    project(which_ref[0], gate_ref, w_ref, refs[PIECES:], refs[:PIECES])


def short_sums(grad, ext_ref, part):
    rows = grad.shape[0]
    return [
        jnp.sum(grad * ext_ref[part, 8 - lag : 8 - lag + rows, :], axis=0, keepdims=True)
        for lag in range(3)
    ]


def lags_kernel(
    group, filt_ref, x_ref, taps_ref, halo_ref, gg_ref, mixed_ref, gext_ref,
    gm_ref, gq_ref, lags_ref, tables_ref, left_ref, upside_ref, ext_ref,
):
    rows, chans = gg_ref.shape
    blocks = rows // SUB
    count = LANES // group

    def tile(j, lanes, left, upside, ext):
        filt = filt_ref[j * count : (j + 1) * count, :]
        fill_table(tables_ref.at[j], filt.astype(F32), False)
        ext[0, 6:8, :] = halo_ref[LANES : LANES + 2, lanes].astype(F32)
        ext[0, 8:, :] = x_ref[0, :, lanes].astype(F32)
        query = feature(ext, taps_ref, lanes, 0, 0, rows)
        grad_mixed = (gg_ref[:, lanes] * query).astype(BF16)
        gm_ref[:, lanes] = grad_mixed
        grad_query = (gg_ref[:, lanes] * mixed_ref[:, lanes]).astype(BF16)
        gq_ref[:, lanes] = grad_query
        sums = short_sums(grad_query.astype(F32), ext, 0)
        lane = group_of_lane(SUB, group)
        for g in range(count):
            for b in range(blocks):
                left[g * SUB : (g + 1) * SUB, b * LANES : (b + 1) * LANES] = jnp.where(
                    lane == g, grad_mixed[b * SUB : (b + 1) * SUB, :], jnp.zeros((), BF16)
                )
        ends = rows // LANES + 1
        flip = (grid_of(LANES, 0) + grid_of(LANES, 1) == LANES - 1).astype(BF16)
        turned = jnp.dot(
            flip,
            jnp.concatenate(
                [gext_ref[b * LANES : (b + 1) * LANES, lanes] for b in range(ends)], axis=1
            ),
            preferred_element_type=F32,
        ).astype(BF16)
        upside[0:LANES, :] = jnp.zeros((LANES, LANES), BF16)
        for b in range(ends):
            upside[LANES * (ends - b) : LANES * (ends - b + 1), :] = turned[
                :, b * LANES : (b + 1) * LANES
            ]
        rights = []
        for b in range(blocks):
            at = rows + LANES - b * SUB
            rights.append(
                jnp.concatenate([upside[at : at + LANES], upside[at - LANES : at]], axis=0)
            )
        products = lax.dot_general(
            left[...],
            jnp.concatenate(rights, axis=1),
            (((1,), (1,)), ((), ())),
            preferred_element_type=F32,
        )
        early = grid_of(SUB, 0) + grid_of(SUB, 1) < LANES - 1
        lag_rows = []
        for g in range(count):
            own = products[g * SUB : (g + 1) * SUB, :]
            ring = jnp.where(early, own[:, 0:LANES], own[:, LANES:])
            ring = pltpu.roll(ring, 0, 1, stride=1, stride_axis=0)
            lag_rows.append(jnp.sum(ring, axis=0, keepdims=True))
        lags = pltpu.roll(jnp.concatenate(lag_rows, axis=0), 1, 1)
        sums.append(jnp.zeros((16 - count - 3, LANES), F32))
        lags_ref[:, lanes] = jnp.concatenate([lags] + sums, axis=0)

    each_tile(chans, tile, left_ref, upside_ref, ext_ref)


def next_rows(ext_ref, taps_ref, x_ref, back_ref, lanes, parts):
    rows = x_ref.shape[1]
    rim = back_ref[LANES:, lanes].astype(F32)
    outs = []
    for part in parts:
        recent = x_ref[part, rows - RIM :, lanes].astype(F32)
        ext_ref[part, 0:8, :] = recent[RIM - 8 :]
        ext_ref[part, 8:10, :] = rim[1 + 2 * part : 3 + 2 * part]
        outs.append(feature(ext_ref, taps_ref, lanes, part, 0, 2))
    return outs, rim[7:9] + rim[9:11]


def next_mixed(back_ref, lanes, grad, query):
    head = back_ref[0 : LANES + RIM, lanes].astype(F32)
    first = (grad * query).astype(BF16).astype(F32)
    return jnp.concatenate([first, head[2:]], axis=0)


def backward_kernel(
    group, x_ref, taps_ref, halo_ref, back_ref, gm_ref, lags_ref, tables_ref,
    gkv_ref, sums_ref, ext_ref, mext_ref, near_ref,
):
    _, rows, chans = x_ref.shape
    blocks = rows // SUB
    count = LANES // group

    def tile(j, lanes, ext, mext, near):
        for part in range(1, 3):
            at = LANES + 2 * part
            ext[part, 6:8, :] = halo_ref[at : at + 2, lanes].astype(F32)
            ext[part, 8:, :] = x_ref[part, :, lanes].astype(F32)
        (query_next,), gg_next = next_rows(near, taps_ref, x_ref, back_ref, lanes, (0,))
        head = next_mixed(back_ref, lanes, gg_next, query_next)
        mext[0:rows, :] = gm_ref[:, lanes]
        mext[rows:, :] = head[0:LANES].astype(BF16)
        wide = jnp.dot(
            tables_ref[j], windows(mext, blocks, slice(None)), preferred_element_type=F32
        )
        grad_gated = pick_groups(wide, group, blocks)
        sums = [None] * 3
        for part in range(1, 3):
            grad = (grad_gated * feature(ext, taps_ref, lanes, 3 - part, 0, rows)).astype(BF16)
            gkv_ref[part - 1, :, lanes] = grad
            sums[part] = short_sums(grad.astype(F32), ext, part)
        early = lags_ref[:, lanes]
        flat = [early[0:count]]
        for lag in range(3):
            flat += [early[count + lag : count + lag + 1], sums[1][lag], sums[2][lag]]
        flat.append(jnp.zeros((32 - count - 9, LANES), F32))
        sums_ref[:, lanes] = jnp.concatenate(flat, axis=0).astype(sums_ref.dtype)

    each_tile(chans, tile, ext_ref, mext_ref, near_ref)


def inputs_kernel(
    group, x_ref, taps_ref, filt_ref, gext_ref, back_ref, gq_ref, gkv_ref, gin_ref, near_ref, gf_ref
):
    _, rows, chans = x_ref.shape
    count = LANES // group

    def tile(j, lanes, near, gf):
        (query, keyed, valued), grad = next_rows(
            near, taps_ref, x_ref, back_ref, lanes, (0, 1, 2)
        )
        head = next_mixed(back_ref, lanes, grad, query)
        filt = filt_ref[j * count : (j + 1) * count, :]
        taps = spread_taps(filt, group, False)
        taps_turned = spread_taps(filt, group, True)
        recent = gext_ref[rows:, lanes].astype(F32)
        recent = jnp.concatenate([recent, (keyed * valued).astype(BF16).astype(F32)], axis=0)
        gated, mixed = [], []
        for t in range(2):
            gated.append(jnp.sum(taps * head[t : t + LANES], axis=0, keepdims=True))
            mixed.append(
                jnp.sum(taps_turned * recent[t + 1 : t + 1 + LANES], axis=0, keepdims=True)
            )
        gated, mixed = jnp.concatenate(gated, axis=0), jnp.concatenate(mixed, axis=0)
        following = (grad * mixed, gated * valued, gated * keyed)
        for part in range(3):
            own = gq_ref[:, lanes] if part == 0 else gkv_ref[part - 1, :, lanes]
            gf[part, 0:rows, :] = own.astype(F32)
            gf[part, rows : rows + 2, :] = following[part].astype(BF16).astype(F32)
            total = taps_ref[0, part : part + 1, lanes] * gf[part, 0:rows, :]
            for lag in range(1, 3):
                tap = taps_ref[lag, part : part + 1, lanes]
                total = total + tap * gf[part, lag : lag + rows, :]
            gin_ref[part, :, lanes] = total.astype(BF16)

    each_tile(chans, tile, near_ref, gf_ref)


def unpack_kernel(group, short_scale, long_scale, *refs):
    short_ref, long_ref = refs[-2:]
    totals = [ref[...].astype(F32) for ref in refs[:-2]]
    while len(totals) > 1:
        totals = [sum(totals[i : i + 2]) for i in range(0, len(totals), 2)]
    total = totals[0]
    count = LANES // group
    for j in range(total.shape[1] // LANES):
        long_ref[j * count : (j + 1) * count, :] = (
            total[0:count, j * LANES : (j + 1) * LANES] * long_scale
        )
    for lag in range(3):
        for part in range(3):
            at = count + 3 * lag + part
            short_ref[lag, part : part + 1, :] = total[at : at + 1] * short_scale


def place_kernel(first, which_ref, own_ref, sibling_ref, *refs):
    out_ref, sems = refs[-2:]
    half = out_ref.shape[1] // 2
    copies = []
    for i, ref in enumerate((own_ref, sibling_ref)):
        side = which_ref[0] if i == 0 else 1 - which_ref[0]
        cols = pl.ds(pl.multiple_of(side * half + first, LANES), ref.shape[1])
        copies.append(pltpu.make_async_copy(ref, out_ref.at[:, cols], sems.at[i]))
    for copy in copies:
        copy.start()
    for copy in copies:
        copy.wait()


def place(result, which, own, sibling, first, width):
    far = pl.BlockSpec(memory_space=pltpu.HBM)
    near = pl.BlockSpec(memory_space=pltpu.VMEM)
    operands = (which, own, sibling) + (() if result is None else (result,))
    return pl.pallas_call(
        functools.partial(place_kernel, first),
        out_shape=shape((own.shape[0], width), BF16),
        in_specs=[pl.BlockSpec(memory_space=pltpu.SMEM), near, near, far][: len(operands)],
        out_specs=far,
        scratch_shapes=[pltpu.SemaphoreType.DMA((2,))],
        compiler_params=pltpu.CompilerParams(vmem_limit_bytes=VMEM_LIMIT),
        input_output_aliases={} if result is None else {3: 0},
        name="place",
    )(*operands)


def local(inputs, short_filter, long_filter, out_weight, out_cotangent):
    rows, _, chans = inputs.shape
    groups, span = long_filter.shape
    width = out_weight.shape[1]
    group = chans // groups
    count = LANES // group
    tiles = chans // LANES
    tokens_all = rows * lax.axis_size("ctx")
    n_tp = lax.axis_size("tp")
    signal = inputs.transpose(1, 0, 2)
    signal, short_filter, long_filter, out_weight, out_cotangent = [
        pltpu.with_memory_space_constraint(value, pltpu.HBM)
        for value in (signal, short_filter, long_filter, out_weight, out_cotangent)
    ]
    table = pltpu.VMEM((tiles, count * SUB, LANES + SUB), BF16)

    sent, signal, short_filter, long_filter = call(
        tail_kernel,
        "tail",
        (
            shape((LANES + EDGE, chans), BF16),
            shape(signal.shape, BF16),
            shape(short_filter.shape, F32),
            shape(long_filter.shape, BF16),
        ),
        [pltpu.VMEM((tiles, 3, 8 + RIM + LANES, LANES), F32), pltpu.SemaphoreType.DMA((6,))],
        far=3,
    )(signal, short_filter, long_filter)
    halo = shifted(sent, "ctx", 1)
    grad_gate, sent_back, out_weight = call(
        grad_gate_kernel,
        "grad_gate",
        (
            shape((rows, chans), F32),
            shape((LANES + RIM, chans), BF16),
            shape(out_weight.shape, BF16),
        ),
        [
            pltpu.VMEM(out_cotangent.shape, BF16),
            pltpu.VMEM((tiles, 1, 8 + RIM + LANES, LANES), F32),
            pltpu.SemaphoreType.DMA,
            pltpu.SemaphoreType.DMA((max(1, chans // 256),)),
        ],
        far=2,
        operands=2,
    )(out_cotangent, out_weight, signal, short_filter)
    back = shifted(sent_back, "ctx", -1)
    core = lax.rem(lax.axis_index("tp"), 2)
    piece = shape((rows, width // 2 // PIECES), BF16)
    *other, gate_out, mixed, gated = call(
        functools.partial(forward_kernel, group),
        "forward",
        (piece,) * PIECES
        + (
            shape((rows, chans), BF16),
            shape((rows, chans), F32),
            shape((LANES + rows, chans), BF16),
        ),
        [pltpu.VMEM((tiles, 3, 8 + rows, LANES), F32), table],
        scalars=1,
        operands=5,
    )(jnp.reshape(1 - core, (1,)), signal, short_filter, long_filter, halo, out_weight)
    theirs = [lax.ppermute(value, "tp", pairwise("tp", 1)) for value in other]
    mine = call(
        keep_kernel, "keep", (piece,) * PIECES, scalars=1, operands=2 + PIECES
    )(jnp.reshape(core, (1,)), gate_out, out_weight, *theirs)
    step = 2
    got = [lax.ppermute(value, "tp", pairwise("tp", step)) for value in mine]

    ext = pltpu.VMEM((tiles, 3, rows + 8, LANES), F32)
    near = pltpu.VMEM((tiles, 3, 16, LANES), F32)
    grad_mixed, grad_query, lags, tables = call(
        functools.partial(lags_kernel, group),
        "lags",
        (
            shape((rows, chans), BF16),
            shape((rows, chans), BF16),
            shape((16, chans), F32),
            shape((chans // LANES, count * SUB, LANES + SUB), BF16),
        ),
        [
            pltpu.VMEM((tiles, count * SUB, rows // SUB * LANES), BF16),
            pltpu.VMEM((tiles, rows + 2 * LANES, LANES), BF16),
            ext,
        ],
        operands=7,
    )(long_filter, signal, short_filter, halo, grad_gate, mixed, gated)
    n_ctx = lax.axis_size("ctx")
    by_pairs = n_ctx & (n_ctx - 1) == 0
    grad_rest, sums = call(
        functools.partial(backward_kernel, group),
        "backward",
        (shape((2, rows, chans), BF16), shape((32, chans), BF16 if by_pairs else F32)),
        [ext, pltpu.VMEM((tiles, rows + LANES, LANES), BF16), near],
        operands=7,
    )(signal, short_filter, halo, back, grad_mixed, lags, tables)
    grad_in = call(
        functools.partial(inputs_kernel, group),
        "inputs",
        shape((3, rows, chans), BF16),
        [near, pltpu.VMEM((tiles, 3, rows + 8, LANES), F32)],
        operands=7,
    )(signal, short_filter, long_filter, gated, back, grad_query, grad_rest)
    if by_pairs:
        hop = 1
        terms = [sums]
        while hop < n_ctx:
            if len(terms) > 1:
                pairs = [a.astype(F32) + b.astype(F32) for a, b in zip(terms[::2], terms[1::2])]
                terms = [sum(pairs).astype(BF16)]
            radix = min(4, n_ctx // hop)
            terms += [
                lax.ppermute(terms[0], "ctx", pairwise("ctx", i * hop)) for i in range(1, radix)
            ]
            if hop == 1:
                terms, grad_in = lax.optimization_barrier((terms, grad_in))
            hop *= radix
    else:
        terms = [lax.psum(sums, "ctx")]
    got, terms = lax.optimization_barrier((got, terms))
    mine = [
        (a.astype(F32) + b.astype(F32)).astype(BF16) for a, b in zip(mine, got, strict=True)
    ]
    step *= 2
    while step < n_tp:
        got = [lax.ppermute(value, "tp", pairwise("tp", step)) for value in mine]
        mine = [
            (a.astype(F32) + b.astype(F32)).astype(BF16) for a, b in zip(mine, got, strict=True)
        ]
        step *= 2
    sibling = [lax.ppermute(value, "tp", pairwise("tp", 1)) for value in mine]
    result = None
    for i in reversed(range(PIECES)):
        result = place(
            result, jnp.reshape(core, (1,)), mine[i], sibling[i], i * (width // 2 // PIECES), width
        )
    grad_short, grad_long = call(
        functools.partial(
            unpack_kernel, group, float(tokens_all) ** (-0.5), float(tokens_all * group) ** (-0.5)
        ),
        "unpack",
        (shape((3, 3, chans), F32), shape((groups, span), F32)),
        operands=len(terms),
    )(*terms)
    return (result, grad_in.transpose(1, 0, 2), grad_short, grad_long)


def solution(mesh):
    in_specs = (
        P("ctx", None, "tp"),
        P(None, None, "tp"),
        P("tp", None),
        P("tp", None),
        P("ctx", None),
    )
    out_specs = (P("ctx", None), P("ctx", None, "tp"), P(None, None, "tp"), P("tp", None))
    return jax.shard_map(local, mesh=mesh, in_specs=in_specs, out_specs=out_specs, check_vma=False)
```

```python
import functools

import jax
import jax.numpy as jnp
from jax import lax
from jax.experimental import pallas as pl
from jax.experimental.pallas import tpu as pltpu
from jax.sharding import PartitionSpec as P

LANES = 128
RIM = 16
EDGE = 8
SUB = 16
COST = 1024
PIECES = 2
F32 = jnp.float32
BF16 = jnp.bfloat16
VMEM_LIMIT = 12 * 1024 * 1024


def pairwise(axis, step):
    return [(source, source ^ step) for source in range(lax.axis_size(axis))]


def shifted(value, axis, steps):
    count = lax.axis_size(axis)
    initial, last = (max(0, -steps), min(count, count - steps))
    return lax.ppermute(value, axis, [(source, source + steps) for source in range(initial, last)])


def call(body, name, outs, scratch=(), scalars=0, far=0, operands=0, cost=COST):
    specs = [pl.BlockSpec(memory_space=pltpu.SMEM)] * scalars
    specs += [pl.BlockSpec(memory_space=pltpu.HBM)] * far
    specs += [pl.BlockSpec(memory_space=pltpu.VMEM)] * operands
    return pl.pallas_call(
        body,
        out_shape=outs,
        in_specs=specs,
        out_specs=jax.tree.map(lambda _: pl.BlockSpec(memory_space=pltpu.VMEM), outs),
        scratch_shapes=scratch,
        compiler_params=pltpu.CompilerParams(vmem_limit_bytes=VMEM_LIMIT),
        cost_estimate=pl.CostEstimate(flops=0, transcendentals=0, bytes_accessed=cost),
        name=name,
    )


def shape(dims, dtype):
    return jax.ShapeDtypeStruct(dims, dtype)


def each_tile(chans, body, *scratch):
    for j in range(chans // LANES):
        body(j, slice(j * LANES, (j + 1) * LANES), *[ref.at[j] for ref in scratch])


def feature(ext_ref, taps_ref, lanes, part, start, rows):
    total = taps_ref[0, part : part + 1, lanes] * ext_ref[part, 8 + start : 8 + start + rows, :]
    for lag in range(1, 3):
        first = 8 + start - lag
        tap = taps_ref[lag, part : part + 1, lanes]
        total = total + tap * ext_ref[part, first : first + rows, :]
    return total


def group_of_lane(rows, group):
    return lax.broadcasted_iota(jnp.int32, (rows, LANES), 1) // group


def grid_of(rows, axis):
    return lax.broadcasted_iota(jnp.int32, (rows, LANES), axis)


def fill_table(table_ref, taps, forward):
    row, col = grid_of(SUB, 0), grid_of(SUB, 1)
    early = (col > row) if forward else (col >= row)
    for g in range(taps.shape[0]):
        wide = jnp.broadcast_to(taps[g : g + 1, :], (SUB, LANES))
        ring = pltpu.roll(wide, 0, 1, stride=1, stride_axis=0)
        rows = slice(g * SUB, (g + 1) * SUB)
        table_ref[rows, 0:LANES] = jnp.where(early, ring, 0.0).astype(BF16)
        table_ref[rows, LANES:] = jnp.where(early, 0.0, ring)[:, 0:SUB].astype(BF16)


def pick_groups(wide, group, blocks):
    lane = group_of_lane(SUB, group)
    outs = []
    for b in range(blocks):
        cols = slice(b * LANES, (b + 1) * LANES)
        total = wide[0:SUB, cols]
        for g in range(1, LANES // group):
            total = jnp.where(lane == g, wide[g * SUB : (g + 1) * SUB, cols], total)
        outs.append(total)
    return jnp.concatenate(outs, axis=0)


def windows(ref, blocks, lanes):
    return jnp.concatenate(
        [ref[b * SUB : (b + 1) * SUB + LANES, lanes] for b in range(blocks)], axis=1
    )


def spread_taps(filt, group, reverse):
    count = filt.shape[0]
    owner = (
        group_of_lane(count, group) == lax.broadcasted_iota(jnp.int32, (count, LANES), 0)
    ).astype(BF16)
    if reverse:
        flip = (grid_of(LANES, 0) + grid_of(LANES, 1) == LANES - 1).astype(BF16)
        filt = jnp.dot(filt, flip, preferred_element_type=F32).astype(BF16)
    return lax.dot_general(filt, owner, (((0,), (0,)), ((), ())), preferred_element_type=F32)


def tail_kernel(
    x_hbm, taps_hbm, filt_hbm, sent_ref, x_ref, taps_ref, filt_ref, ext_ref, sems
):
    _, rows, chans = x_ref.shape
    first = rows - LANES - RIM
    regions = (
        (pl.ds(1, 2), pl.ds(first, LANES + RIM)),
        (pl.ds(0, 1), pl.ds(rows - RIM, RIM)),
        (pl.ds(0, 1), pl.ds(0, rows - RIM)),
        (pl.ds(1, 2), pl.ds(0, first)),
    )
    copies = [pltpu.make_async_copy(taps_hbm, taps_ref, sems.at[0])]
    for i, region in enumerate(regions):
        copies.append(
            pltpu.make_async_copy(x_hbm.at[region], x_ref.at[region], sems.at[1 + i])
        )
    copies.append(pltpu.make_async_copy(filt_hbm, filt_ref, sems.at[5]))
    for copy in copies:
        copy.start()
    for copy in copies[:3]:
        copy.wait()

    def tile(j, lanes, ext):
        for part in range(1, 3):
            ext[part, 8:, :] = x_ref[part, first:, lanes].astype(F32)
        keyed = feature(ext, taps_ref, lanes, 1, RIM, LANES)
        valued = feature(ext, taps_ref, lanes, 2, RIM, LANES)
        sent_ref[0:LANES, lanes] = (keyed * valued).astype(BF16)
        rim = [x_ref[part, rows - RIM :, lanes].astype(F32)[RIM - 2 :] for part in range(3)]
        rim.append(jnp.zeros((EDGE - 6, LANES), F32))
        sent_ref[LANES:, lanes] = jnp.concatenate(rim, axis=0).astype(BF16)

    each_tile(chans, tile, ext_ref)
    for copy in copies[3:]:
        copy.wait()


def grad_gate_kernel(
    c_hbm, w_hbm, x_ref, taps_ref, gg_ref, back_ref, w_ref, c_ref, ext_ref, c_sem, w_sems
):
    chans = w_ref.shape[0]
    chunks = w_sems.shape[0]
    wide = chans // chunks
    span = LANES + RIM

    def chunk(j):
        rows = pl.ds(pl.multiple_of(j * wide, wide), wide)
        return pltpu.make_async_copy(w_hbm.at[rows], w_ref.at[rows], w_sems.at[j])

    load = pltpu.make_async_copy(c_hbm, c_ref, c_sem)
    load.start()
    for j in range(min(2, chunks)):
        chunk(j).start()
    load.wait()

    def product(j, carry):
        chunk(j).wait()

        @pl.when(j + 2 < chunks)
        def _():
            chunk(j + 2).start()

        cols = pl.ds(pl.multiple_of(j * wide, wide), wide)
        gg_ref[:, cols] = lax.dot_general(
            c_ref[...], w_ref[cols, :], (((1,), (1,)), ((), ())), preferred_element_type=F32
        )
        for i in range(wide // LANES):
            at = pl.multiple_of(j * wide + i * LANES, LANES)
            tile(pl.ds(at, LANES), ext_ref.at[i])
        return carry

    def tile(lanes, ext):
        ext[0, 0:8, :] = jnp.zeros((8, LANES), F32)
        ext[0, 8:, :] = x_ref[0, 0:span, lanes].astype(F32)
        query = feature(ext, taps_ref, lanes, 0, 0, span)
        grad_mixed = (gg_ref[0:span, lanes] * query).astype(BF16).astype(F32)
        back_ref[0:LANES, lanes] = grad_mixed[0:LANES].astype(BF16)
        grad = gg_ref[0:2, lanes]
        high = grad.astype(BF16).astype(F32)
        rim = [x_ref[part, 0:RIM, lanes].astype(F32)[0:2] for part in range(3)]
        rim += [high, grad - high, jnp.zeros((RIM - 11, LANES), F32)]
        rim.insert(0, grad_mixed[LANES : LANES + 1])
        back_ref[LANES:, lanes] = jnp.concatenate(rim, axis=0).astype(BF16)

    lax.fori_loop(0, chunks, product, 0)


def forward_kernel(
    group, which_ref, x_ref, taps_ref, filt_ref, halo_ref, w_ref,
    *refs,
):
    sends, (gate_ref, mixed_ref, gext_ref, ext_ref, table_ref) = refs[:PIECES], refs[PIECES:]
    _, rows, chans = x_ref.shape
    blocks = rows // SUB
    count = LANES // group

    def tile(j, lanes, ext, table):
        for part in range(3):
            at = LANES + 2 * part
            ext[part, 6:8, :] = halo_ref[at : at + 2, lanes].astype(F32)
            ext[part, 8:, :] = x_ref[part, :, lanes].astype(F32)
        keyed = feature(ext, taps_ref, lanes, 1, 0, rows)
        valued = feature(ext, taps_ref, lanes, 2, 0, rows)
        gext_ref[0:LANES, lanes] = halo_ref[0:LANES, lanes]
        gext_ref[LANES:, lanes] = (keyed * valued).astype(BF16)
        filt = filt_ref[j * count : (j + 1) * count, :]
        turned = ((grid_of(LANES, 0) + grid_of(LANES, 1)) % LANES == 0).astype(BF16)
        fill_table(table, jnp.dot(filt, turned, preferred_element_type=F32), True)
        wide = jnp.dot(
            table[...], windows(gext_ref, blocks, lanes), preferred_element_type=F32
        )
        mixed = pick_groups(wide, group, blocks)
        mixed_ref[:, lanes] = mixed
        query = feature(ext, taps_ref, lanes, 0, 0, rows)
        gate_ref[:, lanes] = (query * mixed).astype(BF16)

    each_tile(chans, tile, ext_ref, table_ref)
    project(which_ref[0], gate_ref, w_ref, sends)


def project(which, gate_ref, w_ref, out_refs):
    half = w_ref.shape[1] // 2
    part = half // len(out_refs)
    for i, out_ref in enumerate(out_refs):
        cols = pl.ds(pl.multiple_of(which * half + i * part, part), part)
        out_ref[...] = jnp.dot(
            gate_ref[...], w_ref[:, cols], preferred_element_type=F32
        ).astype(BF16)


def keep_kernel(which_ref, gate_ref, w_ref, *keep_refs):
    project(which_ref[0], gate_ref, w_ref, keep_refs)


def short_sums(grad, ext_ref, part):
    rows = grad.shape[0]
    return [
        jnp.sum(grad * ext_ref[part, 8 - lag : 8 - lag + rows, :], axis=0, keepdims=True)
        for lag in range(3)
    ]


def lags_kernel(
    group, filt_ref, x_ref, taps_ref, halo_ref, gg_ref, mixed_ref, gext_ref,
    gm_ref, gq_ref, lags_ref, tables_ref, left_ref, upside_ref, ext_ref,
):
    rows, chans = gg_ref.shape
    blocks = rows // SUB
    count = LANES // group

    def tile(j, lanes, left, upside, ext):
        filt = filt_ref[j * count : (j + 1) * count, :]
        fill_table(tables_ref.at[j], filt.astype(F32), False)
        ext[0, 6:8, :] = halo_ref[LANES : LANES + 2, lanes].astype(F32)
        ext[0, 8:, :] = x_ref[0, :, lanes].astype(F32)
        query = feature(ext, taps_ref, lanes, 0, 0, rows)
        grad_mixed = (gg_ref[:, lanes] * query).astype(BF16)
        gm_ref[:, lanes] = grad_mixed
        grad_query = (gg_ref[:, lanes] * mixed_ref[:, lanes]).astype(BF16)
        gq_ref[:, lanes] = grad_query
        sums = short_sums(grad_query.astype(F32), ext, 0)
        lane = group_of_lane(SUB, group)
        for g in range(count):
            for b in range(blocks):
                left[g * SUB : (g + 1) * SUB, b * LANES : (b + 1) * LANES] = jnp.where(
                    lane == g, grad_mixed[b * SUB : (b + 1) * SUB, :], jnp.zeros((), BF16)
                )
        ends = rows // LANES + 1
        flip = (grid_of(LANES, 0) + grid_of(LANES, 1) == LANES - 1).astype(BF16)
        turned = jnp.dot(
            flip,
            jnp.concatenate(
                [gext_ref[b * LANES : (b + 1) * LANES, lanes] for b in range(ends)], axis=1
            ),
            preferred_element_type=F32,
        ).astype(BF16)
        upside[0:LANES, :] = jnp.zeros((LANES, LANES), BF16)
        for b in range(ends):
            upside[LANES * (ends - b) : LANES * (ends - b + 1), :] = turned[
                :, b * LANES : (b + 1) * LANES
            ]
        rights = []
        for b in range(blocks):
            at = rows + LANES - b * SUB
            rights.append(
                jnp.concatenate([upside[at : at + LANES], upside[at - LANES : at]], axis=0)
            )
        products = lax.dot_general(
            left[...],
            jnp.concatenate(rights, axis=1),
            (((1,), (1,)), ((), ())),
            preferred_element_type=F32,
        )
        early = grid_of(SUB, 0) + grid_of(SUB, 1) < LANES - 1
        lag_rows = []
        for g in range(count):
            own = products[g * SUB : (g + 1) * SUB, :]
            ring = jnp.where(early, own[:, 0:LANES], own[:, LANES:])
            ring = pltpu.roll(ring, 0, 1, stride=1, stride_axis=0)
            lag_rows.append(jnp.sum(ring, axis=0, keepdims=True))
        lags = pltpu.roll(jnp.concatenate(lag_rows, axis=0), 1, 1)
        sums.append(jnp.zeros((16 - count - 3, LANES), F32))
        lags_ref[:, lanes] = jnp.concatenate([lags] + sums, axis=0)

    each_tile(chans, tile, left_ref, upside_ref, ext_ref)


def next_rows(ext_ref, taps_ref, x_ref, back_ref, lanes, parts):
    rows = x_ref.shape[1]
    rim = back_ref[LANES:, lanes].astype(F32)
    outs = []
    for part in parts:
        recent = x_ref[part, rows - RIM :, lanes].astype(F32)
        ext_ref[part, 0:8, :] = recent[RIM - 8 :]
        ext_ref[part, 8:10, :] = rim[1 + 2 * part : 3 + 2 * part]
        outs.append(feature(ext_ref, taps_ref, lanes, part, 0, 2))
    return outs, rim[7:9] + rim[9:11]


def next_mixed(back_ref, lanes, grad, query):
    head = back_ref[0 : LANES + RIM, lanes].astype(F32)
    first = (grad * query).astype(BF16).astype(F32)
    return jnp.concatenate([first, head[2:]], axis=0)


def backward_kernel(
    group, x_ref, taps_ref, halo_ref, back_ref, gm_ref, lags_ref, tables_ref,
    gkv_ref, sums_ref, ext_ref, mext_ref, near_ref,
):
    _, rows, chans = x_ref.shape
    blocks = rows // SUB
    count = LANES // group

    def tile(j, lanes, ext, mext, near):
        for part in range(1, 3):
            at = LANES + 2 * part
            ext[part, 6:8, :] = halo_ref[at : at + 2, lanes].astype(F32)
            ext[part, 8:, :] = x_ref[part, :, lanes].astype(F32)
        (query_next,), gg_next = next_rows(near, taps_ref, x_ref, back_ref, lanes, (0,))
        head = next_mixed(back_ref, lanes, gg_next, query_next)
        mext[0:rows, :] = gm_ref[:, lanes]
        mext[rows:, :] = head[0:LANES].astype(BF16)
        wide = jnp.dot(
            tables_ref[j], windows(mext, blocks, slice(None)), preferred_element_type=F32
        )
        grad_gated = pick_groups(wide, group, blocks)
        sums = [None] * 3
        for part in range(1, 3):
            grad = (grad_gated * feature(ext, taps_ref, lanes, 3 - part, 0, rows)).astype(BF16)
            gkv_ref[part - 1, :, lanes] = grad
            sums[part] = short_sums(grad.astype(F32), ext, part)
        early = lags_ref[:, lanes]
        flat = [early[0:count]]
        for lag in range(3):
            flat += [early[count + lag : count + lag + 1], sums[1][lag], sums[2][lag]]
        flat.append(jnp.zeros((32 - count - 9, LANES), F32))
        sums_ref[:, lanes] = jnp.concatenate(flat, axis=0).astype(sums_ref.dtype)

    each_tile(chans, tile, ext_ref, mext_ref, near_ref)


def inputs_kernel(
    group, x_ref, taps_ref, filt_ref, gext_ref, back_ref, gq_ref, gkv_ref, gin_ref, near_ref, gf_ref
):
    _, rows, chans = x_ref.shape
    count = LANES // group

    def tile(j, lanes, near, gf):
        (query, keyed, valued), grad = next_rows(
            near, taps_ref, x_ref, back_ref, lanes, (0, 1, 2)
        )
        head = next_mixed(back_ref, lanes, grad, query)
        filt = filt_ref[j * count : (j + 1) * count, :]
        taps = spread_taps(filt, group, False)
        taps_turned = spread_taps(filt, group, True)
        recent = gext_ref[rows:, lanes].astype(F32)
        recent = jnp.concatenate([recent, (keyed * valued).astype(BF16).astype(F32)], axis=0)
        gated, mixed = [], []
        for t in range(2):
            gated.append(jnp.sum(taps * head[t : t + LANES], axis=0, keepdims=True))
            mixed.append(
                jnp.sum(taps_turned * recent[t + 1 : t + 1 + LANES], axis=0, keepdims=True)
            )
        gated, mixed = jnp.concatenate(gated, axis=0), jnp.concatenate(mixed, axis=0)
        following = (grad * mixed, gated * valued, gated * keyed)
        for part in range(3):
            own = gq_ref[:, lanes] if part == 0 else gkv_ref[part - 1, :, lanes]
            gf[part, 0:rows, :] = own.astype(F32)
            gf[part, rows : rows + 2, :] = following[part].astype(BF16).astype(F32)
            total = taps_ref[0, part : part + 1, lanes] * gf[part, 0:rows, :]
            for lag in range(1, 3):
                tap = taps_ref[lag, part : part + 1, lanes]
                total = total + tap * gf[part, lag : lag + rows, :]
            gin_ref[part, :, lanes] = total.astype(BF16)

    each_tile(chans, tile, near_ref, gf_ref)


def unpack_kernel(group, short_scale, long_scale, *refs):
    short_ref, long_ref = refs[-2:]
    totals = [ref[...].astype(F32) for ref in refs[:-2]]
    while len(totals) > 1:
        totals = [sum(totals[i : i + 2]) for i in range(0, len(totals), 2)]
    total = totals[0]
    count = LANES // group
    for j in range(total.shape[1] // LANES):
        long_ref[j * count : (j + 1) * count, :] = (
            total[0:count, j * LANES : (j + 1) * LANES] * long_scale
        )
    for lag in range(3):
        for part in range(3):
            at = count + 3 * lag + part
            short_ref[lag, part : part + 1, :] = total[at : at + 1] * short_scale


def place_kernel(first, which_ref, own_ref, sibling_ref, *refs):
    out_ref, sems = refs[-2:]
    half = out_ref.shape[1] // 2
    copies = []
    for i, ref in enumerate((own_ref, sibling_ref)):
        side = which_ref[0] if i == 0 else 1 - which_ref[0]
        cols = pl.ds(pl.multiple_of(side * half + first, LANES), ref.shape[1])
        copies.append(pltpu.make_async_copy(ref, out_ref.at[:, cols], sems.at[i]))
    for copy in copies:
        copy.start()
    for copy in copies:
        copy.wait()


def place(result, which, own, sibling, first, width):
    far = pl.BlockSpec(memory_space=pltpu.HBM)
    near = pl.BlockSpec(memory_space=pltpu.VMEM)
    operands = (which, own, sibling) + (() if result is None else (result,))
    return pl.pallas_call(
        functools.partial(place_kernel, first),
        out_shape=shape((own.shape[0], width), BF16),
        in_specs=[pl.BlockSpec(memory_space=pltpu.SMEM), near, near, far][: len(operands)],
        out_specs=far,
        scratch_shapes=[pltpu.SemaphoreType.DMA((2,))],
        compiler_params=pltpu.CompilerParams(vmem_limit_bytes=VMEM_LIMIT),
        input_output_aliases={} if result is None else {3: 0},
        name="place",
    )(*operands)


def local(inputs, short_filter, long_filter, out_weight, out_cotangent):
    rows, _, chans = inputs.shape
    groups, span = long_filter.shape
    width = out_weight.shape[1]
    group = chans // groups
    count = LANES // group
    tiles = chans // LANES
    tokens_all = rows * lax.axis_size("ctx")
    n_tp = lax.axis_size("tp")
    signal = inputs.transpose(1, 0, 2)
    signal, short_filter, long_filter, out_weight, out_cotangent = [
        pltpu.with_memory_space_constraint(value, pltpu.HBM)
        for value in (signal, short_filter, long_filter, out_weight, out_cotangent)
    ]
    table = pltpu.VMEM((tiles, count * SUB, LANES + SUB), BF16)

    sent, signal, short_filter, long_filter = call(
        tail_kernel,
        "tail",
        (
            shape((LANES + EDGE, chans), BF16),
            shape(signal.shape, BF16),
            shape(short_filter.shape, F32),
            shape(long_filter.shape, BF16),
        ),
        [pltpu.VMEM((tiles, 3, 8 + RIM + LANES, LANES), F32), pltpu.SemaphoreType.DMA((6,))],
        far=3,
    )(signal, short_filter, long_filter)
    halo = shifted(sent, "ctx", 1)
    grad_gate, sent_back, out_weight = call(
        grad_gate_kernel,
        "grad_gate",
        (
            shape((rows, chans), F32),
            shape((LANES + RIM, chans), BF16),
            shape(out_weight.shape, BF16),
        ),
        [
            pltpu.VMEM(out_cotangent.shape, BF16),
            pltpu.VMEM((tiles, 1, 8 + RIM + LANES, LANES), F32),
            pltpu.SemaphoreType.DMA,
            pltpu.SemaphoreType.DMA((max(1, chans // 256),)),
        ],
        far=2,
        operands=2,
    )(out_cotangent, out_weight, signal, short_filter)
    back = shifted(sent_back, "ctx", -1)
    core = lax.rem(lax.axis_index("tp"), 2)
    piece = shape((rows, width // 2 // PIECES), BF16)
    *other, gate_out, mixed, gated = call(
        functools.partial(forward_kernel, group),
        "forward",
        (piece,) * PIECES
        + (
            shape((rows, chans), BF16),
            shape((rows, chans), F32),
            shape((LANES + rows, chans), BF16),
        ),
        [pltpu.VMEM((tiles, 3, 8 + rows, LANES), F32), table],
        scalars=1,
        operands=5,
    )(jnp.reshape(1 - core, (1,)), signal, short_filter, long_filter, halo, out_weight)
    theirs = [lax.ppermute(value, "tp", pairwise("tp", 1)) for value in other]
    kept = call(keep_kernel, "keep", (piece,) * PIECES, scalars=1, operands=2)(
        jnp.reshape(core, (1,)), gate_out, out_weight
    )
    mine = [
        (a.astype(F32) + b.astype(F32)).astype(BF16) for a, b in zip(kept, theirs, strict=True)
    ]
    step = 2
    got = [lax.ppermute(value, "tp", pairwise("tp", step)) for value in mine]

    ext = pltpu.VMEM((tiles, 3, rows + 8, LANES), F32)
    near = pltpu.VMEM((tiles, 3, 16, LANES), F32)
    grad_mixed, grad_query, lags, tables = call(
        functools.partial(lags_kernel, group),
        "lags",
        (
            shape((rows, chans), BF16),
            shape((rows, chans), BF16),
            shape((16, chans), F32),
            shape((chans // LANES, count * SUB, LANES + SUB), BF16),
        ),
        [
            pltpu.VMEM((tiles, count * SUB, rows // SUB * LANES), BF16),
            pltpu.VMEM((tiles, rows + 2 * LANES, LANES), BF16),
            ext,
        ],
        operands=7,
    )(long_filter, signal, short_filter, halo, grad_gate, mixed, gated)
    n_ctx = lax.axis_size("ctx")
    by_pairs = n_ctx & (n_ctx - 1) == 0
    grad_rest, sums = call(
        functools.partial(backward_kernel, group),
        "backward",
        (shape((2, rows, chans), BF16), shape((32, chans), BF16 if by_pairs else F32)),
        [ext, pltpu.VMEM((tiles, rows + LANES, LANES), BF16), near],
        operands=7,
    )(signal, short_filter, halo, back, grad_mixed, lags, tables)
    grad_in = call(
        functools.partial(inputs_kernel, group),
        "inputs",
        shape((3, rows, chans), BF16),
        [near, pltpu.VMEM((tiles, 3, rows + 8, LANES), F32)],
        operands=7,
    )(signal, short_filter, long_filter, gated, back, grad_query, grad_rest)
    if by_pairs:
        hop = 1
        terms = [sums]
        while hop < n_ctx:
            if len(terms) > 1:
                pairs = [a.astype(F32) + b.astype(F32) for a, b in zip(terms[::2], terms[1::2])]
                terms = [sum(pairs).astype(BF16)]
            radix = min(4, n_ctx // hop)
            terms += [
                lax.ppermute(terms[0], "ctx", pairwise("ctx", i * hop)) for i in range(1, radix)
            ]
            if hop == 1:
                terms, grad_in = lax.optimization_barrier((terms, grad_in))
            hop *= radix
    else:
        terms = [lax.psum(sums, "ctx")]
    got, terms = lax.optimization_barrier((got, terms))
    mine = [
        (a.astype(F32) + b.astype(F32)).astype(BF16) for a, b in zip(mine, got, strict=True)
    ]
    step *= 2
    while step < n_tp:
        got = [lax.ppermute(value, "tp", pairwise("tp", step)) for value in mine]
        mine = [
            (a.astype(F32) + b.astype(F32)).astype(BF16) for a, b in zip(mine, got, strict=True)
        ]
        step *= 2
    sibling = [lax.ppermute(value, "tp", pairwise("tp", 1)) for value in mine]
    result = None
    for i in reversed(range(PIECES)):
        result = place(
            result, jnp.reshape(core, (1,)), mine[i], sibling[i], i * (width // 2 // PIECES), width
        )
    grad_short, grad_long = call(
        functools.partial(
            unpack_kernel, group, float(tokens_all) ** (-0.5), float(tokens_all * group) ** (-0.5)
        ),
        "unpack",
        (shape((3, 3, chans), F32), shape((groups, span), F32)),
        operands=len(terms),
    )(*terms)
    return (result, grad_in.transpose(1, 0, 2), grad_short, grad_long)


def solution(mesh):
    in_specs = (
        P("ctx", None, "tp"),
        P(None, None, "tp"),
        P("tp", None),
        P("tp", None),
        P("ctx", None),
    )
    out_specs = (P("ctx", None), P("ctx", None, "tp"), P(None, None, "tp"), P("tp", None))
    return jax.shard_map(local, mesh=mesh, in_specs=in_specs, out_specs=out_specs, check_vma=False)
```
